32 devices in a mesh: tp: 4 (over x, core), ep: 2 (over y), dp: 4 (over z).
Axes of the slice: x: 2, y: 2, z: 4, core: 2. Of those that a mesh axis runs over, the one named last changes fastest.
Arguments:
- tokens: bfloat16 [8, 512, 768], P(('ep', 'dp'), 'tp'), may hold values from -6 to 6
- segment: int32 [8, 512], P(('ep', 'dp')), may hold values from 0 to 7, never falling along the last dimension, each value on 1 to 256 neighbouring positions
- key_mask: int32 [8, 512], P(('ep', 'dp')), may hold values 0 or 1
- routes: int32 [8, 512, 2], P(('ep', 'dp'), 'tp'), may hold values from 0 to 3, all different within a row; in each aligned block of 128 rows (0 to 127, 128 to 255, ..., all dimensions but the last counted through in order) at most 128 rows name the same one
- gates: float32 [8, 512, 2], P(('ep', 'dp'), 'tp'), may hold values from 0.25 to 1
- ln1_gain: float32 [768], replicated, may hold values from 0.5 to 1.5
- ln1_bias: float32 [768], replicated, may hold values from -0.5 to 0.5
- query_weight: bfloat16 [768, 768], P(None, 'tp'), may hold values from -0.21875 to 0.21875
- key_weight: bfloat16 [768, 768], P(None, 'tp'), may hold values from -0.21875 to 0.21875
- value_weight: bfloat16 [768, 768], P(None, 'tp'), may hold values from -0.21875 to 0.21875
- out_weight: bfloat16 [768, 768], P('tp'), may hold values from -2.5 to 2.5
- ln2_gain: float32 [768], replicated, may hold values from 0.5 to 1.5
- ln2_bias: float32 [768], replicated, may hold values from -0.5 to 0.5
- frozen_in: bfloat16 [2, 768, 3072], P('ep'), may hold values from -0.21875 to 0.21875
- frozen_out: bfloat16 [2, 3072, 768], P('ep'), may hold values from -0.109375 to 0.109375
- train_in: bfloat16 [2, 768, 3072], P('ep'), may hold values from -0.21875 to 0.21875
- train_out: bfloat16 [2, 3072, 768], P('ep'), may hold values from -0.109375 to 0.109375
- cotangent: bfloat16 [8, 512, 768], P(('ep', 'dp'), 'tp'), may hold values from -6 to 6
Outputs:
- layer_out: bfloat16 [8, 512, 768], P(('ep', 'dp'), 'tp')
- tokens_grad: float32 [8, 512, 768], P(('ep', 'dp'), 'tp')
- ln1_gain_grad: float32 [768], replicated
- ln1_bias_grad: float32 [768], replicated
- query_grad: float32 [768, 768], P(None, 'tp')
- key_grad: float32 [768, 768], P(None, 'tp')
- value_grad: float32 [768, 768], P(None, 'tp')
- out_grad: float32 [768, 768], P('tp')
- ln2_gain_grad: float32 [768], replicated
- ln2_bias_grad: float32 [768], replicated
- train_in_grad: float32 [2, 768, 3072], P('ep')
- train_out_grad: float32 [2, 3072, 768], P('ep')
- expert_counts: int32 [4], replicated
The draws below stay inside these ranges and needn't reach their ends.
Inputs may be any that keep to these rules, and one draw needn't show every extreme that they name: `segment`: segment numbers never fall along a group; each sequence holds 1 to 256 tokens, one exactly 256. `routes`: the two experts of a token differ. In the tokens of one device (aligned blocks of 128 tokens) no expert is named more than 128 times, a bound that some block reaches.
All inputs are finite; a program needn't handle non-finite values. No bound on the sum of `key_mask` on one device may be relied on, other than what follows from the above.
Results may differ from the reference program's by a relative error of at most 0.017.
Values may be sent and summed in bfloat16 or wider, within the bound.
A program may use at most 192 MiB of HBM per device.

```python
import math
import jax
import jax.numpy as jnp
import numpy as np
from jax import lax

D = 768
HEADS = 12
HD = 64
FF = 3072
TOK_DEV = 128
SEQS = 8
GROUP = 512
GROUPS = 8
LONGEST = 256
EXPERTS = 4
CAP = 128
N_TP = 4
N_EP = 2


def plant(entries, rng, smallest, high):
    spot = [jax.random.randint(jax.random.fold_in(rng, axis), (), 0, length) for axis, length in enumerate(entries.shape)]
    main_axis = entries.shape.index(max(entries.shape))
    next_to = spot[:main_axis] + [(spot[main_axis] + 1) % entries.shape[main_axis]] + spot[main_axis + 1:]
    return entries.at[tuple(spot)].set(smallest).at[tuple(next_to)].set(high)


def levels(key, dims, shards, least, top_value):
    loudness = 1.0
    for dim, shards_of in shards:
        draws = jax.random.uniform(jax.random.fold_in(jax.random.fold_in(key, 6), dim), (shards_of,), jnp.float32, least / len(shards), top_value / len(shards))
        loudness = loudness * jnp.repeat(jnp.exp(draws), dims[dim] // shards_of).reshape((-1,) + (1,) * (len(dims) - 1 - dim))
    return loudness


def split_up(count, total, limit, slope):
    weights = [(1 << 20) // math.isqrt(standing ** slope) + 1 for standing in range(2, count + 1)]
    spare, given = total - limit - (count - 1), [1] * (count - 1)
    while spare > 0:
        candidates = [i for i in range(count - 1) if given[i] < limit]
        mass, budget = sum([weights[i] for i in candidates]), spare
        for i in candidates:
            addition = min(limit - given[i], max(1, budget * weights[i] // mass), spare)
            given[i] = given[i] + addition
            spare = spare - addition
    return np.array([limit] + given)


def uneven_parts(own_key, count, total, most, skew):
    if count == 2:
        one = jax.random.randint(own_key, (), max(1, total - most), min(most, total - 1) + 1)
        return jnp.stack([one, total - one])
    sizes = jnp.asarray(split_up(count, total, most, skew), jnp.int32)
    couples = (count - 1) // 2
    donor, taker = sizes[1:1 + 2 * couples:2], sizes[2:2 + 2 * couples:2]
    slack = jnp.minimum(donor - 1, most - taker)
    passed = jax.random.randint(jax.random.fold_in(own_key, 1), (couples,), 0, 1 << 20) % (slack + 1)
    sizes = sizes.at[1:1 + 2 * couples:2].set(donor - passed).at[2:2 + 2 * couples:2].set(taker + passed)
    return sizes[jax.random.permutation(jax.random.fold_in(own_key, 2), count)]


def assign_block(rng, own, number, rows, count, top, limit, skew):
    sequence = jax.random.permutation(rng, count)
    packed, ordinary = load_shares(count, rows * top, limit, skew, True), load_shares(count, rows * top, limit, skew, False)
    places = jnp.arange(count)

    def named(sizes, turn):
        used = int((sizes > 0).sum())
        fixed = max(1, used // 4)
        moved = fixed + (places - fixed + turn * (used - fixed)) % max(1, count - fixed)
        return jnp.zeros((count,), jnp.int32).at[sequence[jnp.where(places < fixed, places, moved)]].set(jnp.asarray(sizes, jnp.int32))

    sizes = jnp.where(number % 4 == 0, named(packed, number // 4), named(ordinary, number - number // 4 - 1))
    mixed = jax.random.permutation(jax.random.fold_in(own, 3), count)
    donor, taker = mixed[0:count // 2 * 2:2], mixed[1:count // 2 * 2:2]
    margin = jnp.minimum(sizes[donor] - 1, limit - sizes[taker]) // 2
    margin = jnp.where((donor == sequence[0]) | (taker == sequence[0]) | (sizes[taker] == 0), 0, jnp.maximum(margin, 0))
    moved = jax.random.randint(jax.random.fold_in(own, 4), (count // 2,), 0, 1 << 20) % (margin + 1)
    sizes = sizes.at[donor].add(-moved).at[taker].add(moved)
    labels = jnp.searchsorted(jnp.cumsum(sizes), jnp.arange(rows * top), side="right").astype(jnp.int32)
    listing = labels.reshape(top, rows).T
    listing = listing[jax.random.permutation(jax.random.fold_in(own, 1), rows)]
    turn = jax.random.randint(jax.random.fold_in(own, 2), (rows, 1), 0, top)
    return jnp.take_along_axis(listing, (jnp.arange(top)[None, :] + turn) % top, axis=1)


def load_shares(number_of, total, reach, slope, full):
    portions = [(1 << 20) // math.isqrt(rank ** slope) + 1 for rank in range(1, number_of + 1)]
    largest = reach if full else min(reach, max(-(-total // number_of), total * portions[0] // sum(portions)))
    least = 1 if total - largest >= number_of - 1 else 0
    holding, surplus = [largest] + [least] * (number_of - 1), total - largest - least * (number_of - 1)
    while surplus > 0:
        candidates = [i for i in range(1, number_of) if holding[i] < largest] or [i for i in range(1, number_of) if holding[i] < reach]
        whole, remaining = sum([portions[i] for i in candidates]), surplus
        for i in candidates:
            more = min(reach - holding[i], max(1, remaining * portions[i] // whole), surplus)
            holding[i] = holding[i] + more
            surplus = surplus - more
    return np.array(holding)


def centred(own_key, shape, scale, most, split=(), kind=jnp.bfloat16):
    entries = scale * jax.random.normal(own_key, shape, jnp.float32)
    if split:
        entries = entries * levels(own_key, shape, split, -0.22, 0.18)
    return jnp.clip(entries, -most, most).astype(kind)


def setup_inputs(seed: int = 0) -> dict:
    splits = jax.random.split(jax.random.key(seed), 19)
    tokens = centred(splits[0], (GROUPS, GROUP, D), 1.0, 6.0, ((0, 8), (1, 4)))
    segment = jax.vmap(lambda own: jnp.searchsorted(jnp.cumsum(uneven_parts(own, SEQS, GROUP, LONGEST, 2)), jnp.arange(GROUP), side="right"))(jax.random.split(splits[1], GROUPS)).reshape((GROUPS, GROUP)).astype(jnp.int32)
    key_mask = plant((jax.random.randint(splits[2], (GROUPS, GROUP), 0, 8) < 7).astype(jnp.int32), jax.random.fold_in(splits[2], 1), 0, 1)
    routes_keys = jax.random.split(jax.random.fold_in(splits[3], 1), GROUPS * GROUP // TOK_DEV)
    routes_turns = jax.random.permutation(jax.random.fold_in(splits[3], 3), GROUPS * GROUP // TOK_DEV)
    routes = jax.vmap(lambda own, number: assign_block(jax.random.fold_in(splits[3], 2), own, number, TOK_DEV, EXPERTS, 2, CAP, 2))(routes_keys, routes_turns).reshape((GROUPS, GROUP, 2))
    gates = jnp.clip(0.25 + 0.75 * jax.random.uniform(splits[4], (GROUPS, GROUP, 2), jnp.float32) ** levels(splits[4], (GROUPS, GROUP, 2), ((0, 8), (1, 4)), -0.2, 0.2), 0.25, 1.0)
    ln1_gain = jnp.clip(1.0 + 0.1 * jax.random.normal(splits[5], (D,), jnp.float32), 0.5, 1.5)
    ln1_bias = centred(splits[6], (D,), 0.1, 0.5, (), jnp.float32)
    query_weight = centred(splits[7], (D, D), D ** -0.5, 0.21875, ((1, 4),))
    key_weight = centred(splits[8], (D, D), D ** -0.5, 0.21875, ((1, 4),))
    value_weight = centred(splits[9], (D, D), D ** -0.5, 0.21875, ((1, 4),))
    out_weight = centred(splits[10], (D, D), (max(D // 128, 4)) ** -0.5, 2.5, ((0, 4),))
    ln2_gain = jnp.clip(1.0 + 0.1 * jax.random.normal(splits[11], (D,), jnp.float32), 0.5, 1.5)
    ln2_bias = centred(splits[12], (D,), 0.1, 0.5, (), jnp.float32)
    frozen_in = centred(splits[13], (N_EP, D, FF), D ** -0.5, 0.21875, ((0, 2),))
    frozen_out = centred(splits[14], (N_EP, FF, D), FF ** -0.5, 0.109375, ((0, 2),))
    train_in = centred(splits[15], (N_EP, D, FF), D ** -0.5, 0.21875, ((0, 2),))
    train_out = centred(splits[16], (N_EP, FF, D), FF ** -0.5, 0.109375, ((0, 2),))
    cotangent = centred(splits[17], (GROUPS, GROUP, D), 1.0, 6.0, ((0, 8), (1, 4)))
    return {"tokens": tokens, "segment": segment, "key_mask": key_mask, "routes": routes, "gates": gates, "ln1_gain": ln1_gain, "ln1_bias": ln1_bias, "query_weight": query_weight, "key_weight": key_weight, "value_weight": value_weight, "out_weight": out_weight, "ln2_gain": ln2_gain, "ln2_bias": ln2_bias, "frozen_in": frozen_in, "frozen_out": frozen_out, "train_in": train_in, "train_out": train_out, "cotangent": cotangent}


@jax.custom_vjp
def low(v):
    return lax.optimization_barrier(v.astype(jnp.bfloat16)).astype(jnp.float32)

@jax.custom_vjp
def low_back(v):
    return v

def low_keep(v):
    return (low(v), None)

def low_pass(kept, grad):
    return (grad,)

def back_keep(v):
    return (v, None)

def back_low(kept, grad):
    return (low(grad),)
low.defvjp(low_keep, low_pass)
low_back.defvjp(back_keep, back_low)
HIGH = lax.Precision.HIGHEST
EPSILON = 1e-05
MASKED = -1e+30

def layer_norm(values, gain, bias):
    center = lax.optimization_barrier(jnp.mean(values, axis=-1, keepdims=True))
    shifted = values - center
    spread = lax.optimization_barrier(jnp.mean(shifted * shifted, axis=-1, keepdims=True))
    return shifted * lax.rsqrt(spread + EPSILON) * gain + bias

def score_block(item, keys, values, segment_row, keep_row):
    queries, query_segment = item
    scores = low_back(jnp.einsum('hqd,hkd->hqk', queries, keys, precision=HIGH) * HD ** (-0.5))
    allowed = (query_segment[:, None] == segment_row[None, :]) & keep_row[None, :]
    scores = jnp.where(allowed[None], scores, MASKED)
    highest = lax.optimization_barrier(jnp.max(scores, axis=-1, keepdims=True))
    weights = jnp.exp(scores - highest)
    probs = weights / lax.optimization_barrier(jnp.sum(weights, axis=-1, keepdims=True))
    return jnp.einsum('hqk,hkd->hqd', low(probs), values, precision=HIGH)

def attend_group(item):
    queries, keys, values, segment_row, keep_row = item
    block = min(512, GROUP)
    number = GROUP // block
    query_blocks = queries.reshape(HEADS, number, block, HD).transpose(1, 0, 2, 3)
    segment_blocks = segment_row.reshape(number, block)
    blockwise = jax.checkpoint(score_block)
    outputs = lax.map(lambda pair: blockwise(pair, keys, values, segment_row, keep_row), (query_blocks, segment_blocks))
    return outputs.transpose(1, 0, 2, 3).reshape(HEADS, GROUP, HD)

def forward(tokens, ln1_gain, ln1_bias, query_weight, key_weight, value_weight, out_weight, ln2_gain, ln2_bias, frozen_in, frozen_out, train_in, train_out, segment, keep, table, slot_of, gates):
    normed = low(layer_norm(tokens, ln1_gain, ln1_bias)).reshape(-1, D)

    def project(weight):
        heads = low(low_back(jnp.dot(normed, weight, precision=HIGH)))
        return heads.reshape(GROUPS, GROUP, HEADS, HD).transpose(0, 2, 1, 3)
    attended = lax.map(attend_group, (project(query_weight), project(key_weight), project(value_weight), segment, keep))
    mixed_heads = low(low_back(attended.transpose(0, 2, 1, 3).reshape(-1, D)))
    middle = tokens.reshape(-1, D) + low_back(jnp.dot(mixed_heads, out_weight, precision=HIGH))
    second = low(layer_norm(middle, ln2_gain, ln2_bias))
    padded = jnp.concatenate([second, jnp.zeros((1, D), jnp.float32)], axis=0)
    weight_in = jnp.stack([frozen_in, train_in], axis=1).reshape(EXPERTS, D, FF)
    weight_out = jnp.stack([frozen_out, train_out], axis=1).reshape(EXPERTS, FF, D)

    def run_expert(item):
        rows_of, inner, outer = item
        inputs = low_back(padded[rows_of])
        hidden = low_back(jnp.dot(inputs, inner, precision=HIGH))
        active = low(jax.nn.gelu(hidden, approximate=False))
        return low(low_back(jnp.dot(active, outer, precision=HIGH)))
    results = lax.map(jax.checkpoint(run_expert), (table, weight_in, weight_out)).reshape(-1, D)
    mixture = gates[:, 0:1] * results[slot_of[:, 0]] + gates[:, 1:2] * results[slot_of[:, 1]]
    return (middle + mixture).reshape(GROUPS, GROUP, D)

def reference(tokens, segment, key_mask, routes, gates, ln1_gain, ln1_bias, query_weight, key_weight, value_weight, out_weight, ln2_gain, ln2_bias, frozen_in, frozen_out, train_in, train_out, cotangent):
    first = jnp.concatenate([segment[:, :1] == segment[:, :1], segment[:, 1:] != segment[:, :-1]], axis=1)
    keep = (key_mask == 1) | first
    blocks = GROUPS * N_TP
    whole = GROUPS * GROUP
    flat_routes = routes.reshape(blocks, TOK_DEV * 2)
    marks = (flat_routes[:, :, None] == jnp.arange(EXPERTS, dtype=jnp.int32)[None, None, :]).astype(jnp.int32)
    places = lax.optimization_barrier(jnp.sum((jnp.cumsum(marks, axis=1) - 1) * marks, axis=2))
    block_ids = jnp.arange(blocks, dtype=jnp.int32)[:, None]
    slot_flat = (flat_routes * (blocks * CAP) + block_ids * CAP + places).reshape(whole, 2)
    owners = jnp.broadcast_to(jnp.arange(whole, dtype=jnp.int32)[:, None], (whole, 2))
    table = jnp.full((EXPERTS * blocks * CAP,), whole, jnp.int32).at[slot_flat.reshape(-1)].set(owners.reshape(-1))
    table = table.reshape(EXPERTS, blocks * CAP)
    counts = lax.optimization_barrier(jnp.sum(marks, axis=(0, 1))).astype(jnp.int32)
    floats = [array_in.astype(jnp.float32) for array_in in (tokens, ln1_gain, ln1_bias, query_weight, key_weight, value_weight, out_weight, ln2_gain, ln2_bias, frozen_in, frozen_out, train_in, train_out)]
    gate_rows = gates.reshape(whole, 2).astype(jnp.float32)

    def closed(*params):
        return forward(*params, segment, keep, table, slot_flat, gate_rows)
    result, pullback = jax.vjp(closed, *floats)
    grads = pullback(cotangent.astype(jnp.float32))
    return (result.astype(jnp.bfloat16), grads[0], grads[1], grads[2], grads[3], grads[4], grads[5], grads[6], grads[7], grads[8], grads[11], grads[12], counts)
```

```python
import functools
import math

import jax
import jax.numpy as jnp
from jax import lax
from jax.experimental import pallas as pl
from jax.experimental.pallas import tpu as pltpu
from jax.sharding import PartitionSpec as P

HD = 64
EXP_DEV = 2
EPSILON = 1e-05
MASKED = -1e30
MESH = pl.DeviceIdType.MESH
BF = jnp.bfloat16
F32 = jnp.float32
CHUNK = 64


def tp_peers():
    me = lax.axis_index("tp")
    one = me + 1 - 2 * (me % 2)
    return (me, one, (me + 2) % 4, (one + 2) % 4)


def remote(src, dst, send, recv, where):
    return pltpu.make_async_remote_copy(
        src_ref=src, dst_ref=dst, send_sem=send, recv_sem=recv,
        device_id=where, device_id_type=MESH,
    )


def entry_barrier(ep_count, dp_count):
    barrier = pltpu.get_barrier_semaphore()
    _, tp1, tp2, tp3 = tp_peers()
    ep, dp = lax.axis_index("ep"), lax.axis_index("dp")
    for peer in (tp1, tp2, tp3):
        pl.semaphore_signal(barrier, inc=1, device_id={"tp": peer}, device_id_type=MESH)
    for off in range(1, ep_count):
        pl.semaphore_signal(
            barrier, inc=1, device_id={"ep": (ep + off) % ep_count}, device_id_type=MESH
        )
    for off in range(1, dp_count):
        pl.semaphore_signal(
            barrier, inc=1, device_id={"dp": (dp + off) % dp_count}, device_id_type=MESH
        )
    pl.semaphore_wait(barrier, 3 + ep_count - 1 + dp_count - 1)


def gelu_pair(hidden):
    phi = 0.5 * (1.0 + lax.erf(hidden * math.sqrt(0.5)))
    dens = jnp.exp(-0.5 * hidden * hidden) * (1.0 / math.sqrt(2.0 * math.pi))
    return hidden * phi, phi + hidden * dens


def grads_kernel(
    ep_count, dp_count, n,
    xs_ref, w_in_hbm, w_out_hbm, pg_ref, small_ref,
    rg_hbm, full_ref, small_out,
    gx, gs, w_in, w_out, act, slope, own, red, stage, fin, pslot, acc1, dslot, acc2, sm_tp, sm_ep, sm_dp, sm_a, sm_b,
    g_send, g_recv, w_sem, red_send, red_recv, bc_send, bc_recv, x_send, x_recv, out_sem,
    p_send, p_recv, d_send, d_recv, e_send, e_recv, f_send, f_recv, s_send, s_recv,
):
    tp, tp1, tp2, tp3 = tp_peers()
    ep, dp = lax.axis_index("ep"), lax.axis_index("dp")
    last = dp_count - 1
    quarter = w_in.shape[1]
    width = w_in.shape[0]
    start = pl.multiple_of(tp * quarter, quarter)
    in_copy = pltpu.make_async_copy(w_in_hbm.at[:, pl.ds(start, quarter)], w_in, w_sem.at[0])
    out_copy = pltpu.make_async_copy(w_out_hbm.at[pl.ds(start, quarter), :], w_out, w_sem.at[1])
    in_copy.start()
    out_copy.start()
    entry_barrier(ep_count, dp_count)

    token_copies = {}
    for part, buf in ((0, gx), (1, gs)):
        for hop, peer in ((1, tp1), (2, tp2)):
            token_copies[part, hop] = remote(
                xs_ref.at[part], buf.at[hop], g_send.at[part, hop - 1], g_recv.at[part, hop - 1], {"tp": peer}
            )
            token_copies[part, hop].start()
    ep_copies = []
    for off in range(1, ep_count):
        peer = (ep + off) % ep_count
        ep_copies.append(
            remote(pg_ref.at[peer], pslot.at[off - 1], p_send.at[off - 1], p_recv.at[off - 1], {"ep": peer})
        )
        ep_copies[-1].start()
    small_copies = []
    for hop, peer in ((1, tp1), (2, tp2), (3, tp3)):
        small_copies.append(
            remote(small_ref, sm_tp.at[hop - 1], s_send.at[hop - 1], s_recv.at[hop - 1], {"tp": peer})
        )
        small_copies[-1].start()

    gx[0] = xs_ref[0]
    gs[0] = xs_ref[1]
    in_copy.wait()
    out_copy.wait()

    def hidden_block(index):
        rows = gx.shape[1]
        hidden = jnp.dot(gx[index], w_in[...], preferred_element_type=F32)
        through = lax.dot_general(gs[index], w_out[...], (((1,), (1,)), ((), ())), preferred_element_type=F32)
        value, grad = gelu_pair(hidden)
        act[pl.ds(index * rows, rows), :] = value.astype(BF)
        slope[pl.ds(index * rows, rows), :] = (through * grad).astype(BF)

    hidden_block(0)
    for part in (0, 1):
        token_copies[part, 1].wait_recv()
    hidden_block(1)
    forward = []
    for part, buf in ((0, gx), (1, gs)):
        token_copies[part, 2].wait_recv()
        forward.append(remote(buf.at[2], buf.at[3], g_send.at[part, 2], g_recv.at[part, 2], {"tp": tp1}))
        forward[-1].start()
    hidden_block(2)
    for copy in forward:
        copy.wait_recv()
    hidden_block(3)

    for copy in small_copies:
        copy.wait()
    sm_a[...] = small_ref[...] + sm_tp[0] + sm_tp[1] + sm_tp[2]
    small_ep = []
    for off in range(1, ep_count):
        small_ep.append(
            remote(sm_a, sm_ep.at[off - 1], s_send.at[2 + off], s_recv.at[2 + off], {"ep": (ep + off) % ep_count})
        )
        small_ep[-1].start()
    for copy in ep_copies:
        copy.wait()
    total = pg_ref[ep].astype(F32)
    for off in range(1, ep_count):
        total = total + pslot[off - 1].astype(F32)
    acc1[...] = total.astype(BF)
    dp_copies = []
    for off in range(1, dp_count):
        peer = (dp + off) % dp_count
        dp_copies.append(
            remote(acc1.at[peer], dslot.at[off - 1], d_send.at[off - 1], d_recv.at[off - 1], {"dp": peer})
        )
        dp_copies[-1].start()

    step_rows = 2 * CHUNK

    def outer(index, _):
        rows = pl.ds(pl.multiple_of(index * step_rows, step_rows), step_rows)
        x_all = gx[:, :, rows].reshape(-1, step_rows)
        s_all = gs[...].reshape(-1, width)
        piece = lax.dot_general(x_all, slope[...], (((0,), (0,)), ((), ())), preferred_element_type=F32)
        own[0, rows, :] = piece
        piece = lax.dot_general(act[:, rows], s_all, (((0,), (0,)), ((), ())), preferred_element_type=F32)
        own[1, rows, :] = piece
        return 0

    for index in range(width // step_rows):
        outer(index, 0)

    for copy in small_ep:
        copy.wait()
    total = sm_a[...]
    for off in range(1, ep_count):
        total = total + sm_ep[off - 1]
    sm_b[...] = total
    small_dp = []
    for off in range(1, dp_count):
        slot = 2 + ep_count - 1 + off
        small_dp.append(
            remote(sm_b, sm_dp.at[off - 1], s_send.at[slot], s_recv.at[slot], {"dp": (dp + off) % dp_count})
        )
        small_dp[-1].start()

    def chain(half):
        place = last - dp if half == 0 else dp
        onward = (dp + last) % dp_count if half == 0 else (dp + 1) % dp_count
        backward = (dp + 1) % dp_count if half == 0 else (dp + last) % dp_count
        return place, onward, backward

    def red_copy(half, index, onward):
        return remote(
            stage.at[half, index], red.at[half, index], red_send.at[half, index], red_recv.at[half, index],
            {"dp": onward},
        )

    def bc_copy(half, index, backward):
        return remote(
            fin.at[half, index, 0], fin.at[half, index, 0], bc_send.at[half, index], bc_recv.at[half, index],
            {"dp": backward},
        )

    def x_copy(half, index, hop):
        source, peer = ((0, tp1), (0, tp2), (2, tp1))[hop - 1]
        return remote(
            fin.at[half, index, source], fin.at[half, index, hop],
            x_send.at[hop - 1, half, index], x_recv.at[hop - 1, half, index], {"tp": peer},
        )

    def out_copy_of(half, index):
        return pltpu.make_async_copy(fin.at[half, index], rg_hbm.at[half, index], out_sem.at[half, index])

    def step(s, _):
        for half in (0, 1):
            place, onward, backward = chain(half)
            index = s - place
            rows = pl.ds(pl.multiple_of(index * CHUNK, CHUNK), CHUNK)

            @pl.when((index >= 0) & (index < n))
            def _():
                @pl.when(place == 0)
                def _():
                    stage[half, index] = own[half, rows, :].astype(BF)

                @pl.when(place > 0)
                def _():
                    red_copy(half, index, onward).wait_recv()
                    total = (own[half, rows, :] + red[half, index].astype(F32)).astype(BF)

                    @pl.when(place < last)
                    def _():
                        stage[half, index] = total

                    @pl.when(place == last)
                    def _():
                        fin[half, index, 0] = total

                @pl.when(place < last)
                def _():
                    red_copy(half, index, onward).start()

        for half in (0, 1):
            place, onward, backward = chain(half)
            far = last - place
            done = s - last - far

            @pl.when((done >= 0) & (done < n))
            def _():
                @pl.when(far > 0)
                def _():
                    bc_copy(half, done, backward).wait_recv()

                @pl.when(far < last)
                def _():
                    bc_copy(half, done, backward).start()

                x_copy(half, done, 1).start()
                x_copy(half, done, 2).start()

            second = done - 1

            @pl.when((second >= 0) & (second < n))
            def _():
                x_copy(half, second, 2).wait_recv()
                x_copy(half, second, 3).start()

            third = done - 2

            @pl.when((third >= 0) & (third < n))
            def _():
                x_copy(half, third, 1).wait_recv()
                x_copy(half, third, 3).wait_recv()
                out_copy_of(half, third).start()

        return 0

    mid = last + 3
    lax.fori_loop(0, mid, step, 0)

    for copy in dp_copies:
        copy.wait()
    total = acc1[dp].astype(F32)
    for off in range(1, dp_count):
        total = total + dslot[off - 1].astype(F32)
    acc2[...] = total.astype(BF)
    full_ref[ep, dp] = acc2[...]
    dp_gather = []
    for off in range(1, dp_count):
        dp_gather.append(
            remote(
                acc2, full_ref.at[ep, dp], e_send.at[off - 1], e_recv.at[off - 1], {"dp": (dp + off) % dp_count}
            )
        )
        dp_gather[-1].start()
    for copy in small_dp:
        copy.wait()
    total = sm_b[...]
    for off in range(1, dp_count):
        total = total + sm_dp[off - 1]
    small_out[...] = total

    lax.fori_loop(mid, mid + 5, step, 0)
    for off in range(1, dp_count):
        source = (dp + dp_count - off) % dp_count
        dp_gather[off - 1].wait_send()
        remote(
            acc2, full_ref.at[ep, source], e_send.at[off - 1], e_recv.at[off - 1], {"dp": source}
        ).wait_recv()
    ep_gather = []
    for off in range(1, ep_count):
        ep_gather.append(
            remote(
                full_ref.at[ep], full_ref.at[ep], f_send.at[off - 1], f_recv.at[off - 1],
                {"ep": (ep + off) % ep_count},
            )
        )
        ep_gather[-1].start()
    lax.fori_loop(mid + 5, n + 2 * last + 2, step, 0)
    for off in range(1, ep_count):
        source = (ep + ep_count - off) % ep_count
        ep_gather[off - 1].wait_send()
        remote(
            full_ref.at[source], full_ref.at[source], f_send.at[off - 1], f_recv.at[off - 1], {"ep": source}
        ).wait_recv()

    for copy in token_copies.values():
        copy.wait_send()
    for copy in forward:
        copy.wait_send()

    def drain(index, _):
        for half in (0, 1):
            place, onward, backward = chain(half)

            @pl.when(place < last)
            def _():
                red_copy(half, index, onward).wait_send()

            @pl.when(place > 0)
            def _():
                bc_copy(half, index, backward).wait_send()

            for hop in (1, 2, 3):
                x_copy(half, index, hop).wait_send()
            out_copy_of(half, index).wait()
        return 0

    lax.fori_loop(0, n, drain, 0)


def reduce_grads(xs, w_in, w_out, proj, small):
    ep_count, dp_count = lax.axis_size("ep"), lax.axis_size("dp")
    _, rows, width = xs.shape
    hidden = w_in.shape[1]
    quarter = hidden // 4
    n = width // CHUNK
    assert quarter == width
    shard = width // (ep_count * dp_count)
    pg = proj.reshape(ep_count, dp_count, shard, width)
    dma = pltpu.SemaphoreType.DMA
    vmem = pl.BlockSpec(memory_space=pltpu.VMEM)
    hbm = pl.BlockSpec(memory_space=pl.ANY)
    many = 2 + (ep_count - 1) + (dp_count - 1) + 1
    return pl.pallas_call(
        functools.partial(grads_kernel, ep_count, dp_count, n),
        out_shape=(
            jax.ShapeDtypeStruct((2, n, 4, CHUNK, width), BF),
            jax.ShapeDtypeStruct(pg.shape, BF),
            jax.ShapeDtypeStruct(small.shape, F32),
        ),
        in_specs=[vmem, hbm, hbm, vmem, vmem],
        out_specs=(hbm, vmem, vmem),
        scratch_shapes=[
            pltpu.VMEM((4, rows, width), BF),
            pltpu.VMEM((4, rows, width), BF),
            pltpu.VMEM((width, quarter), BF),
            pltpu.VMEM((quarter, width), BF),
            pltpu.VMEM((4 * rows, quarter), BF),
            pltpu.VMEM((4 * rows, quarter), BF),
            pltpu.VMEM((2, width, width), F32),
            pltpu.VMEM((2, n, CHUNK, width), BF),
            pltpu.VMEM((2, n, CHUNK, width), BF),
            pltpu.VMEM((2, n, 4, CHUNK, width), BF),
            pltpu.VMEM((ep_count - 1, dp_count, shard, width), BF),
            pltpu.VMEM((dp_count, shard, width), BF),
            pltpu.VMEM((dp_count - 1, shard, width), BF),
            pltpu.VMEM((shard, width), BF),
            pltpu.VMEM((3,) + small.shape, F32),
            pltpu.VMEM((ep_count - 1,) + small.shape, F32),
            pltpu.VMEM((dp_count - 1,) + small.shape, F32),
            pltpu.VMEM(small.shape, F32),
            pltpu.VMEM(small.shape, F32),
            dma((2, 3)), dma((2, 3)), dma((2,)),
            dma((2, n)), dma((2, n)), dma((2, n)), dma((2, n)),
            dma((3, 2, n)), dma((3, 2, n)), dma((2, n)),
            dma((ep_count - 1,)), dma((ep_count - 1,)),
            dma((dp_count - 1,)), dma((dp_count - 1,)),
            dma((dp_count - 1,)), dma((dp_count - 1,)),
            dma((ep_count - 1,)), dma((ep_count - 1,)),
            dma((many,)), dma((many,)),
        ],
        compiler_params=pltpu.CompilerParams(
            collective_id=0, has_side_effects=True, vmem_limit_bytes=60 * 1024 * 1024
        ),
        name="grads",
    )(xs, w_in, w_out, pg, small)


def finish_kernel(tp_ref, rg_ref, full_ref, gin_ref, gout_ref, q_ref, k_ref, v_ref, o_ref):
    width = gin_ref.shape[0]
    gin_ref[...] = rg_ref[0, :, 0].reshape(width, -1).astype(F32)
    gout_ref[...] = rg_ref[1, :, 0].reshape(-1, width).astype(F32)

    @pl.when(pl.program_id(0) == 0)
    def _():
        cols = q_ref.shape[1]
        for index, ref in enumerate((q_ref, k_ref, v_ref)):
            ref[...] = full_ref[:, index * cols : (index + 1) * cols].astype(F32)
        o_ref[...] = full_ref[:, 3 * cols :].astype(F32).T


def finish(rg, full, cols):
    _, n, _, chunk, width = rg.shape
    hidden = 4 * width
    me = lax.axis_index("tp").astype(jnp.int32).reshape(1)

    def where(quarter, me_ref):
        mine = me_ref[0]
        low = (quarter % 2) != (mine % 2)
        high = (quarter // 2) != (mine // 2)
        return jnp.where(low, 1, 0) + jnp.where(high, 2, 0)

    whole = lambda shape: pl.BlockSpec(shape, lambda q, t: (0, 0))
    return pl.pallas_call(
        finish_kernel,
        grid_spec=pltpu.PrefetchScalarGridSpec(
            num_scalar_prefetch=1,
            grid=(4,),
            in_specs=[
                pl.BlockSpec((2, n, 1, chunk, width), lambda q, t: (0, 0, where(q, t), 0, 0)),
                whole((width, width)),
            ],
            out_specs=[
                pl.BlockSpec((width, width), lambda q, t: (0, q)),
                pl.BlockSpec((width, width), lambda q, t: (q, 0)),
                whole((width, cols)), whole((width, cols)), whole((width, cols)), whole((cols, width)),
            ],
        ),
        out_shape=[
            jax.ShapeDtypeStruct((width, hidden), F32),
            jax.ShapeDtypeStruct((hidden, width), F32),
            jax.ShapeDtypeStruct((width, cols), F32),
            jax.ShapeDtypeStruct((width, cols), F32),
            jax.ShapeDtypeStruct((width, cols), F32),
            jax.ShapeDtypeStruct((cols, width), F32),
        ],
        name="finish",
    )(me, rg, full.reshape(width, width))


def layer_norm(values, gain, bias):
    center = jnp.mean(values, axis=-1, keepdims=True)
    shifted = values - center
    spread = jnp.mean(shifted * shifted, axis=-1, keepdims=True)
    return shifted * lax.rsqrt(spread + EPSILON) * gain + bias


def gelu_exact(values):
    return jax.nn.gelu(values, approximate=False)


def contract(left, right, left_dim, right_dim):
    return lax.dot_general(
        left, right, (((left_dim,), (right_dim,)), ((), ())), preferred_element_type=jnp.float32
    )


def masked_scores(queries, query_segment, keys, segment_row, keep_row):
    scale = queries.shape[-1] ** (-0.5)
    scores = jnp.einsum("hqd,hkd->hqk", queries, keys, preferred_element_type=jnp.float32) * scale
    allowed = (query_segment[:, None] == segment_row[None, :]) & keep_row[None, :]
    return jnp.where(allowed[None], scores, MASKED)


def to_owners(buffer):
    return lax.all_to_all(buffer, "ep", split_axis=0, concat_axis=0, tiled=True)


def to_sources(buffer):
    return lax.all_to_all(buffer, "ep", split_axis=0, concat_axis=0, tiled=True)


def expert_forward(inputs, inner, outer):
    hidden = contract(inputs, inner, 1, 0)
    active = gelu_exact(hidden).astype(jnp.bfloat16)
    return (hidden, active, contract(active, outer, 1, 0))


def expert_backward(inputs, hidden, active, upstream, inner, outer, trainable):
    through = contract(upstream, outer, 1, 1)
    slope = jax.vjp(gelu_exact, hidden)[1](through)[0].astype(jnp.bfloat16)
    back_in = contract(slope, inner, 1, 1)
    return back_in


def local(
    tokens,
    segment,
    key_mask,
    routes,
    gates,
    ln1_gain,
    ln1_bias,
    query_weight,
    key_weight,
    value_weight,
    out_weight,
    ln2_gain,
    ln2_bias,
    frozen_in,
    frozen_out,
    train_in,
    train_out,
    cotangent,
):
    tp_count = lax.axis_size("tp")
    ep_count = lax.axis_size("ep")
    local_rows = tokens.shape[1]
    width = tokens.shape[2]
    group_rows = local_rows * tp_count
    head_cols = query_weight.shape[1]
    local_heads = head_cols // HD
    residual = tokens[0].astype(jnp.float32)
    joined = jnp.concatenate([query_weight, key_weight, value_weight], axis=1)
    first_normed = layer_norm(residual, ln1_gain, ln1_bias).astype(jnp.bfloat16)
    piece = lax.all_gather(first_normed, "tp", axis=0, tiled=True)
    projected = contract(piece, joined, 1, 0)
    gathered = piece
    projected, normed_group = (projected, gathered)
    projected = projected.astype(jnp.bfloat16)
    block = min(512, group_rows)
    blocks = group_rows // block

    def split_heads(matrix):
        return matrix.reshape(group_rows, local_heads, HD).transpose(1, 0, 2)

    def merge_heads(tensor):
        return tensor.transpose(1, 0, 2).reshape(group_rows, head_cols)

    queries = split_heads(projected[:, :head_cols])
    keys = split_heads(projected[:, head_cols : 2 * head_cols])
    values = split_heads(projected[:, 2 * head_cols :])
    query_blocks = queries.reshape(local_heads, blocks, block, HD).transpose(1, 0, 2, 3)
    segment_row = segment[0]
    starts = jnp.concatenate(
        [segment_row[:1] == segment_row[:1], segment_row[1:] != segment_row[:-1]]
    )
    keep_row = (key_mask[0] == 1) | starts
    segment_blocks = segment_row.reshape(blocks, block)

    def forward_block(item):
        block_queries, block_segment = item
        scores = masked_scores(block_queries, block_segment, keys, segment_row, keep_row)
        highest = jnp.max(scores, axis=-1, keepdims=True)
        weights = jnp.exp(scores - highest)
        totals = jnp.sum(weights, axis=-1, keepdims=True)
        probs = (weights / totals).astype(jnp.bfloat16)
        outputs = jnp.einsum("hqk,hkd->hqd", probs, values, preferred_element_type=jnp.float32)
        return (outputs, (highest + jnp.log(totals))[..., 0])

    head_blocks, log_totals = lax.map(forward_block, (query_blocks, segment_blocks))
    attn_heads = (
        head_blocks.transpose(0, 2, 1, 3).reshape(group_rows, head_cols).astype(jnp.bfloat16)
    )
    middle = residual + lax.psum_scatter(
        contract(attn_heads, out_weight, 1, 0), "tp", scatter_dimension=0, tiled=True
    )
    second_normed = layer_norm(middle, ln2_gain, ln2_bias).astype(jnp.bfloat16)
    experts = EXP_DEV * ep_count
    capacity = 4 * local_rows // experts
    slots = experts * capacity
    route = routes[0]
    marks = (route.reshape(-1)[:, None] == jnp.arange(experts, dtype=jnp.int32)[None, :]).astype(
        jnp.int32
    )
    places = jnp.sum((jnp.cumsum(marks, axis=0) - 1) * marks, axis=1).reshape(local_rows, 2)
    slot_ids = route * capacity + places
    slot_range = jnp.arange(slots, dtype=jnp.int32)[None, :]
    pick_first = (slot_ids[:, 0:1] == slot_range).astype(jnp.bfloat16)
    pick_second = (slot_ids[:, 1:2] == slot_range).astype(jnp.bfloat16)
    local_counts = jnp.sum(marks, axis=0).astype(jnp.float32)
    send = contract(pick_first + pick_second, second_normed, 0, 0).astype(jnp.bfloat16)
    arrived = to_owners(send.reshape(ep_count, EXP_DEV, capacity, width))
    inner_list = (frozen_in[0], train_in[0])
    outer_list = (frozen_out[0], train_out[0])
    kept = []
    produced = []
    for index in range(EXP_DEV):
        inputs = arrived[:, index].reshape(-1, width)
        hidden, active, result = expert_forward(inputs, inner_list[index], outer_list[index])
        kept.append((inputs, hidden, active))
        produced.append(result.reshape(ep_count, -1, width))
    produced = jnp.stack(produced, axis=1)
    returned = to_sources(produced.astype(jnp.bfloat16)).reshape(slots, width)
    gate_rows = gates[0]
    mixture = gate_rows[:, 0:1] * contract(pick_first, returned, 1, 0) + gate_rows[
        :, 1:2
    ] * contract(pick_second, returned, 1, 0)
    layer_out = (middle + mixture).astype(jnp.bfloat16)
    upstream = cotangent[0].astype(jnp.float32)
    first_share = (gate_rows[:, 0:1] * upstream).astype(jnp.bfloat16)
    second_share = (gate_rows[:, 1:2] * upstream).astype(jnp.bfloat16)
    back_send = (
        contract(pick_first, first_share, 0, 0) + contract(pick_second, second_share, 0, 0)
    ).astype(jnp.bfloat16)
    back_arrived = to_owners(back_send.reshape(ep_count, EXP_DEV, capacity, width))
    input_terms = []
    for index in range(EXP_DEV):
        inputs, hidden, active = kept[index]
        back_in = expert_backward(
            inputs,
            hidden,
            active,
            back_arrived[:, index].reshape(-1, width),
            inner_list[index],
            outer_list[index],
            index == EXP_DEV - 1,
        )
        input_terms.append(back_in.reshape(ep_count, -1, width))
    input_terms = jnp.stack(input_terms, axis=1)
    back_returned = to_sources(input_terms.astype(jnp.bfloat16)).reshape(slots, width)
    second_grad = contract(pick_first, back_returned, 1, 0) + contract(
        pick_second, back_returned, 1, 0
    )
    middle_part, ln2_gain_grad, ln2_bias_grad = jax.vjp(layer_norm, middle, ln2_gain, ln2_bias)[1](
        second_grad
    )
    middle_grad = upstream + middle_part
    attn_grad = middle_grad.astype(jnp.bfloat16)
    piece = lax.all_gather(attn_grad, "tp", axis=0, tiled=True)
    head_grad = contract(piece, out_weight, 1, 1)
    out_part = contract(attn_heads, piece, 0, 0)
    head_grad, out_part = (head_grad, out_part)
    upstream_blocks = (
        split_heads(head_grad.astype(jnp.bfloat16))
        .reshape(local_heads, blocks, block, HD)
        .transpose(1, 0, 2, 3)
    )

    def backward_block(carry, item):
        key_sum, value_sum = carry
        block_queries, block_segment, block_totals, block_upstream = item
        scores = masked_scores(block_queries, block_segment, keys, segment_row, keep_row)
        probs = jnp.exp(scores - block_totals[..., None])
        prob_grad = jnp.einsum(
            "hqd,hkd->hqk", block_upstream, values, preferred_element_type=jnp.float32
        )
        centered = jnp.sum(probs * prob_grad, axis=-1, keepdims=True)
        score_grad = (probs * (prob_grad - centered)).astype(jnp.bfloat16)
        scale = block_queries.shape[-1] ** (-0.5)
        query_part = (
            jnp.einsum("hqk,hkd->hqd", score_grad, keys, preferred_element_type=jnp.float32) * scale
        )
        key_sum = (
            key_sum
            + jnp.einsum(
                "hqk,hqd->hkd", score_grad, block_queries, preferred_element_type=jnp.float32
            )
            * scale
        )
        value_sum = value_sum + jnp.einsum(
            "hqk,hqd->hkd",
            probs.astype(jnp.bfloat16),
            block_upstream,
            preferred_element_type=jnp.float32,
        )
        return ((key_sum, value_sum), query_part)

    zero_heads = jnp.zeros((local_heads, group_rows, HD), jnp.float32)
    (key_sum, value_sum), query_parts = lax.scan(
        backward_block,
        (zero_heads, zero_heads),
        (query_blocks, segment_blocks, log_totals, upstream_blocks),
    )
    query_full = query_parts.transpose(0, 2, 1, 3).reshape(group_rows, head_cols)
    projected_grad = jnp.concatenate(
        [query_full, merge_heads(key_sum), merge_heads(value_sum)], axis=1
    ).astype(jnp.bfloat16)
    joined_grad = contract(normed_group, projected_grad, 0, 0)
    first_grad = lax.psum_scatter(
        contract(projected_grad, joined, 1, 1).astype(jnp.bfloat16),
        "tp",
        scatter_dimension=0,
        tiled=True,
    ).astype(jnp.float32)
    residual_part, ln1_gain_grad, ln1_bias_grad = jax.vjp(layer_norm, residual, ln1_gain, ln1_bias)[
        1
    ](first_grad)
    tokens_grad = middle_grad + residual_part
    proj = jnp.concatenate([joined_grad, out_part.T], axis=1).astype(jnp.bfloat16)
    counts_row = jnp.zeros((width,), jnp.float32).at[:experts].set(local_counts)
    small = jnp.stack(
        [ln1_gain_grad, ln1_bias_grad, ln2_gain_grad, ln2_bias_grad, counts_row]
        + [jnp.zeros((width,), jnp.float32)] * 3
    )
    xs = jnp.stack([kept[-1][0], back_arrived[:, EXP_DEV - 1].reshape(-1, width)])
    rg, full, sums = reduce_grads(xs, train_in[0], train_out[0], proj, small)
    grad_in, grad_out, *summed = finish(rg, full, head_cols)
    gain_one, bias_one, gain_two, bias_two = sums[0], sums[1], sums[2], sums[3]
    counts = sums[4, :experts]
    return (
        layer_out[None],
        tokens_grad[None],
        gain_one,
        bias_one,
        summed[0],
        summed[1],
        summed[2],
        summed[3],
        gain_two,
        bias_two,
        grad_in[None],
        grad_out[None],
        counts.astype(jnp.int32),
    )


def solution(mesh):
    in_specs = (
        P(("ep", "dp"), "tp", None),
        P(("ep", "dp"), None),
        P(("ep", "dp"), None),
        P(("ep", "dp"), "tp", None),
        P(("ep", "dp"), "tp", None),
        P(),
        P(),
        P(None, "tp"),
        P(None, "tp"),
        P(None, "tp"),
        P("tp", None),
        P(),
        P(),
        P("ep", None, None),
        P("ep", None, None),
        P("ep", None, None),
        P("ep", None, None),
        P(("ep", "dp"), "tp", None),
    )
    out_specs = (
        P(("ep", "dp"), "tp", None),
        P(("ep", "dp"), "tp", None),
        P(),
        P(),
        P(None, "tp"),
        P(None, "tp"),
        P(None, "tp"),
        P("tp", None),
        P(),
        P(),
        P("ep", None, None),
        P("ep", None, None),
        P(),
    )
    return jax.shard_map(local, mesh=mesh, in_specs=in_specs, out_specs=out_specs, check_vma=False)
```

```python
import functools
import math

import jax
import jax.numpy as jnp
from jax import lax
from jax.experimental import pallas as pl
from jax.experimental.pallas import tpu as pltpu
from jax.sharding import PartitionSpec as P

HD = 64
EXP_DEV = 2
EPSILON = 1e-05
MASKED = -1e30
MESH = pl.DeviceIdType.MESH
BF = jnp.bfloat16
F32 = jnp.float32
CHUNK = 64


def tp_peers():
    me = lax.axis_index("tp")
    one = me + 1 - 2 * (me % 2)
    return (me, one, (me + 2) % 4, (one + 2) % 4)


def remote(src, dst, send, recv, where):
    return pltpu.make_async_remote_copy(
        src_ref=src, dst_ref=dst, send_sem=send, recv_sem=recv,
        device_id=where, device_id_type=MESH,
    )


def entry_barrier(ep_count, dp_count):
    barrier = pltpu.get_barrier_semaphore()
    _, tp1, tp2, tp3 = tp_peers()
    ep, dp = lax.axis_index("ep"), lax.axis_index("dp")
    for peer in (tp1, tp2, tp3):
        pl.semaphore_signal(barrier, inc=1, device_id={"tp": peer}, device_id_type=MESH)
    for off in range(1, ep_count):
        pl.semaphore_signal(
            barrier, inc=1, device_id={"ep": (ep + off) % ep_count}, device_id_type=MESH
        )
    for off in range(1, dp_count):
        pl.semaphore_signal(
            barrier, inc=1, device_id={"dp": (dp + off) % dp_count}, device_id_type=MESH
        )
    pl.semaphore_wait(barrier, 3 + ep_count - 1 + dp_count - 1)


def gelu_pair(hidden):
    phi = 0.5 * (1.0 + lax.erf(hidden * math.sqrt(0.5)))
    dens = jnp.exp(-0.5 * hidden * hidden) * (1.0 / math.sqrt(2.0 * math.pi))
    return hidden * phi, phi + hidden * dens


def ln_rows(values, gain, bias):
    center = jnp.mean(values, axis=-1, keepdims=True)
    shifted = values - center
    spread = jnp.mean(shifted * shifted, axis=-1, keepdims=True)
    return shifted * lax.rsqrt(spread + EPSILON) * gain + bias


def route_picks(routes_ref, capacity, slots):
    first, second = routes_ref[:, 0:1], routes_ref[:, 1:2]
    rows = first.shape[0]
    lane = lax.broadcasted_iota(jnp.int32, (rows, 128), 1)
    marks = jnp.where((lane == first) | (lane == second), 1.0, 0.0)
    row_id = lax.broadcasted_iota(jnp.int32, (rows, rows), 0)
    col_id = lax.broadcasted_iota(jnp.int32, (rows, rows), 1)
    lower = jnp.where(row_id > col_id, 1.0, 0.0).astype(BF)
    before = jnp.dot(lower, marks.astype(BF), preferred_element_type=F32)
    slot = lax.broadcasted_iota(jnp.int32, (rows, slots), 1)
    picks = []
    for route in (first, second):
        place = jnp.sum(jnp.where(lane == route, before, 0.0), axis=1, keepdims=True)
        chosen = route * capacity + place.astype(jnp.int32)
        picks.append(jnp.where(slot == chosen, 1.0, 0.0).astype(BF))
    return picks[0], picks[1], marks


def dot_tn(left, right):
    return lax.dot_general(left, right, (((0,), (0,)), ((), ())), preferred_element_type=F32)


def dot_nt(left, right):
    return lax.dot_general(left, right, (((1,), (1,)), ((), ())), preferred_element_type=F32)


def dot_nn(left, right):
    return jnp.dot(left, right, preferred_element_type=F32)


def front_kernel(
    ep_count, heads,
    tok_ref, seg_ref, key_ref, routes_ref, gates_ref, cot_ref, g1_ref, b1_ref, wq_ref, wk_ref, wv_ref, wo_ref,
    g2_ref, b2_ref, fin_hbm, fout_hbm, tin_hbm, tout_hbm,
    group_ref, qkv_ref, heads_ref, lse_ref, middle_ref, back_ref, out_ref, gx, gs,
    weights, joined, bias, part, core_slot, mix, x_slot, sx, ss, ax, as_, out_acc, back_acc,
    w_sem, a_send, a_recv, c_send, c_recv, m_send, m_recv, e_send, e_recv, t_send, t_recv,
):
    tp, tp1, tp2, tp3 = tp_peers()
    ep = lax.axis_index("ep")
    rows, width = tok_ref.shape
    cols = wq_ref.shape[1]
    hidden = fin_hbm.shape[1]
    capacity = sx.shape[2]
    slots = ep_count * EXP_DEV * capacity
    loads = []
    for index, source in enumerate((fin_hbm, tin_hbm)):
        loads.append(pltpu.make_async_copy(source, weights[0].at[index], w_sem.at[0, index]))
    for index, source in enumerate((fout_hbm, tout_hbm)):
        loads.append(pltpu.make_async_copy(source, weights[1].at[index], w_sem.at[1, index]))

    barrier = pltpu.get_barrier_semaphore()
    for peer in (tp1, tp2, tp3):
        pl.semaphore_signal(barrier, inc=1, device_id={"tp": peer}, device_id_type=MESH)
    for off in range(1, ep_count):
        pl.semaphore_signal(
            barrier, inc=1, device_id={"ep": (ep + off) % ep_count}, device_id_type=MESH
        )
    residual = tok_ref[...].astype(F32)
    group_ref[tp] = ln_rows(residual, g1_ref[...], b1_ref[...]).astype(BF)
    pl.semaphore_wait(barrier, 3 + ep_count - 1)

    def gather_copy(slot, index, peer):
        return remote(group_ref.at[slot], group_ref.at[slot], a_send.at[index], a_recv.at[index], {"tp": peer})

    sends = [gather_copy(tp, 1, tp2), gather_copy(tp, 0, tp1)]
    for copy in sends:
        copy.start()
    for copy in (loads[0], loads[2], loads[1], loads[3]):
        copy.start()

    pick0, pick1, _ = route_picks(routes_ref, capacity, slots)
    upstream = cot_ref[...].astype(F32)
    share0 = (gates_ref[:, 0:1] * upstream).astype(BF)
    share1 = (gates_ref[:, 1:2] * upstream).astype(BF)
    ss[...] = (dot_tn(pick0, share0) + dot_tn(pick1, share1)).astype(BF).reshape(ss.shape)

    def owner_copies(kind, source, target):
        return [
            remote(
                source.at[(ep + off) % ep_count], target.at[ep], e_send.at[kind, off - 1], e_recv.at[kind, off - 1],
                {"ep": (ep + off) % ep_count},
            )
            for off in range(1, ep_count)
        ]

    def owner_waits(kind, target):
        for off in range(1, ep_count):
            source = (ep + ep_count - off) % ep_count
            remote(
                target.at[source], target.at[source], e_send.at[kind, off - 1], e_recv.at[kind, off - 1],
                {"ep": source},
            ).wait_recv()

    share_sends = owner_copies(1, ss, as_)
    for copy in share_sends:
        copy.start()
    as_[ep] = ss[ep]

    for index, ref in enumerate((wq_ref, wk_ref, wv_ref)):
        joined[:, index * cols : (index + 1) * cols] = ref[...]

    segment = seg_ref[...]
    group_rows = segment.shape[1]
    lane = lax.broadcasted_iota(jnp.int32, segment.shape, 1)
    starts = (segment != pltpu.roll(segment, 1, 1)) | (lane == 0)
    keep = (key_ref[...] == 1) | starts
    segment = segment.astype(F32)
    column = jnp.broadcast_to(segment, (8, group_rows)).T[:, 0:1]
    kept = jnp.where(keep, segment, -1.0)
    bias[...] = jnp.where(column == kept, 0.0, MASKED)

    def project(slot):
        at = pl.ds(pl.multiple_of(slot * rows, rows), rows)
        qkv_ref[at, :] = dot_nn(group_ref[slot], joined[...]).astype(BF)

    project(tp)
    gather_copy(tp1, 0, tp1).wait_recv()
    project(tp1)
    gather_copy(tp2, 1, tp2).wait_recv()
    sends.append(gather_copy(tp2, 2, tp1))
    sends[-1].start()
    project(tp2)
    gather_copy(tp3, 2, tp1).wait_recv()
    project(tp3)

    def token_copy(kind, buf, source, hop, peer):
        return remote(source, buf.at[hop], t_send.at[kind, hop - 1], t_recv.at[kind, hop - 1], {"tp": peer})

    owner_waits(1, as_)
    train = EXP_DEV - 1
    token_sends = [
        token_copy(1, gs, as_.at[:, train], 2, tp2), token_copy(1, gs, as_.at[:, train], 1, tp1)
    ]
    for copy in token_sends:
        copy.start()
    gs[0] = as_[:, train]

    scale = HD ** (-0.5)
    block = min(256, group_rows)
    for head in range(heads):
        def attend(index, _, head=head):
            at = pl.ds(pl.multiple_of(index * block, block), block)
            query = qkv_ref[at, head * HD : (head + 1) * HD]
            keys = qkv_ref[:, cols + head * HD : cols + (head + 1) * HD]
            values = qkv_ref[:, 2 * cols + head * HD : 2 * cols + (head + 1) * HD]
            scores = dot_nt(query, keys) * scale + bias[at, :]
            highest = jnp.max(scores, axis=-1, keepdims=True)
            weight = jnp.exp(scores - highest)
            total = jnp.sum(weight, axis=-1, keepdims=True)
            probs = (weight * (1.0 / total)).astype(BF)
            heads_ref[at, head * HD : (head + 1) * HD] = dot_nn(probs, values).astype(BF)
            lse_ref[at, head : head + 1] = highest + jnp.log(total)
            return 0

        for index in range(group_rows // block):
            attend(index, 0)

    def partial(slot):
        at = pl.ds(pl.multiple_of(slot * rows, rows), rows)
        return dot_nn(heads_ref[at, :], wo_ref[...])

    def core_copy(index):
        return remote(part.at[index], core_slot.at[index], c_send.at[index], c_recv.at[index], {"tp": tp1})

    part[0] = partial(tp3)
    core_copy(0).start()
    part[1] = partial(tp1)
    core_copy(1).start()
    crossing = partial(tp2)
    own = residual + partial(tp)
    token_copy(1, gs, as_.at[:, train], 2, tp2).wait_recv()
    token_sends.append(token_copy(1, gs, gs.at[2], 3, tp1))
    token_sends[-1].start()
    core_copy(0).wait_recv()
    mix[...] = (crossing + core_slot[0]).astype(BF)
    cross = remote(mix, x_slot, m_send, m_recv, {"tp": tp2})
    cross.start()
    core_copy(1).wait_recv()
    own = own + core_slot[1]
    cross.wait_recv()
    middle = own + x_slot[...].astype(F32)
    middle_ref[...] = middle
    normed = ln_rows(middle, g2_ref[...], b2_ref[...]).astype(BF)
    sx[...] = dot_tn(pick0 + pick1, normed).astype(BF).reshape(sx.shape)
    input_sends = owner_copies(0, sx, ax)
    for copy in input_sends:
        copy.start()
    ax[ep] = sx[ep]
    for copy in loads:
        copy.wait()
    owner_waits(0, ax)
    token_sends.append(token_copy(0, gx, ax.at[:, train], 2, tp2))
    token_sends.append(token_copy(0, gx, ax.at[:, train], 1, tp1))
    for copy in token_sends[-2:]:
        copy.start()
    gx[0] = ax[:, train]

    step = width
    for expert in range(EXP_DEV):
        inputs = ax[:, expert].reshape(-1, width)
        shares = as_[:, expert].reshape(-1, width)

        def piece(index, _, expert=expert, inputs=inputs, shares=shares):
            at = pl.ds(pl.multiple_of(index * step, step), step)
            inner, outer = weights[0].at[expert], weights[1].at[expert]
            before = dot_nn(inputs, inner[:, at])
            through = dot_nt(shares, outer[at, :])
            value, grad = gelu_pair(before)
            slope = (through * grad).astype(BF)
            produced = dot_nn(value.astype(BF), outer[at, :])
            returned = dot_nt(slope, inner[:, at])

            @pl.when(index == 0)
            def _():
                out_acc[...] = produced
                back_acc[...] = returned

            @pl.when(index > 0)
            def _():
                out_acc[...] += produced
                back_acc[...] += returned

            return 0

        lax.fori_loop(0, hidden // step, piece, 0)
        out_ref[:, expert] = out_acc[...].astype(BF).reshape(ep_count, capacity, width)
        back_ref[:, expert] = back_acc[...].astype(BF).reshape(ep_count, capacity, width)
        if expert == 0:
            token_copy(0, gx, ax.at[:, train], 2, tp2).wait_recv()
            token_sends.append(token_copy(0, gx, gx.at[2], 3, tp1))
            token_sends[-1].start()

    for kind, buf in ((0, gx), (1, gs)):
        token_copy(kind, buf, buf.at[1], 1, tp1).wait_recv()
        token_copy(kind, buf, buf.at[3], 3, tp1).wait_recv()
    for copy in sends + share_sends + input_sends + token_sends + [core_copy(0), core_copy(1), cross]:
        copy.wait_send()


def front(tokens, segment, key_mask, routes, gates, cot, g1, b1, wq, wk, wv, wo, g2, b2, fin, fout, tin, tout):
    ep_count = lax.axis_size("ep")
    rows, width = tokens.shape
    group_rows = segment.shape[1]
    cols = wq.shape[1]
    hidden = fin.shape[1]
    experts = EXP_DEV * ep_count
    capacity = 4 * rows // experts
    dma = pltpu.SemaphoreType.DMA
    vmem = pl.BlockSpec(memory_space=pltpu.VMEM)
    hbm = pl.BlockSpec(memory_space=pl.ANY)
    struct = jax.ShapeDtypeStruct
    block = (ep_count, EXP_DEV, capacity, width)
    gathered = (4, ep_count, capacity, width)
    others = ep_count - 1
    return pl.pallas_call(
        functools.partial(front_kernel, ep_count, cols // HD),
        out_shape=(
            struct((4, rows, width), BF),
            struct((group_rows, 3 * cols), BF),
            struct((group_rows, cols), BF),
            struct((group_rows, 8), F32),
            struct((rows, width), F32),
            struct(block, BF), struct(block, BF), struct(gathered, BF), struct(gathered, BF),
        ),
        in_specs=[vmem] * 14 + [hbm] * 4,
        out_specs=tuple([vmem] * 9),
        scratch_shapes=[
            [pltpu.VMEM((2, width, hidden), BF), pltpu.VMEM((2, hidden, width), BF)],
            pltpu.VMEM((width, 3 * cols), BF),
            pltpu.VMEM((group_rows, group_rows), F32),
            pltpu.VMEM((2, rows, width), F32),
            pltpu.VMEM((2, rows, width), F32),
            pltpu.VMEM((rows, width), BF),
            pltpu.VMEM((rows, width), BF),
            pltpu.VMEM(block, BF), pltpu.VMEM(block, BF), pltpu.VMEM(block, BF), pltpu.VMEM(block, BF),
            pltpu.VMEM((ep_count * capacity, width), F32),
            pltpu.VMEM((ep_count * capacity, width), F32),
            dma((2, 2)), dma((3,)), dma((3,)), dma((2,)), dma((2,)), dma(()), dma(()),
            dma((2, others)), dma((2, others)), dma((2, 3)), dma((2, 3)),
        ],
        compiler_params=pltpu.CompilerParams(
            collective_id=1, has_side_effects=True, vmem_limit_bytes=62 * 1024 * 1024
        ),
        name="front",
    )(tokens, segment, key_mask, routes, gates, cot, g1, b1, wq, wk, wv, wo, g2, b2, fin, fout, tin, tout)


def grads_kernel(
    ep_count, dp_count, n,
    gx_ref, gs_ref, w_in_hbm, w_out_hbm, pg_ref, small_ref,
    rg_hbm, full_ref, small_out,
    w_in, w_out, act, slope, own, red, stage, fin, pslot, acc1, dslot, acc2, sm_tp, sm_ep, sm_dp, sm_a, sm_b,
    w_sem, red_send, red_recv, bc_send, bc_recv, x_send, x_recv, out_sem,
    p_send, p_recv, d_send, d_recv, e_send, e_recv, f_send, f_recv, s_send, s_recv,
):
    tp, tp1, tp2, tp3 = tp_peers()
    ep, dp = lax.axis_index("ep"), lax.axis_index("dp")
    last = dp_count - 1
    quarter = w_in.shape[1]
    width = w_in.shape[0]
    start = pl.multiple_of(tp * quarter, quarter)
    in_copy = pltpu.make_async_copy(w_in_hbm.at[:, pl.ds(start, quarter)], w_in, w_sem.at[0])
    out_copy = pltpu.make_async_copy(w_out_hbm.at[pl.ds(start, quarter), :], w_out, w_sem.at[1])
    in_copy.start()
    out_copy.start()
    entry_barrier(ep_count, dp_count)

    ep_copies = []
    for off in range(1, ep_count):
        peer = (ep + off) % ep_count
        ep_copies.append(
            remote(pg_ref.at[peer], pslot.at[off - 1], p_send.at[off - 1], p_recv.at[off - 1], {"ep": peer})
        )
        ep_copies[-1].start()
    small_copies = []
    for hop, peer in ((1, tp1), (2, tp2), (3, tp3)):
        small_copies.append(
            remote(small_ref, sm_tp.at[hop - 1], s_send.at[hop - 1], s_recv.at[hop - 1], {"tp": peer})
        )
        small_copies[-1].start()

    in_copy.wait()
    out_copy.wait()

    rows = gx_ref.shape[1] * gx_ref.shape[2]

    def hidden_block(index, _):
        hidden = jnp.dot(gx_ref[index].reshape(rows, width), w_in[...], preferred_element_type=F32)
        through = dot_nt(gs_ref[index].reshape(rows, width), w_out[...])
        value, grad = gelu_pair(hidden)
        at = pl.ds(pl.multiple_of(index * rows, rows), rows)
        act[at, :] = value.astype(BF)
        slope[at, :] = (through * grad).astype(BF)
        return 0

    lax.fori_loop(0, 4, hidden_block, 0)

    for copy in small_copies:
        copy.wait()
    sm_a[...] = small_ref[...] + sm_tp[0] + sm_tp[1] + sm_tp[2]
    small_ep = []
    for off in range(1, ep_count):
        small_ep.append(
            remote(sm_a, sm_ep.at[off - 1], s_send.at[2 + off], s_recv.at[2 + off], {"ep": (ep + off) % ep_count})
        )
        small_ep[-1].start()
    for copy in ep_copies:
        copy.wait()
    total = pg_ref[ep].astype(F32)
    for off in range(1, ep_count):
        total = total + pslot[off - 1].astype(F32)
    acc1[...] = total.astype(BF)
    dp_copies = []
    for off in range(1, dp_count):
        peer = (dp + off) % dp_count
        dp_copies.append(
            remote(acc1.at[peer], dslot.at[off - 1], d_send.at[off - 1], d_recv.at[off - 1], {"dp": peer})
        )
        dp_copies[-1].start()

    step_rows = 2 * CHUNK

    def outer(index, _):
        at = pl.ds(pl.multiple_of(index * step_rows, step_rows), step_rows)
        x_all = gx_ref[:, :, :, at].reshape(-1, step_rows)
        s_all = gs_ref[...].reshape(-1, width)
        piece = lax.dot_general(x_all, slope[...], (((0,), (0,)), ((), ())), preferred_element_type=F32)
        own[0, at, :] = piece
        piece = lax.dot_general(act[:, at], s_all, (((0,), (0,)), ((), ())), preferred_element_type=F32)
        own[1, at, :] = piece
        return 0

    for index in range(width // step_rows):
        outer(index, 0)

    for copy in small_ep:
        copy.wait()
    total = sm_a[...]
    for off in range(1, ep_count):
        total = total + sm_ep[off - 1]
    sm_b[...] = total
    small_dp = []
    for off in range(1, dp_count):
        slot = 2 + ep_count - 1 + off
        small_dp.append(
            remote(sm_b, sm_dp.at[off - 1], s_send.at[slot], s_recv.at[slot], {"dp": (dp + off) % dp_count})
        )
        small_dp[-1].start()

    def chain(half):
        place = last - dp if half == 0 else dp
        onward = (dp + last) % dp_count if half == 0 else (dp + 1) % dp_count
        backward = (dp + 1) % dp_count if half == 0 else (dp + last) % dp_count
        return place, onward, backward

    def red_copy(half, index, onward):
        return remote(
            stage.at[half, index], red.at[half, index], red_send.at[half, index], red_recv.at[half, index],
            {"dp": onward},
        )

    def bc_copy(half, index, backward):
        return remote(
            fin.at[half, index, 0], fin.at[half, index, 0], bc_send.at[half, index], bc_recv.at[half, index],
            {"dp": backward},
        )

    def x_copy(half, index, hop):
        source, peer = ((0, tp1), (0, tp2), (2, tp1))[hop - 1]
        return remote(
            fin.at[half, index, source], fin.at[half, index, hop],
            x_send.at[hop - 1, half, index], x_recv.at[hop - 1, half, index], {"tp": peer},
        )

    def out_copy_of(half, index):
        return pltpu.make_async_copy(fin.at[half, index], rg_hbm.at[half, index], out_sem.at[half, index])

    def step(s, _):
        for half in (0, 1):
            place, onward, backward = chain(half)
            index = s - place
            rows = pl.ds(pl.multiple_of(index * CHUNK, CHUNK), CHUNK)

            @pl.when((index >= 0) & (index < n))
            def _():
                @pl.when(place == 0)
                def _():
                    stage[half, index] = own[half, rows, :].astype(BF)

                @pl.when(place > 0)
                def _():
                    red_copy(half, index, onward).wait_recv()
                    total = (own[half, rows, :] + red[half, index].astype(F32)).astype(BF)

                    @pl.when(place < last)
                    def _():
                        stage[half, index] = total

                    @pl.when(place == last)
                    def _():
                        fin[half, index, 0] = total

                @pl.when(place < last)
                def _():
                    red_copy(half, index, onward).start()

        for half in (0, 1):
            place, onward, backward = chain(half)
            far = last - place
            done = s - last - far

            @pl.when((done >= 0) & (done < n))
            def _():
                @pl.when(far > 0)
                def _():
                    bc_copy(half, done, backward).wait_recv()

                @pl.when(far < last)
                def _():
                    bc_copy(half, done, backward).start()

                x_copy(half, done, 1).start()
                x_copy(half, done, 2).start()

            second = done - 1

            @pl.when((second >= 0) & (second < n))
            def _():
                x_copy(half, second, 2).wait_recv()
                x_copy(half, second, 3).start()

            third = done - 2

            @pl.when((third >= 0) & (third < n))
            def _():
                x_copy(half, third, 1).wait_recv()
                x_copy(half, third, 3).wait_recv()
                out_copy_of(half, third).start()

        return 0

    mid = last + 3
    lax.fori_loop(0, mid, step, 0)

    for copy in dp_copies:
        copy.wait()
    total = acc1[dp].astype(F32)
    for off in range(1, dp_count):
        total = total + dslot[off - 1].astype(F32)
    acc2[...] = total.astype(BF)
    full_ref[ep, dp] = acc2[...]
    dp_gather = []
    for off in range(1, dp_count):
        dp_gather.append(
            remote(
                acc2, full_ref.at[ep, dp], e_send.at[off - 1], e_recv.at[off - 1], {"dp": (dp + off) % dp_count}
            )
        )
        dp_gather[-1].start()
    for copy in small_dp:
        copy.wait()
    total = sm_b[...]
    for off in range(1, dp_count):
        total = total + sm_dp[off - 1]
    small_out[...] = total

    lax.fori_loop(mid, mid + 5, step, 0)
    for off in range(1, dp_count):
        source = (dp + dp_count - off) % dp_count
        dp_gather[off - 1].wait_send()
        remote(
            acc2, full_ref.at[ep, source], e_send.at[off - 1], e_recv.at[off - 1], {"dp": source}
        ).wait_recv()
    ep_gather = []
    for off in range(1, ep_count):
        ep_gather.append(
            remote(
                full_ref.at[ep], full_ref.at[ep], f_send.at[off - 1], f_recv.at[off - 1],
                {"ep": (ep + off) % ep_count},
            )
        )
        ep_gather[-1].start()
    lax.fori_loop(mid + 5, n + 2 * last + 2, step, 0)
    for off in range(1, ep_count):
        source = (ep + ep_count - off) % ep_count
        ep_gather[off - 1].wait_send()
        remote(
            full_ref.at[source], full_ref.at[source], f_send.at[off - 1], f_recv.at[off - 1], {"ep": source}
        ).wait_recv()


    def drain(index, _):
        for half in (0, 1):
            place, onward, backward = chain(half)

            @pl.when(place < last)
            def _():
                red_copy(half, index, onward).wait_send()

            @pl.when(place > 0)
            def _():
                bc_copy(half, index, backward).wait_send()

            for hop in (1, 2, 3):
                x_copy(half, index, hop).wait_send()
            out_copy_of(half, index).wait()
        return 0

    lax.fori_loop(0, n, drain, 0)


def reduce_grads(gx, gs, w_in, w_out, proj, small):
    ep_count, dp_count = lax.axis_size("ep"), lax.axis_size("dp")
    width = gx.shape[3]
    rows = gx.shape[1] * gx.shape[2]
    hidden = w_in.shape[1]
    quarter = hidden // 4
    n = width // CHUNK
    assert quarter == width
    shard = width // (ep_count * dp_count)
    pg = proj.reshape(ep_count, dp_count, shard, width)
    dma = pltpu.SemaphoreType.DMA
    vmem = pl.BlockSpec(memory_space=pltpu.VMEM)
    hbm = pl.BlockSpec(memory_space=pl.ANY)
    many = 2 + (ep_count - 1) + (dp_count - 1) + 1
    return pl.pallas_call(
        functools.partial(grads_kernel, ep_count, dp_count, n),
        out_shape=(
            jax.ShapeDtypeStruct((2, n, 4, CHUNK, width), BF),
            jax.ShapeDtypeStruct(pg.shape, BF),
            jax.ShapeDtypeStruct(small.shape, F32),
        ),
        in_specs=[vmem, vmem, hbm, hbm, vmem, vmem],
        out_specs=(hbm, vmem, vmem),
        scratch_shapes=[
            pltpu.VMEM((width, quarter), BF),
            pltpu.VMEM((quarter, width), BF),
            pltpu.VMEM((4 * rows, quarter), BF),
            pltpu.VMEM((4 * rows, quarter), BF),
            pltpu.VMEM((2, width, width), F32),
            pltpu.VMEM((2, n, CHUNK, width), BF),
            pltpu.VMEM((2, n, CHUNK, width), BF),
            pltpu.VMEM((2, n, 4, CHUNK, width), BF),
            pltpu.VMEM((ep_count - 1, dp_count, shard, width), BF),
            pltpu.VMEM((dp_count, shard, width), BF),
            pltpu.VMEM((dp_count - 1, shard, width), BF),
            pltpu.VMEM((shard, width), BF),
            pltpu.VMEM((3,) + small.shape, F32),
            pltpu.VMEM((ep_count - 1,) + small.shape, F32),
            pltpu.VMEM((dp_count - 1,) + small.shape, F32),
            pltpu.VMEM(small.shape, F32),
            pltpu.VMEM(small.shape, F32),
            dma((2,)),
            dma((2, n)), dma((2, n)), dma((2, n)), dma((2, n)),
            dma((3, 2, n)), dma((3, 2, n)), dma((2, n)),
            dma((ep_count - 1,)), dma((ep_count - 1,)),
            dma((dp_count - 1,)), dma((dp_count - 1,)),
            dma((dp_count - 1,)), dma((dp_count - 1,)),
            dma((ep_count - 1,)), dma((ep_count - 1,)),
            dma((many,)), dma((many,)),
        ],
        compiler_params=pltpu.CompilerParams(
            collective_id=0, has_side_effects=True, vmem_limit_bytes=60 * 1024 * 1024
        ),
        name="grads",
    )(gx, gs, w_in, w_out, pg, small)


def finish_kernel(tp_ref, rg_ref, full_ref, gin_ref, gout_ref, q_ref, k_ref, v_ref, o_ref):
    width = gin_ref.shape[0]
    gin_ref[...] = rg_ref[0, :, 0].reshape(width, -1).astype(F32)
    gout_ref[...] = rg_ref[1, :, 0].reshape(-1, width).astype(F32)

    @pl.when(pl.program_id(0) == 0)
    def _():
        cols = q_ref.shape[1]
        for index, ref in enumerate((q_ref, k_ref, v_ref)):
            ref[...] = full_ref[:, index * cols : (index + 1) * cols].astype(F32)
        o_ref[...] = full_ref[:, 3 * cols :].astype(F32).T


def finish(rg, full, cols):
    _, n, _, chunk, width = rg.shape
    hidden = 4 * width
    me = lax.axis_index("tp").astype(jnp.int32).reshape(1)

    def where(quarter, me_ref):
        mine = me_ref[0]
        low = (quarter % 2) != (mine % 2)
        high = (quarter // 2) != (mine // 2)
        return jnp.where(low, 1, 0) + jnp.where(high, 2, 0)

    whole = lambda shape: pl.BlockSpec(shape, lambda q, t: (0, 0))
    return pl.pallas_call(
        finish_kernel,
        grid_spec=pltpu.PrefetchScalarGridSpec(
            num_scalar_prefetch=1,
            grid=(4,),
            in_specs=[
                pl.BlockSpec((2, n, 1, chunk, width), lambda q, t: (0, 0, where(q, t), 0, 0)),
                whole((width, width)),
            ],
            out_specs=[
                pl.BlockSpec((width, width), lambda q, t: (0, q)),
                pl.BlockSpec((width, width), lambda q, t: (q, 0)),
                whole((width, cols)), whole((width, cols)), whole((width, cols)), whole((cols, width)),
            ],
        ),
        out_shape=[
            jax.ShapeDtypeStruct((width, hidden), F32),
            jax.ShapeDtypeStruct((hidden, width), F32),
            jax.ShapeDtypeStruct((width, cols), F32),
            jax.ShapeDtypeStruct((width, cols), F32),
            jax.ShapeDtypeStruct((width, cols), F32),
            jax.ShapeDtypeStruct((cols, width), F32),
        ],
        name="finish",
    )(me, rg, full.reshape(width, width))


def layer_norm(values, gain, bias):
    center = jnp.mean(values, axis=-1, keepdims=True)
    shifted = values - center
    spread = jnp.mean(shifted * shifted, axis=-1, keepdims=True)
    return shifted * lax.rsqrt(spread + EPSILON) * gain + bias


def gelu_exact(values):
    return jax.nn.gelu(values, approximate=False)


def contract(left, right, left_dim, right_dim):
    return lax.dot_general(
        left, right, (((left_dim,), (right_dim,)), ((), ())), preferred_element_type=jnp.float32
    )


def masked_scores(queries, query_segment, keys, segment_row, keep_row):
    scale = queries.shape[-1] ** (-0.5)
    scores = jnp.einsum("hqd,hkd->hqk", queries, keys, preferred_element_type=jnp.float32) * scale
    allowed = (query_segment[:, None] == segment_row[None, :]) & keep_row[None, :]
    return jnp.where(allowed[None], scores, MASKED)


def to_sources(buffer):
    return lax.all_to_all(buffer, "ep", split_axis=0, concat_axis=0, tiled=True)


def local(
    tokens,
    segment,
    key_mask,
    routes,
    gates,
    ln1_gain,
    ln1_bias,
    query_weight,
    key_weight,
    value_weight,
    out_weight,
    ln2_gain,
    ln2_bias,
    frozen_in,
    frozen_out,
    train_in,
    train_out,
    cotangent,
):
    tp_count = lax.axis_size("tp")
    ep_count = lax.axis_size("ep")
    local_rows = tokens.shape[1]
    width = tokens.shape[2]
    group_rows = local_rows * tp_count
    head_cols = query_weight.shape[1]
    local_heads = head_cols // HD
    residual = tokens[0].astype(jnp.float32)
    joined = jnp.concatenate([query_weight, key_weight, value_weight], axis=1)
    line = lambda vector: vector.reshape(1, width)
    group, projected, attn_heads, lse, middle, back_rows, out_rows, gx, gs = front(
        tokens[0], segment, key_mask, routes[0], gates[0], cotangent[0], line(ln1_gain), line(ln1_bias),
        query_weight, key_weight, value_weight, out_weight, line(ln2_gain), line(ln2_bias),
        frozen_in[0], frozen_out[0], train_in[0], train_out[0],
    )
    normed_group = group.reshape(group_rows, width)
    log_totals = lse[:, :local_heads].T[None]
    block = min(512, group_rows)
    blocks = group_rows // block

    def split_heads(matrix):
        return matrix.reshape(group_rows, local_heads, HD).transpose(1, 0, 2)

    def merge_heads(tensor):
        return tensor.transpose(1, 0, 2).reshape(group_rows, head_cols)

    queries = split_heads(projected[:, :head_cols])
    keys = split_heads(projected[:, head_cols : 2 * head_cols])
    values = split_heads(projected[:, 2 * head_cols :])
    query_blocks = queries.reshape(local_heads, blocks, block, HD).transpose(1, 0, 2, 3)
    segment_row = segment[0]
    starts = jnp.concatenate(
        [segment_row[:1] == segment_row[:1], segment_row[1:] != segment_row[:-1]]
    )
    keep_row = (key_mask[0] == 1) | starts
    segment_blocks = segment_row.reshape(blocks, block)

    experts = EXP_DEV * ep_count
    capacity = 4 * local_rows // experts
    slots = experts * capacity
    route = routes[0]
    marks = (route.reshape(-1)[:, None] == jnp.arange(experts, dtype=jnp.int32)[None, :]).astype(
        jnp.int32
    )
    places = jnp.sum((jnp.cumsum(marks, axis=0) - 1) * marks, axis=1).reshape(local_rows, 2)
    slot_ids = route * capacity + places
    slot_range = jnp.arange(slots, dtype=jnp.int32)[None, :]
    pick_first = (slot_ids[:, 0:1] == slot_range).astype(jnp.bfloat16)
    pick_second = (slot_ids[:, 1:2] == slot_range).astype(jnp.bfloat16)
    local_counts = jnp.sum(marks, axis=0).astype(jnp.float32)
    returned = to_sources(out_rows).reshape(slots, width)
    gate_rows = gates[0]
    mixture = gate_rows[:, 0:1] * contract(pick_first, returned, 1, 0) + gate_rows[
        :, 1:2
    ] * contract(pick_second, returned, 1, 0)
    layer_out = (middle + mixture).astype(jnp.bfloat16)
    upstream = cotangent[0].astype(jnp.float32)
    back_returned = to_sources(back_rows).reshape(slots, width)
    second_grad = contract(pick_first, back_returned, 1, 0) + contract(
        pick_second, back_returned, 1, 0
    )
    middle_part, ln2_gain_grad, ln2_bias_grad = jax.vjp(layer_norm, middle, ln2_gain, ln2_bias)[1](
        second_grad
    )
    middle_grad = upstream + middle_part
    attn_grad = middle_grad.astype(jnp.bfloat16)
    piece = lax.all_gather(attn_grad, "tp", axis=0, tiled=True)
    head_grad = contract(piece, out_weight, 1, 1)
    out_part = contract(attn_heads, piece, 0, 0)
    head_grad, out_part = (head_grad, out_part)
    upstream_blocks = (
        split_heads(head_grad.astype(jnp.bfloat16))
        .reshape(local_heads, blocks, block, HD)
        .transpose(1, 0, 2, 3)
    )

    def backward_block(carry, item):
        key_sum, value_sum = carry
        block_queries, block_segment, block_totals, block_upstream = item
        scores = masked_scores(block_queries, block_segment, keys, segment_row, keep_row)
        probs = jnp.exp(scores - block_totals[..., None])
        prob_grad = jnp.einsum(
            "hqd,hkd->hqk", block_upstream, values, preferred_element_type=jnp.float32
        )
        centered = jnp.sum(probs * prob_grad, axis=-1, keepdims=True)
        score_grad = (probs * (prob_grad - centered)).astype(jnp.bfloat16)
        scale = block_queries.shape[-1] ** (-0.5)
        query_part = (
            jnp.einsum("hqk,hkd->hqd", score_grad, keys, preferred_element_type=jnp.float32) * scale
        )
        key_sum = (
            key_sum
            + jnp.einsum(
                "hqk,hqd->hkd", score_grad, block_queries, preferred_element_type=jnp.float32
            )
            * scale
        )
        value_sum = value_sum + jnp.einsum(
            "hqk,hqd->hkd",
            probs.astype(jnp.bfloat16),
            block_upstream,
            preferred_element_type=jnp.float32,
        )
        return ((key_sum, value_sum), query_part)

    zero_heads = jnp.zeros((local_heads, group_rows, HD), jnp.float32)
    (key_sum, value_sum), query_parts = lax.scan(
        backward_block,
        (zero_heads, zero_heads),
        (query_blocks, segment_blocks, log_totals, upstream_blocks),
    )
    query_full = query_parts.transpose(0, 2, 1, 3).reshape(group_rows, head_cols)
    projected_grad = jnp.concatenate(
        [query_full, merge_heads(key_sum), merge_heads(value_sum)], axis=1
    ).astype(jnp.bfloat16)
    joined_grad = contract(normed_group, projected_grad, 0, 0)
    first_grad = lax.psum_scatter(
        contract(projected_grad, joined, 1, 1).astype(jnp.bfloat16),
        "tp",
        scatter_dimension=0,
        tiled=True,
    ).astype(jnp.float32)
    residual_part, ln1_gain_grad, ln1_bias_grad = jax.vjp(layer_norm, residual, ln1_gain, ln1_bias)[
        1
    ](first_grad)
    tokens_grad = middle_grad + residual_part
    proj = jnp.concatenate([joined_grad, out_part.T], axis=1).astype(jnp.bfloat16)
    counts_row = jnp.zeros((width,), jnp.float32).at[:experts].set(local_counts)
    small = jnp.stack(
        [ln1_gain_grad, ln1_bias_grad, ln2_gain_grad, ln2_bias_grad, counts_row]
        + [jnp.zeros((width,), jnp.float32)] * 3
    )
    rg, full, sums = reduce_grads(gx, gs, train_in[0], train_out[0], proj, small)
    grad_in, grad_out, *summed = finish(rg, full, head_cols)
    gain_one, bias_one, gain_two, bias_two = sums[0], sums[1], sums[2], sums[3]
    counts = sums[4, :experts]
    return (
        layer_out[None],
        tokens_grad[None],
        gain_one,
        bias_one,
        summed[0],
        summed[1],
        summed[2],
        summed[3],
        gain_two,
        bias_two,
        grad_in[None],
        grad_out[None],
        counts.astype(jnp.int32),
    )


def solution(mesh):
    in_specs = (
        P(("ep", "dp"), "tp", None),
        P(("ep", "dp"), None),
        P(("ep", "dp"), None),
        P(("ep", "dp"), "tp", None),
        P(("ep", "dp"), "tp", None),
        P(),
        P(),
        P(None, "tp"),
        P(None, "tp"),
        P(None, "tp"),
        P("tp", None),
        P(),
        P(),
        P("ep", None, None),
        P("ep", None, None),
        P("ep", None, None),
        P("ep", None, None),
        P(("ep", "dp"), "tp", None),
    )
    out_specs = (
        P(("ep", "dp"), "tp", None),
        P(("ep", "dp"), "tp", None),
        P(),
        P(),
        P(None, "tp"),
        P(None, "tp"),
        P(None, "tp"),
        P("tp", None),
        P(),
        P(),
        P("ep", None, None),
        P("ep", None, None),
        P(),
    )
    return jax.shard_map(local, mesh=mesh, in_specs=in_specs, out_specs=out_specs, check_vma=False)
```

```python
import functools
import math

import jax
import jax.numpy as jnp
from jax import lax
from jax.experimental import pallas as pl
from jax.experimental.pallas import tpu as pltpu
from jax.sharding import PartitionSpec as P

HD = 64
EXP_DEV = 2
EPSILON = 1e-05
MASKED = -1e30
MESH = pl.DeviceIdType.MESH
BF = jnp.bfloat16
F32 = jnp.float32
CHUNK = 32


def tp_peers():
    me = lax.axis_index("tp")
    one = me + 1 - 2 * (me % 2)
    return (me, one, (me + 2) % 4, (one + 2) % 4)


def remote(src, dst, send, recv, where):
    return pltpu.make_async_remote_copy(
        src_ref=src, dst_ref=dst, send_sem=send, recv_sem=recv,
        device_id=where, device_id_type=MESH,
    )


def entry_barrier(ep_count, dp_count):
    barrier = pltpu.get_barrier_semaphore()
    _, tp1, tp2, tp3 = tp_peers()
    ep, dp = lax.axis_index("ep"), lax.axis_index("dp")
    for peer in (tp1, tp2, tp3):
        pl.semaphore_signal(barrier, inc=1, device_id={"tp": peer}, device_id_type=MESH)
    for off in range(1, ep_count):
        pl.semaphore_signal(
            barrier, inc=1, device_id={"ep": (ep + off) % ep_count}, device_id_type=MESH
        )
    for off in range(1, dp_count):
        pl.semaphore_signal(
            barrier, inc=1, device_id={"dp": (dp + off) % dp_count}, device_id_type=MESH
        )
    pl.semaphore_wait(barrier, 3 + ep_count - 1 + dp_count - 1)


def gelu_pair(hidden):
    phi = 0.5 * (1.0 + lax.erf(hidden * math.sqrt(0.5)))
    dens = jnp.exp(-0.5 * hidden * hidden) * (1.0 / math.sqrt(2.0 * math.pi))
    return hidden * phi, phi + hidden * dens


def row_of(ref):
    return ref[...].reshape(1, -1)


def columns_of(ref):
    value = ref[...].astype(F32)
    padded = jnp.concatenate([value, jnp.zeros((6, value.shape[1]), F32)], axis=0)
    flipped = padded.T
    return flipped[:, 0:1], flipped[:, 1:2]


def fill_bias(seg_ref, key_ref, bias):
    segment = seg_ref[...]
    group_rows = segment.shape[1]
    lane = lax.broadcasted_iota(jnp.int32, segment.shape, 1)
    starts = (segment != pltpu.roll(segment, 1, 1)) | (lane == 0)
    keep = (key_ref[...] == 1) | starts
    segment = segment.astype(F32)
    column = jnp.broadcast_to(segment, (8, group_rows)).T[:, 0:1]
    kept = jnp.where(keep, segment, -1.0)
    bias[...] = jnp.where(column == kept, 0.0, MASKED)


def ln_rows(values, gain, bias):
    center = jnp.mean(values, axis=-1, keepdims=True)
    shifted = values - center
    spread = jnp.mean(shifted * shifted, axis=-1, keepdims=True)
    return shifted * lax.rsqrt(spread + EPSILON) * gain + bias


def route_picks(routes_ref, capacity, slots):
    first, second = (column.astype(jnp.int32) for column in columns_of(routes_ref))
    rows = first.shape[0]
    lane = lax.broadcasted_iota(jnp.int32, (rows, 128), 1)
    marks = jnp.where((lane == first) | (lane == second), 1.0, 0.0)
    row_id = lax.broadcasted_iota(jnp.int32, (rows, rows), 0)
    col_id = lax.broadcasted_iota(jnp.int32, (rows, rows), 1)
    lower = jnp.where(row_id > col_id, 1.0, 0.0).astype(BF)
    before = jnp.dot(lower, marks.astype(BF), preferred_element_type=F32)
    slot = lax.broadcasted_iota(jnp.int32, (rows, slots), 1)
    picks = []
    for route in (first, second):
        place = jnp.sum(jnp.where(lane == route, before, 0.0), axis=1, keepdims=True)
        chosen = route * capacity + place.astype(jnp.int32)
        picks.append(jnp.where(slot == chosen, 1.0, 0.0).astype(BF))
    return picks[0], picks[1], marks


def dot_tn(left, right):
    return lax.dot_general(left, right, (((0,), (0,)), ((), ())), preferred_element_type=F32)


def dot_nt(left, right):
    return lax.dot_general(left, right, (((1,), (1,)), ((), ())), preferred_element_type=F32)


def dot_nn(left, right):
    return jnp.dot(left, right, preferred_element_type=F32)


def front_kernel(
    ep_count, heads,
    tok_ref, seg_ref, key_ref, routes_ref, gates_ref, cot_ref, g1_ref, b1_ref, wq_ref, wk_ref, wv_ref, wo_ref,
    g2_ref, b2_ref, fin_hbm, fout_hbm, tin_hbm, tout_hbm,
    group_ref, qkv_ref, heads_ref, lse_ref, middle_ref, back_ref, out_ref, gx, gs,
    weights, joined, bias, part, core_slot, mix, x_slot, sx, ss, ax, as_, out_acc, back_acc,
    w_sem, a_send, a_recv, c_send, c_recv, m_send, m_recv, e_send, e_recv, t_send, t_recv,
):
    tp, tp1, tp2, tp3 = tp_peers()
    ep = lax.axis_index("ep")
    rows, width = tok_ref.shape
    cols = wq_ref.shape[0]
    hidden = fin_hbm.shape[1]
    capacity = sx.shape[2]
    slots = ep_count * EXP_DEV * capacity
    loads = []
    for index, source in enumerate((fin_hbm, tin_hbm)):
        loads.append(pltpu.make_async_copy(source, weights[0].at[index], w_sem.at[0, index]))
    for index, source in enumerate((fout_hbm, tout_hbm)):
        loads.append(pltpu.make_async_copy(source, weights[1].at[index], w_sem.at[1, index]))

    barrier = pltpu.get_barrier_semaphore()
    for peer in (tp1, tp2, tp3):
        pl.semaphore_signal(barrier, inc=1, device_id={"tp": peer}, device_id_type=MESH)
    for off in range(1, ep_count):
        pl.semaphore_signal(
            barrier, inc=1, device_id={"ep": (ep + off) % ep_count}, device_id_type=MESH
        )
    residual = tok_ref[...].astype(F32)
    group_ref[tp] = ln_rows(residual, row_of(g1_ref), row_of(b1_ref)).astype(BF)
    pl.semaphore_wait(barrier, 3 + ep_count - 1)

    def gather_copy(slot, index, peer):
        return remote(group_ref.at[slot], group_ref.at[slot], a_send.at[index], a_recv.at[index], {"tp": peer})

    sends = [gather_copy(tp, 1, tp2), gather_copy(tp, 0, tp1)]
    for copy in sends:
        copy.start()
    for copy in (loads[0], loads[2], loads[1], loads[3]):
        copy.start()

    pick0, pick1, _ = route_picks(routes_ref, capacity, slots)
    upstream = cot_ref[...].astype(F32)
    gate0, gate1 = columns_of(gates_ref)
    share0 = (gate0 * upstream).astype(BF)
    share1 = (gate1 * upstream).astype(BF)
    ss[...] = (dot_tn(pick0, share0) + dot_tn(pick1, share1)).astype(BF).reshape(ss.shape)

    def owner_copies(kind, source, target):
        return [
            remote(
                source.at[(ep + off) % ep_count], target.at[ep], e_send.at[kind, off - 1], e_recv.at[kind, off - 1],
                {"ep": (ep + off) % ep_count},
            )
            for off in range(1, ep_count)
        ]

    def owner_waits(kind, target):
        for off in range(1, ep_count):
            source = (ep + ep_count - off) % ep_count
            remote(
                target.at[source], target.at[source], e_send.at[kind, off - 1], e_recv.at[kind, off - 1],
                {"ep": source},
            ).wait_recv()

    share_sends = owner_copies(1, ss, as_)
    for copy in share_sends:
        copy.start()
    as_[ep] = ss[ep]

    for index, ref in enumerate((wq_ref, wk_ref, wv_ref)):
        joined[index * cols : (index + 1) * cols, :] = ref[...]

    group_rows = seg_ref.shape[1]
    fill_bias(seg_ref, key_ref, bias)

    def project(slot):
        at = pl.ds(pl.multiple_of(slot * rows, rows), rows)
        qkv_ref[at, :] = dot_nt(group_ref[slot], joined[...]).astype(BF)

    project(tp)
    gather_copy(tp1, 0, tp1).wait_recv()
    project(tp1)
    gather_copy(tp2, 1, tp2).wait_recv()
    sends.append(gather_copy(tp2, 2, tp1))
    sends[-1].start()
    project(tp2)
    gather_copy(tp3, 2, tp1).wait_recv()
    project(tp3)

    def token_copy(kind, buf, source, hop, peer):
        return remote(source, buf.at[hop], t_send.at[kind, hop - 1], t_recv.at[kind, hop - 1], {"tp": peer})

    owner_waits(1, as_)
    train = EXP_DEV - 1
    token_sends = [
        token_copy(1, gs, as_.at[:, train], 2, tp2), token_copy(1, gs, as_.at[:, train], 1, tp1)
    ]
    for copy in token_sends:
        copy.start()
    gs[0] = as_[:, train]

    scale = HD ** (-0.5)
    block = min(256, group_rows)
    for head in range(heads):
        def attend(index, _, head=head):
            at = pl.ds(pl.multiple_of(index * block, block), block)
            query = qkv_ref[at, head * HD : (head + 1) * HD]
            keys = qkv_ref[:, cols + head * HD : cols + (head + 1) * HD]
            values = qkv_ref[:, 2 * cols + head * HD : 2 * cols + (head + 1) * HD]
            scores = dot_nt(query, keys) * scale + bias[at, :]
            highest = jnp.max(scores, axis=-1, keepdims=True)
            weight = jnp.exp(scores - highest)
            total = jnp.sum(weight, axis=-1, keepdims=True)
            probs = (weight * (1.0 / total)).astype(BF)
            heads_ref[at, head * HD : (head + 1) * HD] = dot_nn(probs, values).astype(BF)
            lse_ref[at, head : head + 1] = highest + jnp.log(total)
            return 0

        for index in range(group_rows // block):
            attend(index, 0)

    def partial(slot):
        at = pl.ds(pl.multiple_of(slot * rows, rows), rows)
        return dot_nn(heads_ref[at, :], wo_ref[...])

    def core_copy(index):
        return remote(part.at[index], core_slot.at[index], c_send.at[index], c_recv.at[index], {"tp": tp1})

    part[0] = partial(tp3)
    core_copy(0).start()
    part[1] = partial(tp1)
    core_copy(1).start()
    crossing = partial(tp2)
    own = residual + partial(tp)
    token_copy(1, gs, as_.at[:, train], 2, tp2).wait_recv()
    token_sends.append(token_copy(1, gs, gs.at[2], 3, tp1))
    token_sends[-1].start()
    core_copy(0).wait_recv()
    mix[...] = (crossing + core_slot[0]).astype(BF)
    cross = remote(mix, x_slot, m_send, m_recv, {"tp": tp2})
    cross.start()
    core_copy(1).wait_recv()
    own = own + core_slot[1]
    cross.wait_recv()
    middle = own + x_slot[...].astype(F32)
    middle_ref[...] = middle
    normed = ln_rows(middle, row_of(g2_ref), row_of(b2_ref)).astype(BF)
    sx[...] = dot_tn(pick0 + pick1, normed).astype(BF).reshape(sx.shape)
    input_sends = owner_copies(0, sx, ax)
    for copy in input_sends:
        copy.start()
    ax[ep] = sx[ep]
    for copy in loads:
        copy.wait()
    owner_waits(0, ax)
    token_sends.append(token_copy(0, gx, ax.at[:, train], 2, tp2))
    token_sends.append(token_copy(0, gx, ax.at[:, train], 1, tp1))
    for copy in token_sends[-2:]:
        copy.start()
    gx[0] = ax[:, train]

    step = width
    for expert in range(EXP_DEV):
        inputs = ax[:, expert].reshape(-1, width)
        shares = as_[:, expert].reshape(-1, width)

        def piece(index, _, expert=expert, inputs=inputs, shares=shares):
            at = pl.ds(pl.multiple_of(index * step, step), step)
            inner, outer = weights[0].at[expert], weights[1].at[expert]
            before = dot_nn(inputs, inner[:, at])
            through = dot_nt(shares, outer[at, :])
            value, grad = gelu_pair(before)
            slope = (through * grad).astype(BF)
            produced = dot_nn(value.astype(BF), outer[at, :])
            returned = dot_nt(slope, inner[:, at])

            @pl.when(index == 0)
            def _():
                out_acc[...] = produced
                back_acc[...] = returned

            @pl.when(index > 0)
            def _():
                out_acc[...] += produced
                back_acc[...] += returned

            return 0

        lax.fori_loop(0, hidden // step, piece, 0)
        out_ref[:, expert] = out_acc[...].astype(BF).reshape(ep_count, capacity, width)
        back_ref[:, expert] = back_acc[...].astype(BF).reshape(ep_count, capacity, width)
        if expert == 0:
            token_copy(0, gx, ax.at[:, train], 2, tp2).wait_recv()
            token_sends.append(token_copy(0, gx, gx.at[2], 3, tp1))
            token_sends[-1].start()

    for kind, buf in ((0, gx), (1, gs)):
        token_copy(kind, buf, buf.at[1], 1, tp1).wait_recv()
        token_copy(kind, buf, buf.at[3], 3, tp1).wait_recv()
    for copy in sends + share_sends + input_sends + token_sends + [core_copy(0), core_copy(1), cross]:
        copy.wait_send()


def front(tokens, segment, key_mask, routes, gates, cot, g1, b1, wq, wk, wv, wo, g2, b2, fin, fout, tin, tout):
    ep_count = lax.axis_size("ep")
    rows, width = tokens.shape
    group_rows = segment.shape[1]
    cols = wq.shape[0]
    hidden = fin.shape[1]
    experts = EXP_DEV * ep_count
    capacity = 4 * rows // experts
    dma = pltpu.SemaphoreType.DMA
    vmem = pl.BlockSpec(memory_space=pltpu.VMEM)
    hbm = pl.BlockSpec(memory_space=pl.ANY)
    struct = jax.ShapeDtypeStruct
    block = (ep_count, EXP_DEV, capacity, width)
    gathered = (4, ep_count, capacity, width)
    others = ep_count - 1
    return pl.pallas_call(
        functools.partial(front_kernel, ep_count, cols // HD),
        out_shape=(
            struct((4, rows, width), BF),
            struct((group_rows, 3 * cols), BF),
            struct((group_rows, cols), BF),
            struct((group_rows, 8), F32),
            struct((rows, width), F32),
            struct(block, BF), struct(block, BF), struct(gathered, BF), struct(gathered, BF),
        ),
        in_specs=[vmem] * 14 + [hbm] * 4,
        out_specs=tuple([vmem] * 9),
        scratch_shapes=[
            [pltpu.VMEM((2, width, hidden), BF), pltpu.VMEM((2, hidden, width), BF)],
            pltpu.VMEM((3 * cols, width), BF),
            pltpu.VMEM((group_rows, group_rows), F32),
            pltpu.VMEM((2, rows, width), F32),
            pltpu.VMEM((2, rows, width), F32),
            pltpu.VMEM((rows, width), BF),
            pltpu.VMEM((rows, width), BF),
            pltpu.VMEM(block, BF), pltpu.VMEM(block, BF), pltpu.VMEM(block, BF), pltpu.VMEM(block, BF),
            pltpu.VMEM((ep_count * capacity, width), F32),
            pltpu.VMEM((ep_count * capacity, width), F32),
            dma((2, 2)), dma((3,)), dma((3,)), dma((2,)), dma((2,)), dma(()), dma(()),
            dma((2, others)), dma((2, others)), dma((2, 3)), dma((2, 3)),
        ],
        compiler_params=pltpu.CompilerParams(
            collective_id=1, has_side_effects=True, vmem_limit_bytes=62 * 1024 * 1024
        ),
        name="front",
    )(tokens, segment, key_mask, routes, gates, cot, g1, b1, wq, wk, wv, wo, g2, b2, fin, fout, tin, tout)


def ln_backward(values, gain, upstream):
    center = jnp.mean(values, axis=-1, keepdims=True)
    shifted = values - center
    spread = jnp.mean(shifted * shifted, axis=-1, keepdims=True)
    scale = lax.rsqrt(spread + EPSILON)
    unit = shifted * scale
    inner = upstream * gain
    along = jnp.mean(inner * unit, axis=-1, keepdims=True)
    grad = scale * (inner - jnp.mean(inner, axis=-1, keepdims=True) - unit * along)
    return grad, jnp.sum(upstream * unit, axis=0, keepdims=True), jnp.sum(upstream, axis=0, keepdims=True)


class Chain:
    def __init__(self, base, count, own, stage, red_a, red_b, final, sems, hooks):
        self.base, self.count, self.own, self.stage = base, count, own, stage
        self.red_a, self.red_b, self.final, self.hooks = red_a, red_b, final, hooks
        self.red_send, self.recv_a, self.recv_b, self.bc_send, self.bc_recv = sems
        self.dp = lax.axis_index("dp")

    def place(self, half):
        return 3 - self.dp if half == 0 else self.dp

    def peers(self, half):
        down, up = (self.dp + 3) % 4, (self.dp + 1) % 4
        return (down, up) if half == 0 else (up, down)

    def red(self, half, index, near):
        toward, away = self.peers(half)
        target, sem = (self.red_b, self.recv_b) if near else (self.red_a, self.recv_a)
        return remote(
            self.stage.at[half, index], target.at[half, index], self.red_send.at[half, index], sem.at[half, index],
            {"dp": away if near else toward},
        )

    def spread(self, half, index, near):
        toward, away = self.peers(half)
        ref = self.final(half, index)
        return remote(
            ref, ref, self.bc_send.at[1 if near else 0, half, index], self.bc_recv.at[half, index],
            {"dp": toward if near else away},
        )

    def step(self, s):
        for half in (0, 1):
            place = self.place(half)
            index = s - self.base - (2 * place - 4 * (place // 3))

            @pl.when((index >= 0) & (index < self.count))
            def _():
                own = self.own(half, index)

                @pl.when(place == 0)
                def _():
                    self.stage[half, index] = own.astype(BF)
                    self.red(half, index, False).start()

                @pl.when(place == 3)
                def _():
                    self.stage[half, index] = own.astype(BF)
                    self.red(half, index, True).start()

                @pl.when(place == 1)
                def _():
                    self.red(half, index, False).wait_recv()
                    self.stage[half, index] = (own + self.red_a[half, index].astype(F32)).astype(BF)
                    self.red(half, index, False).start()

                @pl.when(place == 2)
                def _():
                    self.red(half, index, False).wait_recv()
                    self.red(half, index, True).wait_recv()
                    total = own + self.red_a[half, index].astype(F32) + self.red_b[half, index].astype(F32)
                    self.final(half, index)[...] = total.astype(BF)

        for half in (0, 1):
            place = self.place(half)
            index = s - self.base - (8 - 2 * place + 4 * (place // 3))

            @pl.when((index >= 0) & (index < self.count))
            def _():
                @pl.when(place == 2)
                def _():
                    self.spread(half, index, False).start()
                    self.spread(half, index, True).start()

                @pl.when(place != 2)
                def _():
                    self.spread(half, index, False).wait_recv()

                @pl.when(place == 1)
                def _():
                    self.spread(half, index, False).start()

                self.hooks[0](half, index)

            for later, hook in enumerate(self.hooks[1:]):
                after = index - 2 * (later + 1)
                pl.when((after >= 0) & (after < self.count))(functools.partial(hook, half, after))

    def drain(self, index):
        for half in (0, 1):
            place = self.place(half)

            @pl.when(place != 2)
            def _():
                self.red(half, index, False).wait_send()

            @pl.when((place == 1) | (place == 2))
            def _():
                self.spread(half, index, False).wait_send()

            @pl.when(place == 2)
            def _():
                self.spread(half, index, True).wait_send()


def back_kernel(
    ep_count, heads, n,
    tok_ref, seg_ref, key_ref, routes_ref, gates_ref, cot_ref, g1_ref, wq_ref, wk_ref, wv_ref, wo_ref, g2_ref,
    group_ref, qkv_ref, heads_ref, lse_ref, middle_ref, back_ref, out_ref, gx_ref, gs_ref, w_in_hbm, w_out_hbm,
    rg_hbm, pfin, small_out, grad_ref, layer_ref,
    w_in, w_out, act, slope, own, red_a, red_b, stage, fin, acc, pred_a, pred_b, pstage, pgbuf, yslot,
    ret_back, ret_out, piece, up_heads, pgrad, joined, bias, part, core_slot, mix, x_slot,
    sm, sm_tp, sm_ep, sm_dp, sm_a, sm_b,
    w_sem, red_send, recv_a, recv_b, bc_send, bc_recv, x_send, x_recv, out_sem,
    pred_send, precv_a, precv_b, pbc_send, pbc_recv, y_send, y_recv, g_send, g_recv,
    b_send, b_recv, a_send, a_recv, c_send, c_recv, m_send, m_recv, s_send, s_recv,
):
    tp, tp1, tp2, tp3 = tp_peers()
    ep, dp = lax.axis_index("ep"), lax.axis_index("dp")
    quarter, width = w_out.shape
    rows = tok_ref.shape[0]
    group_rows = qkv_ref.shape[0]
    cols = wq_ref.shape[0]
    start = pl.multiple_of(tp * quarter, quarter)
    in_copy = pltpu.make_async_copy(w_in_hbm.at[:, pl.ds(start, quarter)], w_in, w_sem.at[0])
    out_copy = pltpu.make_async_copy(w_out_hbm.at[pl.ds(start, quarter), :], w_out, w_sem.at[1])
    in_copy.start()
    out_copy.start()
    entry_barrier(ep_count, 4)

    def ep_copies(kind, source, target):
        return [
            remote(
                source.at[(ep + off) % ep_count], target.at[ep], b_send.at[kind, off - 1], b_recv.at[kind, off - 1],
                {"ep": (ep + off) % ep_count},
            )
            for off in range(1, ep_count)
        ]

    def ep_waits(kind, target):
        for off in range(1, ep_count):
            source = (ep + ep_count - off) % ep_count
            remote(
                target.at[source], target.at[source], b_send.at[kind, off - 1], b_recv.at[kind, off - 1],
                {"ep": source},
            ).wait_recv()

    sends = ep_copies(0, back_ref, ret_back) + ep_copies(1, out_ref, ret_out)
    for copy in sends:
        copy.start()
    ret_back[ep] = back_ref[ep]
    ret_out[ep] = out_ref[ep]
    in_copy.wait()
    out_copy.wait()

    tokens = gx_ref.shape[1] * gx_ref.shape[2]

    def hidden_block(index, _):
        hidden = dot_nn(gx_ref[index].reshape(tokens, width), w_in[...])
        through = dot_nt(gs_ref[index].reshape(tokens, width), w_out[...])
        value, grad = gelu_pair(hidden)
        at = pl.ds(pl.multiple_of(index * tokens, tokens), tokens)
        act[at, :] = value.astype(BF)
        slope[at, :] = (through * grad).astype(BF)
        return 0

    lax.fori_loop(0, 4, hidden_block, 0)
    span = 128

    def outer(index, _):
        at = pl.ds(pl.multiple_of(index * span, span), span)
        own[0, at, :] = dot_tn(gx_ref[:, :, :, at].reshape(-1, span), slope[...])
        own[1, at, :] = dot_tn(act[:, at], gs_ref[...].reshape(-1, width))
        return 0

    lax.fori_loop(0, width // span, outer, 0)

    def x_copy(half, index, hop):
        source, peer = ((0, tp1), (0, tp2), (2, tp1))[hop - 1]
        return remote(
            fin.at[half, index, source], fin.at[half, index, hop],
            x_send.at[hop - 1, half, index], x_recv.at[hop - 1, half, index], {"tp": peer},
        )

    def out_copy_of(half, index):
        return pltpu.make_async_copy(fin.at[half, index], rg_hbm.at[half, index], out_sem.at[half, index])

    def cross_first(half, index):
        x_copy(half, index, 2).start()
        x_copy(half, index, 1).start()

    def cross_second(half, index):
        x_copy(half, index, 2).wait_recv()
        x_copy(half, index, 3).start()

    def cross_third(half, index):
        x_copy(half, index, 1).wait_recv()
        x_copy(half, index, 3).wait_recv()
        out_copy_of(half, index).start()

    expert_chain = Chain(
        0, n, lambda half, index: own[half, pl.ds(pl.multiple_of(index * CHUNK, CHUNK), CHUNK), :],
        stage, red_a, red_b, lambda half, index: fin.at[half, index, 0],
        (red_send, recv_a, recv_b, bc_send, bc_recv), (cross_first, cross_second, cross_third),
    )

    def y_gather(half, index, off):
        chunk = 2 * index + half
        return remote(
            pfin.at[ep, chunk], pfin.at[ep, chunk], g_send.at[off - 1, half, index], g_recv.at[off - 1, half, index],
            {"ep": (ep + off) % ep_count},
        )

    def y_first(half, index):
        for off in range(1, ep_count):
            y_gather(half, index, off).start()

    proj_n = acc.shape[0] // 2
    proj_chain = Chain(
        n, proj_n, lambda half, index: acc[2 * index + half], pstage, pred_a, pred_b,
        lambda half, index: pfin.at[ep, 2 * index + half],
        (pred_send, precv_a, precv_b, pbc_send, pbc_recv), (y_first,),
    )
    clock = [0]

    def run(count, proj=False):
        def body(s, _):
            expert_chain.step(s)
            if proj:
                proj_chain.step(s)
            return 0

        lax.fori_loop(clock[0], clock[0] + count, body, 0)
        clock[0] += count
        assert proj or clock[0] <= n

    run(2)
    capacity = back_ref.shape[2]
    slots = ep_count * EXP_DEV * capacity
    pick0, pick1, marks = route_picks(routes_ref, capacity, slots)
    upstream = cot_ref[...].astype(F32)
    middle = middle_ref[...]
    ep_waits(0, ret_back)
    second = dot_nn(pick0 + pick1, ret_back[...].reshape(slots, width))
    inner_grad, gain_two, bias_two = ln_backward(middle, row_of(g2_ref), second)
    middle_grad = upstream + inner_grad
    grad_ref[...] = middle_grad
    piece[tp] = middle_grad.astype(BF)

    def gather_copy(slot, index, peer):
        return remote(piece.at[slot], piece.at[slot], a_send.at[index], a_recv.at[index], {"tp": peer})

    sends += [gather_copy(tp, 1, tp2), gather_copy(tp, 0, tp1)]
    for copy in sends[-2:]:
        copy.start()
    sm[...] = jnp.zeros_like(sm)
    sm[2:3, :] = gain_two
    sm[3:4, :] = bias_two
    sm[4:5, 0:128] = jnp.sum(marks, axis=0, keepdims=True)
    for index, ref in enumerate((wq_ref, wk_ref, wv_ref)):
        joined[index * cols : (index + 1) * cols, :] = ref[...]
    fill_bias(seg_ref, key_ref, bias)
    run(1)

    def head_rows(slot):
        at = pl.ds(pl.multiple_of(slot * rows, rows), rows)
        up_heads[at, :] = dot_nt(piece[slot], wo_ref[...]).astype(BF)

    head_rows(tp)
    gather_copy(tp1, 0, tp1).wait_recv()
    head_rows(tp1)
    gather_copy(tp2, 1, tp2).wait_recv()
    sends.append(gather_copy(tp2, 2, tp1))
    sends[-1].start()
    head_rows(tp2)
    run(1)
    gather_copy(tp3, 2, tp1).wait_recv()
    head_rows(tp3)

    def y_scatter(batch, off):
        peer = (ep + off) % ep_count
        return remote(
            pgbuf.at[batch, peer], yslot.at[batch, off - 1], y_send.at[batch, off - 1], y_recv.at[batch, off - 1],
            {"ep": peer},
        )

    def proj_start(batch, value):
        pgbuf[batch] = value.astype(BF).reshape(pgbuf.shape[1:])
        for off in range(1, ep_count):
            y_scatter(batch, off).start()

    def proj_sum(batch):
        total = pgbuf[batch, ep].astype(F32)
        for off in range(1, ep_count):
            y_scatter(batch, off).wait_recv()
            total = total + yslot[batch, off - 1].astype(F32)
        acc[3 * batch : 3 * batch + 3] = total.reshape((3,) + acc.shape[1:])

    proj_start(0, dot_tn(heads_ref[...], piece[...].reshape(group_rows, width)))
    run(1)
    scale = HD ** (-0.5)
    block = min(256, group_rows)
    for head in range(heads):
        low, high = head * HD, (head + 1) * HD
        key_sum = value_sum = None
        for index in range(group_rows // block):
            at = slice(index * block, (index + 1) * block)
            query = qkv_ref[at, low:high]
            keys = qkv_ref[:, cols + low : cols + high]
            values = qkv_ref[:, 2 * cols + low : 2 * cols + high]
            above = up_heads[at, low:high]
            scores = dot_nt(query, keys) * scale + bias[at, :]
            probs = jnp.exp(scores - lse_ref[at, head : head + 1])
            prob_grad = dot_nt(above, values)
            centered = jnp.sum(probs * prob_grad, axis=-1, keepdims=True)
            score_grad = (probs * (prob_grad - centered)).astype(BF)
            pgrad[at, low:high] = (dot_nn(score_grad, keys) * scale).astype(BF)
            key_part = dot_tn(score_grad, query)
            value_part = dot_tn(probs.astype(BF), above)
            key_sum = key_part if key_sum is None else key_sum + key_part
            value_sum = value_part if value_sum is None else value_sum + value_part
            if index + 1 == group_rows // block:
                pgrad[:, cols + low : cols + high] = (key_sum * scale).astype(BF)
                pgrad[:, 2 * cols + low : 2 * cols + high] = value_sum.astype(BF)
            run(1)

    def partial(slot):
        at = pl.ds(pl.multiple_of(slot * rows, rows), rows)
        return dot_nn(pgrad[at, :], joined[...])

    def core_copy(index):
        return remote(part.at[index], core_slot.at[index], c_send.at[index], c_recv.at[index], {"tp": tp1})

    part[0] = partial(tp3).astype(BF)
    core_copy(0).start()
    part[1] = partial(tp1).astype(BF)
    core_copy(1).start()
    crossing = partial(tp2)
    mine = partial(tp)
    core_copy(0).wait_recv()
    mix[...] = (crossing + core_slot[0].astype(F32)).astype(BF)
    cross = remote(mix, x_slot, m_send, m_recv, {"tp": tp2})
    cross.start()
    normed = group_ref[...].reshape(group_rows, width)
    for batch, part_index in ((1, 2), (2, 0), (3, 1)):
        proj_start(batch, dot_tn(pgrad[:, part_index * cols : (part_index + 1) * cols], normed))
        run(1)
    core_copy(1).wait_recv()
    cross.wait_recv()
    first = mine + core_slot[1].astype(F32) + x_slot[...].astype(F32)
    residual_part, gain_one, bias_one = ln_backward(tok_ref[...].astype(F32), row_of(g1_ref), first)
    grad_ref[...] += residual_part
    sm[0:1, :] = gain_one
    sm[1:2, :] = bias_one

    small = []

    def small_copy(slot, source, target, where):
        small.append(remote(source, target, s_send.at[slot], s_recv.at[slot], where))
        small[-1].start()

    for hop, peer in ((1, tp1), (2, tp2), (3, tp3)):
        small_copy(hop - 1, sm, sm_tp.at[hop - 1], {"tp": peer})
    run(1)
    ep_waits(1, ret_out)
    returned = ret_out[...].reshape(slots, width)
    gate0, gate1 = columns_of(gates_ref)
    mixture = gate0 * dot_nn(pick0, returned) + gate1 * dot_nn(pick1, returned)
    layer_ref[...] = (middle_ref[...] + mixture).astype(BF)
    for copy in small:
        copy.wait_recv()
    sm_a[...] = sm[...] + sm_tp[0] + sm_tp[1] + sm_tp[2]
    for off in range(1, ep_count):
        small_copy(2 + off, sm_a, sm_ep.at[off - 1], {"ep": (ep + off) % ep_count})
    for batch in range(4):
        proj_sum(batch)
    run(1)
    for copy in small[3:]:
        copy.wait_recv()
    total = sm_a[...]
    for off in range(1, ep_count):
        total = total + sm_ep[off - 1]
    sm_b[...] = total
    for off in range(1, 4):
        small_copy(1 + ep_count + off, sm_b, sm_dp.at[off - 1], {"dp": (dp + off) % 4})
    run(2)
    for copy in small[2 + ep_count :]:
        copy.wait_recv()
    small_out[...] = sm_b[...] + sm_dp[0] + sm_dp[1] + sm_dp[2]
    run(max(n + 12, n + proj_n + 8) - clock[0], proj=True)

    def y_finish(index, _):
        for half in (0, 1):
            chunk = 2 * index + half
            for off in range(1, ep_count):
                source = (ep + ep_count - off) % ep_count
                y_gather(half, index, off).wait_send()
                remote(
                    pfin.at[source, chunk], pfin.at[source, chunk],
                    g_send.at[off - 1, half, index], g_recv.at[off - 1, half, index], {"ep": source},
                ).wait_recv()
        proj_chain.drain(index)
        return 0

    lax.fori_loop(0, proj_n, y_finish, 0)
    for batch in range(4):
        for off in range(1, ep_count):
            y_scatter(batch, off).wait_send()
    for copy in sends + small + [core_copy(0), core_copy(1), cross]:
        copy.wait_send()

    def drain(index, _):
        expert_chain.drain(index)
        for half in (0, 1):
            for hop in (1, 2, 3):
                x_copy(half, index, hop).wait_send()
            out_copy_of(half, index).wait()
        return 0

    lax.fori_loop(0, n, drain, 0)


def back(tokens, segment, key_mask, routes, gates, cot, g1, wq, wk, wv, wo, g2, kept, tin, tout):
    ep_count = lax.axis_size("ep")
    assert lax.axis_size("dp") == 4 and lax.axis_size("tp") == 4
    rows, width = tokens.shape
    group_rows = segment.shape[1]
    cols = wq.shape[0]
    quarter = tin.shape[1] // 4
    assert quarter == width and 4 * cols == width
    gx = kept[-2]
    gathered = 4 * gx.shape[1] * gx.shape[2]
    n = width // CHUNK
    proj = 12
    chunk = width // (proj * ep_count)
    dma = pltpu.SemaphoreType.DMA
    vmem = pl.BlockSpec(memory_space=pltpu.VMEM)
    hbm = pl.BlockSpec(memory_space=pl.ANY)
    struct = jax.ShapeDtypeStruct
    block = kept[5].shape
    others = ep_count - 1
    small = (8, width)
    proj_half = (2, proj // 2, chunk, width)
    pg_shape = (4, ep_count, cols // ep_count, width)
    y_shape = (4, others, cols // ep_count, width)
    many = 3 + others + 3
    return pl.pallas_call(
        functools.partial(back_kernel, ep_count, cols // HD, n),
        out_shape=(
            struct((2, n, 4, CHUNK, width), BF),
            struct((ep_count, proj, chunk, width), BF),
            struct(small, F32), struct((rows, width), F32), struct((rows, width), BF),
        ),
        in_specs=[vmem] * (12 + len(kept)) + [hbm] * 2,
        out_specs=(hbm, vmem, vmem, vmem, vmem),
        scratch_shapes=[
            pltpu.VMEM((width, quarter), BF), pltpu.VMEM((quarter, width), BF),
            pltpu.VMEM((gathered, quarter), BF), pltpu.VMEM((gathered, quarter), BF),
            pltpu.VMEM((2, width, width), F32),
            pltpu.VMEM((2, n, CHUNK, width), BF), pltpu.VMEM((2, n, CHUNK, width), BF),
            pltpu.VMEM((2, n, CHUNK, width), BF), pltpu.VMEM((2, n, 4, CHUNK, width), BF),
            pltpu.VMEM((proj, chunk, width), F32),
            pltpu.VMEM(proj_half, BF), pltpu.VMEM(proj_half, BF), pltpu.VMEM(proj_half, BF),
            pltpu.VMEM(pg_shape, BF), pltpu.VMEM(y_shape, BF),
            pltpu.VMEM(block, BF), pltpu.VMEM(block, BF),
            pltpu.VMEM((4, rows, width), BF),
            pltpu.VMEM((group_rows, cols), BF), pltpu.VMEM((group_rows, 3 * cols), BF),
            pltpu.VMEM((3 * cols, width), BF), pltpu.VMEM((group_rows, group_rows), F32),
            pltpu.VMEM((2, rows, width), BF), pltpu.VMEM((2, rows, width), BF),
            pltpu.VMEM((rows, width), BF), pltpu.VMEM((rows, width), BF),
            pltpu.VMEM(small, F32), pltpu.VMEM((3,) + small, F32), pltpu.VMEM((others,) + small, F32),
            pltpu.VMEM((3,) + small, F32), pltpu.VMEM(small, F32), pltpu.VMEM(small, F32),
            dma((2,)),
            dma((2, n)), dma((2, n)), dma((2, n)), dma((2, 2, n)), dma((2, n)),
            dma((3, 2, n)), dma((3, 2, n)), dma((2, n)),
            dma((2, proj // 2)), dma((2, proj // 2)), dma((2, proj // 2)), dma((2, 2, proj // 2)), dma((2, proj // 2)),
            dma((4, others)), dma((4, others)), dma((others, 2, proj // 2)), dma((others, 2, proj // 2)),
            dma((2, others)), dma((2, others)), dma((3,)), dma((3,)), dma((2,)), dma((2,)), dma(()), dma(()),
            dma((many,)), dma((many,)),
        ],
        compiler_params=pltpu.CompilerParams(
            collective_id=0, has_side_effects=True, vmem_limit_bytes=62 * 1024 * 1024
        ),
        name="back",
    )(tokens, segment, key_mask, routes, gates, cot, g1, wq, wk, wv, wo, g2, *kept, tin, tout)


def finish_kernel(
    tp_ref, rg_ref, pfin_ref, small_ref, grad_ref, layer_ref,
    gin_ref, gout_ref, o_ref, v_ref, q_ref, k_ref, tokens_ref, result_ref, a_ref, b_ref, c_ref, d_ref, count_ref,
):
    width = gin_ref.shape[0]
    gin_ref[...] = rg_ref[0, :, 0].reshape(width, -1).astype(F32)
    gout_ref[...] = rg_ref[1, :, 0].reshape(-1, width).astype(F32)

    @pl.when(pl.program_id(0) == 0)
    def _():
        owners = pfin_ref.shape[0]
        span = q_ref.shape[0] // owners
        for index, ref in enumerate((o_ref, v_ref, q_ref, k_ref)):
            for owner in range(owners):
                value = pfin_ref[owner, 3 * index : 3 * index + 3].reshape(span, width)
                ref[owner * span : (owner + 1) * span, :] = value.astype(F32)
        tokens_ref[...] = grad_ref[...]
        result_ref[...] = layer_ref[...]
        for index, ref in enumerate((a_ref, b_ref, c_ref, d_ref)):
            ref[...] = small_ref[index : index + 1, :]
        count_ref[...] = small_ref[4:5, 0:128].astype(jnp.int32)


def finish(rg, pfin, small, grad, layer, cols):
    _, n, _, chunk, width = rg.shape
    hidden = 4 * width
    me = lax.axis_index("tp").astype(jnp.int32).reshape(1)
    struct = jax.ShapeDtypeStruct

    def where(quarter, me_ref):
        mine = me_ref[0]
        low = (quarter % 2) != (mine % 2)
        high = (quarter // 2) != (mine // 2)
        return jnp.where(low, 1, 0) + jnp.where(high, 2, 0)

    def whole(shape):
        return pl.BlockSpec(shape, lambda q, t: (0,) * len(shape))

    outs = [struct((cols, width), F32)] * 4 + [struct(grad.shape, F32), struct(layer.shape, BF)]
    outs += [struct((1, width), F32)] * 4 + [struct((1, 128), jnp.int32)]
    return pl.pallas_call(
        finish_kernel,
        grid_spec=pltpu.PrefetchScalarGridSpec(
            num_scalar_prefetch=1,
            grid=(4,),
            in_specs=[
                pl.BlockSpec((2, n, 1, chunk, width), lambda q, t: (0, 0, where(q, t), 0, 0)),
                whole(pfin.shape), whole(small.shape), whole(grad.shape), whole(layer.shape),
            ],
            out_specs=[
                pl.BlockSpec((width, width), lambda q, t: (0, q)),
                pl.BlockSpec((width, width), lambda q, t: (q, 0)),
            ] + [whole(out.shape) for out in outs],
        ),
        out_shape=[struct((width, hidden), F32), struct((hidden, width), F32)] + outs,
        name="finish",
    )(me, rg, pfin, small, grad, layer)


def local(
    tokens,
    segment,
    key_mask,
    routes,
    gates,
    ln1_gain,
    ln1_bias,
    query_weight,
    key_weight,
    value_weight,
    out_weight,
    ln2_gain,
    ln2_bias,
    frozen_in,
    frozen_out,
    train_in,
    train_out,
    cotangent,
):
    vectors = (ln1_gain, ln1_bias, ln2_gain, ln2_bias)
    flat = (query_weight.T, key_weight.T, value_weight.T, out_weight)
    cols, width = out_weight.shape
    token_args = (tokens[0], segment, key_mask, routes[0].T, gates[0].T, cotangent[0])
    kept = front(
        *token_args, *vectors[:2], *flat, *vectors[2:], frozen_in[0], frozen_out[0], train_in[0], train_out[0]
    )
    rg, pfin, small, grad, layer = back(*token_args, ln1_gain, *flat, ln2_gain, kept, train_in[0], train_out[0])
    grad_in, grad_out, out, value, query, key, grad, layer, *sums, counts = finish(
        rg, pfin, small, grad, layer, cols
    )
    gain_one, bias_one, gain_two, bias_two = (row.reshape(width) for row in sums)
    experts = EXP_DEV * lax.axis_size("ep")
    return (
        layer[None], grad[None], gain_one, bias_one, query.T, key.T, value.T, out, gain_two, bias_two,
        grad_in[None], grad_out[None], counts[0, :experts],
    )


def solution(mesh):
    in_specs = (
        P(("ep", "dp"), "tp", None),
        P(("ep", "dp"), None),
        P(("ep", "dp"), None),
        P(("ep", "dp"), "tp", None),
        P(("ep", "dp"), "tp", None),
        P(),
        P(),
        P(None, "tp"),
        P(None, "tp"),
        P(None, "tp"),
        P("tp", None),
        P(),
        P(),
        P("ep", None, None),
        P("ep", None, None),
        P("ep", None, None),
        P("ep", None, None),
        P(("ep", "dp"), "tp", None),
    )
    out_specs = (
        P(("ep", "dp"), "tp", None),
        P(("ep", "dp"), "tp", None),
        P(),
        P(),
        P(None, "tp"),
        P(None, "tp"),
        P(None, "tp"),
        P("tp", None),
        P(),
        P(),
        P("ep", None, None),
        P("ep", None, None),
        P(),
    )
    return jax.shard_map(local, mesh=mesh, in_specs=in_specs, out_specs=out_specs, check_vma=False)
```

```python
import functools
import math

import jax
import jax.numpy as jnp
from jax import lax
from jax.experimental import pallas as pl
from jax.experimental.pallas import tpu as pltpu
from jax.sharding import PartitionSpec as P

HD = 64
EXP_DEV = 2
EPSILON = 1e-05
MASKED = -1e30
MESH = pl.DeviceIdType.MESH
BF = jnp.bfloat16
F32 = jnp.float32
CHUNK = 32


def tp_peers():
    me = lax.axis_index("tp")
    one = me + 1 - 2 * (me % 2)
    return (me, one, (me + 2) % 4, (one + 2) % 4)


def remote(src, dst, send, recv, where):
    return pltpu.make_async_remote_copy(
        src_ref=src, dst_ref=dst, send_sem=send, recv_sem=recv,
        device_id=where, device_id_type=MESH,
    )


def entry_barrier(ep_count, dp_count):
    barrier = pltpu.get_barrier_semaphore()
    _, tp1, tp2, tp3 = tp_peers()
    ep, dp = lax.axis_index("ep"), lax.axis_index("dp")
    for peer in (tp1, tp2, tp3):
        pl.semaphore_signal(barrier, inc=1, device_id={"tp": peer}, device_id_type=MESH)
    for off in range(1, ep_count):
        pl.semaphore_signal(
            barrier, inc=1, device_id={"ep": (ep + off) % ep_count}, device_id_type=MESH
        )
    for off in range(1, dp_count):
        pl.semaphore_signal(
            barrier, inc=1, device_id={"dp": (dp + off) % dp_count}, device_id_type=MESH
        )
    pl.semaphore_wait(barrier, 3 + ep_count - 1 + dp_count - 1)


def gelu_pair(hidden):
    phi = 0.5 * (1.0 + lax.erf(hidden * math.sqrt(0.5)))
    dens = jnp.exp(-0.5 * hidden * hidden) * (1.0 / math.sqrt(2.0 * math.pi))
    return hidden * phi, phi + hidden * dens


def row_of(ref):
    return ref[...].reshape(1, -1)


def columns_of(ref):
    value = ref[...].astype(F32)
    padded = jnp.concatenate([value, jnp.zeros((6, value.shape[1]), F32)], axis=0)
    flipped = padded.T
    return flipped[:, 0:1], flipped[:, 1:2]


def fill_bias(seg_ref, key_ref, bias):
    segment = seg_ref[...]
    group_rows = segment.shape[1]
    lane = lax.broadcasted_iota(jnp.int32, segment.shape, 1)
    starts = (segment != pltpu.roll(segment, 1, 1)) | (lane == 0)
    keep = (key_ref[...] == 1) | starts
    segment = segment.astype(F32)
    column = jnp.broadcast_to(segment, (8, group_rows)).T[:, 0:1]
    kept = jnp.where(keep, segment, -1.0)
    bias[...] = jnp.where(column == kept, 0.0, MASKED)


def ln_rows(values, gain, bias):
    center = jnp.mean(values, axis=-1, keepdims=True)
    shifted = values - center
    spread = jnp.mean(shifted * shifted, axis=-1, keepdims=True)
    return shifted * lax.rsqrt(spread + EPSILON) * gain + bias


def route_picks(routes_ref, capacity, slots):
    first, second = (column.astype(jnp.int32) for column in columns_of(routes_ref))
    rows = first.shape[0]
    lane = lax.broadcasted_iota(jnp.int32, (rows, 128), 1)
    marks = jnp.where((lane == first) | (lane == second), 1.0, 0.0)
    row_id = lax.broadcasted_iota(jnp.int32, (rows, rows), 0)
    col_id = lax.broadcasted_iota(jnp.int32, (rows, rows), 1)
    lower = jnp.where(row_id > col_id, 1.0, 0.0).astype(BF)
    before = jnp.dot(lower, marks.astype(BF), preferred_element_type=F32)
    slot = lax.broadcasted_iota(jnp.int32, (rows, slots), 1)
    picks = []
    for route in (first, second):
        place = jnp.sum(jnp.where(lane == route, before, 0.0), axis=1, keepdims=True)
        chosen = route * capacity + place.astype(jnp.int32)
        picks.append(jnp.where(slot == chosen, 1.0, 0.0).astype(BF))
    return picks[0], picks[1], marks


def dot_tn(left, right):
    return lax.dot_general(left, right, (((0,), (0,)), ((), ())), preferred_element_type=F32)


def dot_nt(left, right):
    return lax.dot_general(left, right, (((1,), (1,)), ((), ())), preferred_element_type=F32)


def dot_nn(left, right):
    return jnp.dot(left, right, preferred_element_type=F32)


def ln_backward(values, gain, upstream):
    center = jnp.mean(values, axis=-1, keepdims=True)
    shifted = values - center
    spread = jnp.mean(shifted * shifted, axis=-1, keepdims=True)
    scale = lax.rsqrt(spread + EPSILON)
    unit = shifted * scale
    inner = upstream * gain
    along = jnp.mean(inner * unit, axis=-1, keepdims=True)
    grad = scale * (inner - jnp.mean(inner, axis=-1, keepdims=True) - unit * along)
    return grad, jnp.sum(upstream * unit, axis=0, keepdims=True), jnp.sum(upstream, axis=0, keepdims=True)


class Chain:
    def __init__(self, base, count, own, stage, final, sems, hooks):
        self.base, self.count, self.own, self.stage = base, count, own, stage
        self.final, self.hooks = final, hooks
        self.red_send, self.recv_a, self.recv_b, self.bc_send, self.bc_recv = sems
        self.dp = lax.axis_index("dp")

    def place(self, half):
        return 3 - self.dp if half == 0 else self.dp

    def peers(self, half):
        down, up = (self.dp + 3) % 4, (self.dp + 1) % 4
        return (down, up) if half == 0 else (up, down)

    def red(self, half, index, near):
        toward, away = self.peers(half)
        landing = self.stage.at[half, index]
        target, sem = (self.final(half, index), self.recv_b) if near else (landing, self.recv_a)
        return remote(
            landing, target, self.red_send.at[half, index], sem.at[half, index],
            {"dp": away if near else toward},
        )

    def spread(self, half, index, near):
        toward, away = self.peers(half)
        ref = self.final(half, index)
        return remote(
            ref, ref, self.bc_send.at[1 if near else 0, half, index], self.bc_recv.at[half, index],
            {"dp": toward if near else away},
        )

    def step(self, s):
        for half in (0, 1):
            place = self.place(half)
            index = s - self.base - (2 * place - 4 * (place // 3))

            @pl.when((index >= 0) & (index < self.count))
            def _():
                own = self.own(half, index)

                @pl.when(place == 0)
                def _():
                    self.stage[half, index] = own.astype(BF)
                    self.red(half, index, False).start()

                @pl.when(place == 3)
                def _():
                    self.stage[half, index] = own.astype(BF)
                    self.red(half, index, True).start()

                @pl.when(place == 1)
                def _():
                    self.red(half, index, False).wait_recv()
                    self.stage[half, index] = (own + self.stage[half, index].astype(F32)).astype(BF)
                    self.red(half, index, False).start()

                @pl.when(place == 2)
                def _():
                    self.red(half, index, False).wait_recv()
                    self.red(half, index, True).wait_recv()
                    total = own + self.stage[half, index].astype(F32) + self.final(half, index)[...].astype(F32)
                    self.final(half, index)[...] = total.astype(BF)

        for half in (0, 1):
            place = self.place(half)
            index = s - self.base - (8 - 2 * place + 4 * (place // 3))

            @pl.when((index >= 0) & (index < self.count))
            def _():
                @pl.when(place == 2)
                def _():
                    self.spread(half, index, False).start()
                    self.spread(half, index, True).start()

                @pl.when(place != 2)
                def _():
                    self.spread(half, index, False).wait_recv()

                @pl.when(place == 1)
                def _():
                    self.spread(half, index, False).start()

                self.hooks[0](half, index)

            for later, hook in enumerate(self.hooks[1:]):
                after = index - 2 * (later + 1)
                pl.when((after >= 0) & (after < self.count))(functools.partial(hook, half, after))

    def drain(self, index):
        for half in (0, 1):
            place = self.place(half)

            @pl.when(place != 2)
            def _():
                self.red(half, index, False).wait_send()

            @pl.when((place == 1) | (place == 2))
            def _():
                self.spread(half, index, False).wait_send()

            @pl.when(place == 2)
            def _():
                self.spread(half, index, True).wait_send()


def layer_kernel(
    ep_count, heads, n,
    tok_ref, seg_ref, key_ref, routes_ref, gates_ref, cot_ref, g1_ref, b1_ref, wq_ref, wk_ref, wv_ref, wo_ref,
    g2_ref, b2_ref, fin_hbm, fout_hbm, tin_hbm, tout_hbm,
    rg_hbm, pfin, small_out, grad_ref, layer_ref,
    weights, group_ref, qkv_ref, heads_ref, lse_ref, middle_ref, gx, gs, picks, joined, bias,
    part, core_slot, mix, x_slot, sx, ss, ax, as_, out_acc, back_acc, out_ref, back_ref,
    act, slope, own, stage, fin, acc, pstage, pgbuf, yslot, ret_back, ret_out,
    piece, up_heads, pgrad, bpart, bcore_slot, bmix, bx_slot,
    sm, sm_tp, sm_ep, sm_dp, sm_a, sm_b,
    w_sem, a_send, a_recv, c_send, c_recv, m_send, m_recv, e_send, e_recv, t_send, t_recv,
    red_send, recv_a, recv_b, bc_send, bc_recv, x_send, x_recv, out_sem,
    pred_send, precv_a, precv_b, pbc_send, pbc_recv, y_send, y_recv, g_send, g_recv,
    b_send, b_recv, s_send, s_recv,
):
    tp, tp1, tp2, tp3 = tp_peers()
    ep, dp = lax.axis_index("ep"), lax.axis_index("dp")
    rows, width = tok_ref.shape
    cols = wq_ref.shape[0]
    group_rows = seg_ref.shape[1]
    pieces = weights.shape[0]
    capacity = sx.shape[2]
    slots = ep_count * EXP_DEV * capacity
    tokens = ep_count * capacity
    frozen, train = 0, 1
    offsets = range(1, ep_count)

    def weight_loads(expert, index):
        source_in, source_out = ((fin_hbm, fout_hbm), (tin_hbm, tout_hbm))[expert]
        at = pl.ds(pl.multiple_of(index * width, width), width)
        return [
            pltpu.make_async_copy(source_in.at[:, at], weights.at[index, 0], w_sem.at[expert, 0, index]),
            pltpu.make_async_copy(source_out.at[at, :], weights.at[index, 1], w_sem.at[expert, 1, index]),
        ]

    residual = tok_ref[...].astype(F32)
    group_ref[tp] = ln_rows(residual, row_of(g1_ref), row_of(b1_ref)).astype(BF)
    entry_barrier(ep_count, 4)
    sends = []

    def send(copy):
        sends.append(copy)
        copy.start()

    def gather_copy(stage_of, buf, slot, index, peer):
        return remote(
            buf.at[slot], buf.at[slot], a_send.at[stage_of, index], a_recv.at[stage_of, index], {"tp": peer}
        )

    send(gather_copy(0, group_ref, tp, 1, tp2))
    send(gather_copy(0, group_ref, tp, 0, tp1))
    for index in range(pieces):
        for copy in weight_loads(train, index):
            copy.start()

    pick0, pick1, marks = route_picks(routes_ref, capacity, slots)
    picks[0] = pick0
    picks[1] = pick1
    sm[...] = jnp.zeros_like(sm)
    sm[4:5, 0:128] = jnp.sum(marks, axis=0, keepdims=True)
    upstream = cot_ref[...].astype(F32)
    gate0, gate1 = columns_of(gates_ref)
    share0 = (gate0 * upstream).astype(BF)
    share1 = (gate1 * upstream).astype(BF)
    ss[...] = (dot_tn(pick0, share0) + dot_tn(pick1, share1)).astype(BF).reshape(ss.shape)

    def landing(kind, expert, source):
        if expert == train:
            return (gx, gs)[kind].at[0, source]
        return (ax, as_)[kind].at[source]

    def owner_copy(kind, expert, off):
        peer = (ep + off) % ep_count
        return remote(
            (sx, ss)[kind].at[peer, expert], landing(kind, expert, ep),
            e_send.at[kind, expert, off - 1], e_recv.at[kind, expert, off - 1], {"ep": peer},
        )

    def owner_wait(kind, expert, off):
        source = (ep + ep_count - off) % ep_count
        target = landing(kind, expert, source)
        remote(
            target, target, e_send.at[kind, expert, off - 1], e_recv.at[kind, expert, off - 1], {"ep": source}
        ).wait_recv()

    def token_copy(kind, rel, hop):
        buf = (gx, gs)[kind]
        origin = (ep + ep_count - rel) % ep_count
        source, peer = ((0, tp1), (0, tp2), (2, tp1))[hop - 1]
        return remote(
            buf.at[source, origin], buf.at[hop, origin],
            t_send.at[kind, rel, hop - 1], t_recv.at[kind, rel, hop - 1], {"tp": peer},
        )

    def dispatch(kind, source):
        for off in offsets:
            send(owner_copy(kind, train, off))
        (gx, gs)[kind][0, ep] = source[ep, train]
        send(token_copy(kind, 0, 2))
        send(token_copy(kind, 0, 1))
        for off in offsets:
            send(owner_copy(kind, frozen, off))
        (ax, as_)[kind][ep] = source[ep, frozen]

    def pass_on(kind):
        for off in offsets:
            owner_wait(kind, train, off)
            send(token_copy(kind, off, 2))
            send(token_copy(kind, off, 1))

    def forward(kind, rel):
        token_copy(kind, rel, 2).wait_recv()
        send(token_copy(kind, rel, 3))

    dispatch(1, ss)
    for index, ref in enumerate((wq_ref, wk_ref, wv_ref)):
        joined[index * cols : (index + 1) * cols, :] = ref[...]
    fill_bias(seg_ref, key_ref, bias)

    def project(slot):
        at = pl.ds(pl.multiple_of(slot * rows, rows), rows)
        qkv_ref[at, :] = dot_nt(group_ref[slot], joined[...]).astype(BF)

    project(tp)
    gather_copy(0, group_ref, tp1, 0, tp1).wait_recv()
    project(tp1)
    gather_copy(0, group_ref, tp2, 1, tp2).wait_recv()
    send(gather_copy(0, group_ref, tp2, 2, tp1))
    project(tp2)
    pass_on(1)
    gather_copy(0, group_ref, tp3, 2, tp1).wait_recv()
    project(tp3)

    scale = HD ** (-0.5)
    block = min(256, group_rows)
    for head in range(heads):
        low, high = head * HD, (head + 1) * HD
        for index in range(group_rows // block):
            at = slice(index * block, (index + 1) * block)
            query = qkv_ref[at, low:high]
            keys = qkv_ref[:, cols + low : cols + high]
            values = qkv_ref[:, 2 * cols + low : 2 * cols + high]
            scores = dot_nt(query, keys) * scale + bias[at, :]
            highest = jnp.max(scores, axis=-1, keepdims=True)
            weight = jnp.exp(scores - highest)
            total = jnp.sum(weight, axis=-1, keepdims=True)
            probs = (weight * (1.0 / total)).astype(BF)
            heads_ref[at, low:high] = dot_nn(probs, values).astype(BF)
            lse_ref[at, head : head + 1] = highest + jnp.log(total)

    def partial(slot):
        at = pl.ds(pl.multiple_of(slot * rows, rows), rows)
        return dot_nn(heads_ref[at, :], wo_ref[...])

    def core_copy(index):
        return remote(part.at[index], core_slot.at[index], c_send.at[0, index], c_recv.at[0, index], {"tp": tp1})

    part[0] = partial(tp3)
    send(core_copy(0))
    part[1] = partial(tp1)
    send(core_copy(1))
    crossing = partial(tp2)
    mine = tok_ref[...].astype(F32) + partial(tp)
    core_copy(0).wait_recv()
    mix[...] = (crossing + core_slot[0]).astype(BF)
    cross = remote(mix, x_slot, m_send.at[0], m_recv.at[0], {"tp": tp2})
    send(cross)
    forward(1, 0)
    core_copy(1).wait_recv()
    mine = mine + core_slot[1]
    cross.wait_recv()
    middle = mine + x_slot[...].astype(F32)
    middle_ref[...] = middle
    normed = ln_rows(middle, row_of(g2_ref), row_of(b2_ref)).astype(BF)
    sx[...] = dot_tn(picks[0] + picks[1], normed).astype(BF).reshape(sx.shape)
    dispatch(0, sx)
    for off in offsets:
        forward(1, off)
    pass_on(0)

    def expert_piece(index, inputs, shares):
        before = dot_nn(inputs, weights[index, 0])
        through = dot_nt(shares, weights[index, 1])
        value, grad = gelu_pair(before)
        slopes = (through * grad).astype(BF)
        produced = dot_nn(value.astype(BF), weights[index, 1])
        returned = dot_nt(slopes, weights[index, 0])

        @pl.when(index == 0)
        def _():
            out_acc[...] = produced
            back_acc[...] = returned

        @pl.when(index > 0)
        def _():
            out_acc[...] += produced
            back_acc[...] += returned

    def return_copy(kind, expert, off):
        peer = (ep + off) % ep_count
        source, target = ((back_ref, ret_back), (out_ref, ret_out))[kind]
        return remote(
            source.at[peer, expert], target.at[ep, expert],
            b_send.at[kind, expert, off - 1], b_recv.at[kind, expert, off - 1], {"ep": peer},
        )

    def return_wait(kind):
        target = (ret_back, ret_out)[kind]
        for expert in range(EXP_DEV):
            for off in offsets:
                source = (ep + ep_count - off) % ep_count
                remote(
                    target.at[source, expert], target.at[source, expert],
                    b_send.at[kind, expert, off - 1], b_recv.at[kind, expert, off - 1], {"ep": source},
                ).wait_recv()

    def give_back(expert):
        back_ref[:, expert] = back_acc[...].astype(BF).reshape(ep_count, capacity, width)
        out_ref[:, expert] = out_acc[...].astype(BF).reshape(ep_count, capacity, width)
        for kind in (0, 1):
            for off in offsets:
                send(return_copy(kind, expert, off))
        ret_back[ep, expert] = back_ref[ep, expert]
        ret_out[ep, expert] = out_ref[ep, expert]

    def train_piece(index, _):
        for copy in weight_loads(train, index):
            copy.wait()
        expert_piece(index, gx[0].reshape(tokens, width), gs[0].reshape(tokens, width))

        @pl.when(index == 1)
        def _():
            token_copy(0, 0, 2).wait_recv()
            token_copy(0, 0, 3).start()

        return 0

    lax.fori_loop(0, pieces, train_piece, 0)
    sends.append(token_copy(0, 0, 3))
    give_back(train)
    for off in offsets:
        forward(0, off)

    def hidden_block(index, _):
        for hop, when in ((1, 1), (3, 3)):
            @pl.when(index == when)
            def _(hop=hop):
                for kind in (0, 1):
                    for rel in range(ep_count):
                        token_copy(kind, rel, hop).wait_recv()

        before = dot_nn(gx[index].reshape(tokens, width), weights[tp, 0])
        through = dot_nt(gs[index].reshape(tokens, width), weights[tp, 1])
        value, grad = gelu_pair(before)
        at = pl.ds(pl.multiple_of(index * tokens, tokens), tokens)
        act[at, :] = value.astype(BF)
        slope[at, :] = (through * grad).astype(BF)
        return 0

    lax.fori_loop(0, 4, hidden_block, 0)
    for index in range(pieces):
        for copy in weight_loads(frozen, index):
            copy.start()

    def x_copy(half, index, hop):
        source, peer = ((0, tp1), (0, tp2), (2, tp1))[hop - 1]
        return remote(
            fin.at[half, index, source], fin.at[half, index, hop],
            x_send.at[hop - 1, half, index], x_recv.at[hop - 1, half, index], {"tp": peer},
        )

    def out_copy_of(half, index):
        return pltpu.make_async_copy(fin.at[half, index], rg_hbm.at[half, index], out_sem.at[half, index])

    def cross_first(half, index):
        x_copy(half, index, 2).start()
        x_copy(half, index, 1).start()

    def cross_second(half, index):
        x_copy(half, index, 2).wait_recv()
        x_copy(half, index, 3).start()

    def cross_third(half, index):
        x_copy(half, index, 1).wait_recv()
        x_copy(half, index, 3).wait_recv()
        out_copy_of(half, index).start()

    expert_chain = Chain(
        0, n, lambda half, index: own[half, pl.ds(pl.multiple_of(index * CHUNK, CHUNK), CHUNK), :],
        stage, lambda half, index: fin.at[half, index, 0],
        (red_send, recv_a, recv_b, bc_send, bc_recv), (cross_first, cross_second, cross_third),
    )
    span = 128

    def outer(index, _):
        at = pl.ds(pl.multiple_of(index * span, span), span)
        own[0, at, :] = dot_tn(gx[:, :, :, at].reshape(-1, span), slope[...])
        own[1, at, :] = dot_tn(act[:, at], gs[...].reshape(-1, width))
        expert_chain.step(index)
        return 0

    first_steps = width // span
    lax.fori_loop(0, first_steps, outer, 0)

    def frozen_piece(index, _):
        for copy in weight_loads(frozen, index):
            copy.wait()
        expert_piece(index, ax[...].reshape(tokens, width), as_[...].reshape(tokens, width))
        expert_chain.step(first_steps + index)
        return 0

    for kind in (0, 1):
        for off in offsets:
            owner_wait(kind, frozen, off)
    lax.fori_loop(0, pieces, frozen_piece, 0)
    give_back(frozen)
    clock = [first_steps + pieces]
    proj_chain = None

    def run(count):
        def body(s, _):
            expert_chain.step(s)
            if proj_chain is not None:
                proj_chain.step(s)
            return 0

        lax.fori_loop(clock[0], clock[0] + count, body, 0)
        clock[0] += count

    run(2)
    return_wait(0)
    second = dot_nn(picks[0] + picks[1], ret_back[...].reshape(slots, width))
    inner_grad, gain_two, bias_two = ln_backward(middle_ref[...], row_of(g2_ref), second)
    middle_grad = cot_ref[...].astype(F32) + inner_grad
    grad_ref[...] = middle_grad
    piece[tp] = middle_grad.astype(BF)
    send(gather_copy(1, piece, tp, 1, tp2))
    send(gather_copy(1, piece, tp, 0, tp1))
    sm[2:3, :] = gain_two
    sm[3:4, :] = bias_two
    run(1)

    def head_rows(slot):
        at = pl.ds(pl.multiple_of(slot * rows, rows), rows)
        up_heads[at, :] = dot_nt(piece[slot], wo_ref[...]).astype(BF)

    head_rows(tp)
    gather_copy(1, piece, tp1, 0, tp1).wait_recv()
    head_rows(tp1)
    gather_copy(1, piece, tp2, 1, tp2).wait_recv()
    send(gather_copy(1, piece, tp2, 2, tp1))
    head_rows(tp2)
    run(1)
    gather_copy(1, piece, tp3, 2, tp1).wait_recv()
    head_rows(tp3)

    def y_scatter(batch, off):
        peer = (ep + off) % ep_count
        return remote(
            pgbuf.at[batch, peer], yslot.at[batch, off - 1], y_send.at[batch, off - 1], y_recv.at[batch, off - 1],
            {"ep": peer},
        )

    def proj_start(batch, value):
        pgbuf[batch] = value.astype(BF).reshape(pgbuf.shape[1:])
        for off in offsets:
            send(y_scatter(batch, off))

    def proj_sum(batch):
        total = pgbuf[batch, ep].astype(F32)
        for off in offsets:
            y_scatter(batch, off).wait_recv()
            total = total + yslot[batch, off - 1].astype(F32)
        acc[3 * batch : 3 * batch + 3] = total.reshape((3,) + acc.shape[1:])

    proj_start(0, dot_tn(heads_ref[...], piece[...].reshape(group_rows, width)))
    run(1)
    for head in range(heads):
        low, high = head * HD, (head + 1) * HD
        key_sum = value_sum = None
        for index in range(group_rows // block):
            at = slice(index * block, (index + 1) * block)
            query = qkv_ref[at, low:high]
            keys = qkv_ref[:, cols + low : cols + high]
            values = qkv_ref[:, 2 * cols + low : 2 * cols + high]
            above = up_heads[at, low:high]
            scores = dot_nt(query, keys) * scale + bias[at, :]
            probs = jnp.exp(scores - lse_ref[at, head : head + 1])
            prob_grad = dot_nt(above, values)
            centered = jnp.sum(probs * prob_grad, axis=-1, keepdims=True)
            score_grad = (probs * (prob_grad - centered)).astype(BF)
            pgrad[at, low:high] = (dot_nn(score_grad, keys) * scale).astype(BF)
            key_part = dot_tn(score_grad, query)
            value_part = dot_tn(probs.astype(BF), above)
            key_sum = key_part if key_sum is None else key_sum + key_part
            value_sum = value_part if value_sum is None else value_sum + value_part
        pgrad[:, cols + low : cols + high] = (key_sum * scale).astype(BF)
        pgrad[:, 2 * cols + low : 2 * cols + high] = value_sum.astype(BF)
        run(1)

    def back_partial(slot):
        at = pl.ds(pl.multiple_of(slot * rows, rows), rows)
        return dot_nn(pgrad[at, :], joined[...])

    def back_core_copy(index):
        return remote(bpart.at[index], bcore_slot.at[index], c_send.at[1, index], c_recv.at[1, index], {"tp": tp1})

    bpart[0] = back_partial(tp3).astype(BF)
    send(back_core_copy(0))
    bpart[1] = back_partial(tp1).astype(BF)
    send(back_core_copy(1))
    crossing = back_partial(tp2)
    mine = back_partial(tp)
    back_core_copy(0).wait_recv()
    bmix[...] = (crossing + bcore_slot[0].astype(F32)).astype(BF)
    back_cross = remote(bmix, bx_slot, m_send.at[1], m_recv.at[1], {"tp": tp2})
    send(back_cross)
    normed = group_ref[...].reshape(group_rows, width)
    for batch, part_index in ((1, 2), (2, 0), (3, 1)):
        proj_start(batch, dot_tn(pgrad[:, part_index * cols : (part_index + 1) * cols], normed))
        run(1)
    back_core_copy(1).wait_recv()
    back_cross.wait_recv()
    first = mine + bcore_slot[1].astype(F32) + bx_slot[...].astype(F32)
    residual_part, gain_one, bias_one = ln_backward(tok_ref[...].astype(F32), row_of(g1_ref), first)
    grad_ref[...] += residual_part
    sm[0:1, :] = gain_one
    sm[1:2, :] = bias_one

    small = []

    def small_copy(slot, source, target, where):
        small.append(remote(source, target, s_send.at[slot], s_recv.at[slot], where))
        send(small[-1])

    for hop, peer in ((1, tp1), (2, tp2), (3, tp3)):
        small_copy(hop - 1, sm, sm_tp.at[hop - 1], {"tp": peer})
    for batch in range(4):
        proj_sum(batch)

    def y_gather(half, index, off):
        chunk = 2 * index + half
        return remote(
            pfin.at[ep, chunk], pfin.at[ep, chunk], g_send.at[off - 1, half, index], g_recv.at[off - 1, half, index],
            {"ep": (ep + off) % ep_count},
        )

    def y_first(half, index):
        for off in offsets:
            y_gather(half, index, off).start()

    proj_n = acc.shape[0] // 2
    proj_base = max(n, clock[0])
    proj_chain = Chain(
        proj_base, proj_n, lambda half, index: acc[2 * index + half], pstage,
        lambda half, index: pfin.at[ep, 2 * index + half],
        (pred_send, precv_a, precv_b, pbc_send, pbc_recv), (y_first,),
    )
    run(1)
    return_wait(1)
    returned = ret_out[...].reshape(slots, width)
    gate0, gate1 = columns_of(gates_ref)
    mixture = gate0 * dot_nn(picks[0], returned) + gate1 * dot_nn(picks[1], returned)
    layer_ref[...] = (middle_ref[...] + mixture).astype(BF)
    for copy in small:
        copy.wait_recv()
    sm_a[...] = sm[...] + sm_tp[0] + sm_tp[1] + sm_tp[2]
    for off in offsets:
        small_copy(2 + off, sm_a, sm_ep.at[off - 1], {"ep": (ep + off) % ep_count})
    run(2)
    for copy in small[3:]:
        copy.wait_recv()
    total = sm_a[...]
    for off in offsets:
        total = total + sm_ep[off - 1]
    sm_b[...] = total
    for off in range(1, 4):
        small_copy(1 + ep_count + off, sm_b, sm_dp.at[off - 1], {"dp": (dp + off) % 4})
    run(2)
    for copy in small[2 + ep_count :]:
        copy.wait_recv()
    small_out[...] = sm_b[...] + sm_dp[0] + sm_dp[1] + sm_dp[2]
    run(max(n + 12, proj_base + proj_n + 8) - clock[0])

    def y_finish(index, _):
        for half in (0, 1):
            chunk = 2 * index + half
            for off in offsets:
                source = (ep + ep_count - off) % ep_count
                y_gather(half, index, off).wait_send()
                remote(
                    pfin.at[source, chunk], pfin.at[source, chunk],
                    g_send.at[off - 1, half, index], g_recv.at[off - 1, half, index], {"ep": source},
                ).wait_recv()
        proj_chain.drain(index)
        return 0

    lax.fori_loop(0, proj_n, y_finish, 0)
    for copy in sends:
        copy.wait_send()

    def drain(index, _):
        expert_chain.drain(index)
        for half in (0, 1):
            for hop in (1, 2, 3):
                x_copy(half, index, hop).wait_send()
            out_copy_of(half, index).wait()
        return 0

    lax.fori_loop(0, n, drain, 0)


def layer_step(tokens, segment, key_mask, routes, gates, cot, g1, b1, wq, wk, wv, wo, g2, b2, fin, fout, tin, tout):
    ep_count = lax.axis_size("ep")
    assert lax.axis_size("dp") == 4 and lax.axis_size("tp") == 4
    rows, width = tokens.shape
    group_rows = segment.shape[1]
    cols = wq.shape[0]
    hidden = tin.shape[1]
    quarter = hidden // 4
    assert quarter == width and 4 * cols == width
    capacity = 4 * rows // (EXP_DEV * ep_count)
    gathered = 4 * ep_count * capacity
    n = width // CHUNK
    proj = 12
    chunk = width // (proj * ep_count)
    dma = pltpu.SemaphoreType.DMA
    vmem = pl.BlockSpec(memory_space=pltpu.VMEM)
    hbm = pl.BlockSpec(memory_space=pl.ANY)
    struct = jax.ShapeDtypeStruct
    block = (ep_count, EXP_DEV, capacity, width)
    single = (ep_count, capacity, width)
    others = ep_count - 1
    small = (8, width)
    pg_shape = (4, ep_count, cols // ep_count, width)
    y_shape = (4, others, cols // ep_count, width)
    many = 3 + others + 3
    return pl.pallas_call(
        functools.partial(layer_kernel, ep_count, cols // HD, n),
        out_shape=(
            struct((2, n, 4, CHUNK, width), BF),
            struct((ep_count, proj, chunk, width), BF),
            struct(small, F32), struct((rows, width), F32), struct((rows, width), BF),
        ),
        in_specs=[vmem] * 14 + [hbm] * 4,
        out_specs=(hbm, vmem, vmem, vmem, vmem),
        scratch_shapes=[
            pltpu.VMEM((hidden // width, 2, width, width), BF),
            pltpu.VMEM((4, rows, width), BF), pltpu.VMEM((group_rows, 3 * cols), BF),
            pltpu.VMEM((group_rows, cols), BF), pltpu.VMEM((group_rows, 8), F32), pltpu.VMEM((rows, width), F32),
            pltpu.VMEM((4,) + single, BF), pltpu.VMEM((4,) + single, BF),
            pltpu.VMEM((2, rows, ep_count * EXP_DEV * capacity), BF),
            pltpu.VMEM((3 * cols, width), BF), pltpu.VMEM((group_rows, group_rows), F32),
            pltpu.VMEM((2, rows, width), F32), pltpu.VMEM((2, rows, width), F32),
            pltpu.VMEM((rows, width), BF), pltpu.VMEM((rows, width), BF),
            pltpu.VMEM(block, BF), pltpu.VMEM(block, BF), pltpu.VMEM(single, BF), pltpu.VMEM(single, BF),
            pltpu.VMEM((ep_count * capacity, width), F32), pltpu.VMEM((ep_count * capacity, width), F32),
            pltpu.VMEM(block, BF), pltpu.VMEM(block, BF),
            pltpu.VMEM((gathered, quarter), BF), pltpu.VMEM((gathered, quarter), BF),
            pltpu.VMEM((2, width, width), F32),
            pltpu.VMEM((2, n, CHUNK, width), BF), pltpu.VMEM((2, n, 4, CHUNK, width), BF),
            pltpu.VMEM((proj, chunk, width), F32), pltpu.VMEM((2, proj // 2, chunk, width), BF),
            pltpu.VMEM(pg_shape, BF), pltpu.VMEM(y_shape, BF),
            pltpu.VMEM(block, BF), pltpu.VMEM(block, BF),
            pltpu.VMEM((4, rows, width), BF),
            pltpu.VMEM((group_rows, cols), BF), pltpu.VMEM((group_rows, 3 * cols), BF),
            pltpu.VMEM((2, rows, width), BF), pltpu.VMEM((2, rows, width), BF),
            pltpu.VMEM((rows, width), BF), pltpu.VMEM((rows, width), BF),
            pltpu.VMEM(small, F32), pltpu.VMEM((3,) + small, F32), pltpu.VMEM((others,) + small, F32),
            pltpu.VMEM((3,) + small, F32), pltpu.VMEM(small, F32), pltpu.VMEM(small, F32),
            dma((2, 2, hidden // width)), dma((2, 3)), dma((2, 3)), dma((2, 2)), dma((2, 2)), dma((2,)), dma((2,)),
            dma((2, 2, others)), dma((2, 2, others)), dma((2, ep_count, 3)), dma((2, ep_count, 3)),
            dma((2, n)), dma((2, n)), dma((2, n)), dma((2, 2, n)), dma((2, n)),
            dma((3, 2, n)), dma((3, 2, n)), dma((2, n)),
            dma((2, proj // 2)), dma((2, proj // 2)), dma((2, proj // 2)), dma((2, 2, proj // 2)), dma((2, proj // 2)),
            dma((4, others)), dma((4, others)), dma((others, 2, proj // 2)), dma((others, 2, proj // 2)),
            dma((2, 2, others)), dma((2, 2, others)), dma((many,)), dma((many,)),
        ],
        compiler_params=pltpu.CompilerParams(
            collective_id=0, has_side_effects=True, vmem_limit_bytes=62 * 1024 * 1024
        ),
        name="layer",
    )(tokens, segment, key_mask, routes, gates, cot, g1, b1, wq, wk, wv, wo, g2, b2, fin, fout, tin, tout)


def finish_kernel(
    tp_ref, rg_ref, pfin_ref, small_ref, grad_ref, layer_ref,
    gin_ref, gout_ref, o_ref, v_ref, q_ref, k_ref, tokens_ref, result_ref, a_ref, b_ref, c_ref, d_ref, count_ref,
):
    width = gin_ref.shape[0]
    gin_ref[...] = rg_ref[0, :, 0].reshape(width, -1).astype(F32)
    gout_ref[...] = rg_ref[1, :, 0].reshape(-1, width).astype(F32)

    @pl.when(pl.program_id(0) == 0)
    def _():
        owners = pfin_ref.shape[0]
        span = q_ref.shape[0] // owners
        for index, ref in enumerate((o_ref, v_ref, q_ref, k_ref)):
            for owner in range(owners):
                value = pfin_ref[owner, 3 * index : 3 * index + 3].reshape(span, width)
                ref[owner * span : (owner + 1) * span, :] = value.astype(F32)
        tokens_ref[...] = grad_ref[...]
        result_ref[...] = layer_ref[...]
        for index, ref in enumerate((a_ref, b_ref, c_ref, d_ref)):
            ref[...] = small_ref[index : index + 1, :].reshape(width)
        count_ref[...] = small_ref[4:5, 0:128].astype(jnp.int32).reshape(128)[: count_ref.shape[0]]


def finish(rg, pfin, small, grad, layer, cols, experts):
    _, n, _, chunk, width = rg.shape
    hidden = 4 * width
    me = lax.axis_index("tp").astype(jnp.int32).reshape(1)
    struct = jax.ShapeDtypeStruct

    def where(quarter, me_ref):
        mine = me_ref[0]
        low = (quarter % 2) != (mine % 2)
        high = (quarter // 2) != (mine // 2)
        return jnp.where(low, 1, 0) + jnp.where(high, 2, 0)

    def whole(shape):
        return pl.BlockSpec(shape, lambda q, t: (0,) * len(shape))

    outs = [struct((cols, width), F32)] * 4 + [struct(grad.shape, F32), struct(layer.shape, BF)]
    outs += [struct((width,), F32)] * 4 + [struct((experts,), jnp.int32)]
    return pl.pallas_call(
        finish_kernel,
        grid_spec=pltpu.PrefetchScalarGridSpec(
            num_scalar_prefetch=1,
            grid=(4,),
            in_specs=[
                pl.BlockSpec((2, n, 1, chunk, width), lambda q, t: (0, 0, where(q, t), 0, 0)),
                whole(pfin.shape), whole(small.shape), whole(grad.shape), whole(layer.shape),
            ],
            out_specs=[
                pl.BlockSpec((width, width), lambda q, t: (0, q)),
                pl.BlockSpec((width, width), lambda q, t: (q, 0)),
            ] + [whole(out.shape) for out in outs],
        ),
        out_shape=[struct((width, hidden), F32), struct((hidden, width), F32)] + outs,
        name="finish",
    )(me, rg, pfin, small, grad, layer)


def local(
    tokens,
    segment,
    key_mask,
    routes,
    gates,
    ln1_gain,
    ln1_bias,
    query_weight,
    key_weight,
    value_weight,
    out_weight,
    ln2_gain,
    ln2_bias,
    frozen_in,
    frozen_out,
    train_in,
    train_out,
    cotangent,
):
    vectors = (ln1_gain, ln1_bias, ln2_gain, ln2_bias)
    flat = (query_weight.T, key_weight.T, value_weight.T, out_weight)
    cols = out_weight.shape[0]
    token_args = (tokens[0], segment, key_mask, routes[0].T, gates[0].T, cotangent[0])
    rg, pfin, small, grad, layer = layer_step(
        *token_args, *vectors[:2], *flat, *vectors[2:], frozen_in[0], frozen_out[0], train_in[0], train_out[0]
    )
    grad_in, grad_out, out, value, query, key, grad, layer, *sums, counts = finish(
        rg, pfin, small, grad, layer, cols, EXP_DEV * lax.axis_size("ep")
    )
    gain_one, bias_one, gain_two, bias_two = sums
    return (
        layer[None], grad[None], gain_one, bias_one, query.T, key.T, value.T, out, gain_two, bias_two,
        grad_in[None], grad_out[None], counts,
    )


def solution(mesh):
    in_specs = (
        P(("ep", "dp"), "tp", None),
        P(("ep", "dp"), None),
        P(("ep", "dp"), None),
        P(("ep", "dp"), "tp", None),
        P(("ep", "dp"), "tp", None),
        P(),
        P(),
        P(None, "tp"),
        P(None, "tp"),
        P(None, "tp"),
        P("tp", None),
        P(),
        P(),
        P("ep", None, None),
        P("ep", None, None),
        P("ep", None, None),
        P("ep", None, None),
        P(("ep", "dp"), "tp", None),
    )
    out_specs = (
        P(("ep", "dp"), "tp", None),
        P(("ep", "dp"), "tp", None),
        P(),
        P(),
        P(None, "tp"),
        P(None, "tp"),
        P(None, "tp"),
        P("tp", None),
        P(),
        P(),
        P("ep", None, None),
        P("ep", None, None),
        P(),
    )
    return jax.shard_map(local, mesh=mesh, in_specs=in_specs, out_specs=out_specs, check_vma=False)
```

```python
import functools
import math

import jax
import jax.numpy as jnp
from jax import lax
from jax.experimental import pallas as pl
from jax.experimental.pallas import tpu as pltpu
from jax.sharding import PartitionSpec as P

HD = 64
EXP_DEV = 2
EPSILON = 1e-05
MASKED = -1e30
MESH = pl.DeviceIdType.MESH
BF = jnp.bfloat16
F32 = jnp.float32
CHUNK = 32
STEPS = (6, 3, 3, 1, 1, 3, 3, 3)
LAGS = (6, 8)
AHEAD = 2
FIRST = 1


def tp_peers():
    me = lax.axis_index("tp")
    one = me + 1 - 2 * (me % 2)
    return (me, one, (me + 2) % 4, (one + 2) % 4)


def remote(src, dst, send, recv, where):
    return pltpu.make_async_remote_copy(
        src_ref=src, dst_ref=dst, send_sem=send, recv_sem=recv,
        device_id=where, device_id_type=MESH,
    )


def entry_barrier(ep_count, dp_count):
    barrier = pltpu.get_barrier_semaphore()
    _, tp1, tp2, tp3 = tp_peers()
    ep, dp = lax.axis_index("ep"), lax.axis_index("dp")
    for peer in (tp1, tp2, tp3):
        pl.semaphore_signal(barrier, inc=1, device_id={"tp": peer}, device_id_type=MESH)
    for off in range(1, ep_count):
        pl.semaphore_signal(
            barrier, inc=1, device_id={"ep": (ep + off) % ep_count}, device_id_type=MESH
        )
    for off in range(1, dp_count):
        pl.semaphore_signal(
            barrier, inc=1, device_id={"dp": (dp + off) % dp_count}, device_id_type=MESH
        )
    pl.semaphore_wait(barrier, 3 + ep_count - 1 + dp_count - 1)


def gelu_pair(hidden):
    phi = 0.5 * (1.0 + lax.erf(hidden * math.sqrt(0.5)))
    dens = jnp.exp(-0.5 * hidden * hidden) * (1.0 / math.sqrt(2.0 * math.pi))
    return hidden * phi, phi + hidden * dens


def row_of(ref):
    return ref[...].reshape(1, -1)


def columns_of(ref):
    value = ref[...].astype(F32)
    padded = jnp.concatenate([value, jnp.zeros((6, value.shape[1]), F32)], axis=0)
    flipped = padded.T
    return flipped[:, 0:1], flipped[:, 1:2]


def fill_bias(seg_ref, key_ref, bias):
    segment = seg_ref[...]
    group_rows = segment.shape[1]
    lane = lax.broadcasted_iota(jnp.int32, segment.shape, 1)
    starts = (segment != pltpu.roll(segment, 1, 1)) | (lane == 0)
    keep = (key_ref[...] == 1) | starts
    segment = segment.astype(F32)
    column = jnp.broadcast_to(segment, (8, group_rows)).T[:, 0:1]
    kept = jnp.where(keep, segment, -1.0)
    bias[...] = jnp.where(column == kept, 0.0, MASKED)


def ln_rows(values, gain, bias):
    center = jnp.mean(values, axis=-1, keepdims=True)
    shifted = values - center
    spread = jnp.mean(shifted * shifted, axis=-1, keepdims=True)
    return shifted * lax.rsqrt(spread + EPSILON) * gain + bias


def route_picks(routes_ref, capacity, slots):
    first, second = (column.astype(jnp.int32) for column in columns_of(routes_ref))
    rows = first.shape[0]
    lane = lax.broadcasted_iota(jnp.int32, (rows, 128), 1)
    marks = jnp.where((lane == first) | (lane == second), 1.0, 0.0)
    row_id = lax.broadcasted_iota(jnp.int32, (rows, rows), 0)
    col_id = lax.broadcasted_iota(jnp.int32, (rows, rows), 1)
    lower = jnp.where(row_id > col_id, 1.0, 0.0).astype(BF)
    before = jnp.dot(lower, marks.astype(BF), preferred_element_type=F32)
    slot = lax.broadcasted_iota(jnp.int32, (rows, slots), 1)
    picks = []
    for route in (first, second):
        place = jnp.sum(jnp.where(lane == route, before, 0.0), axis=1, keepdims=True)
        chosen = route * capacity + place.astype(jnp.int32)
        picks.append(jnp.where(slot == chosen, 1.0, 0.0).astype(BF))
    return picks[0], picks[1], marks


def dot_tn(left, right):
    return lax.dot_general(left, right, (((0,), (0,)), ((), ())), preferred_element_type=F32)


def dot_nt(left, right):
    return lax.dot_general(left, right, (((1,), (1,)), ((), ())), preferred_element_type=F32)


def dot_nn(left, right):
    return jnp.dot(left, right, preferred_element_type=F32)


def ln_backward(values, gain, upstream):
    center = jnp.mean(values, axis=-1, keepdims=True)
    shifted = values - center
    spread = jnp.mean(shifted * shifted, axis=-1, keepdims=True)
    scale = lax.rsqrt(spread + EPSILON)
    unit = shifted * scale
    inner = upstream * gain
    along = jnp.mean(inner * unit, axis=-1, keepdims=True)
    grad = scale * (inner - jnp.mean(inner, axis=-1, keepdims=True) - unit * along)
    return grad, jnp.sum(upstream * unit, axis=0, keepdims=True), jnp.sum(upstream, axis=0, keepdims=True)


class Chain:
    def __init__(self, base, count, own, stage, near, home, final, sems, hooks):
        self.base, self.count, self.own, self.stage = base, count, own, stage
        self.near, self.home, self.final, self.hooks = near, home, final, hooks
        self.red_send, self.recv_a, self.recv_b, self.bc_send, self.bc_recv = sems
        self.dp = lax.axis_index("dp")

    def place(self, half):
        return 3 - self.dp if half == 0 else self.dp

    def peers(self, half):
        down, up = (self.dp + 3) % 4, (self.dp + 1) % 4
        return (down, up) if half == 0 else (up, down)

    def red(self, half, index, near):
        toward, away = self.peers(half)
        landing = self.stage.at[half, index]
        target, sem = (self.near(half, index), self.recv_b) if near else (landing, self.recv_a)
        return remote(
            landing, target, self.red_send.at[half, index], sem.at[half, index],
            {"dp": away if near else toward},
        )

    def spread(self, half, index, near, source=None):
        toward, away = self.peers(half)
        ref = self.final(half, index)
        return remote(
            (source or self.final)(half, index), ref, self.bc_send.at[1 if near else 0, half, index], self.bc_recv.at[half, index],
            {"dp": toward if near else away},
        )

    def offer(self, index):
        for half in (0, 1):
            place = self.place(half)

            @pl.when((place == 0) | (place == 3))
            def _():
                self.stage[half, index] = self.own(half, index).astype(BF)

            pl.when(place == 0)(lambda: self.red(half, index, False).start())
            pl.when(place == 3)(lambda: self.red(half, index, True).start())

    def step(self, s):
        for half in (0, 1):
            place = self.place(half)
            index = s - self.base - 2 * place

            @pl.when((index >= 0) & (index < self.count) & ((place == 1) | (place == 2)))
            def _():
                own = self.own(half, index)

                @pl.when(place == 1)
                def _():
                    self.red(half, index, False).wait_recv()
                    self.stage[half, index] = (own + self.stage[half, index].astype(F32)).astype(BF)
                    self.red(half, index, False).start()

                @pl.when(place == 2)
                def _():
                    self.red(half, index, False).wait_recv()
                    self.red(half, index, True).wait_recv()
                    total = own + self.stage[half, index].astype(F32) + self.near(half, index)[...].astype(F32)
                    self.home(half, index)[...] = total.astype(BF)

        for half in (0, 1):
            place = self.place(half)
            index = s - self.base - (8 - 2 * place + 4 * (place // 3))

            @pl.when((index >= 0) & (index < self.count))
            def _():
                @pl.when(place == 2)
                def _():
                    self.spread(half, index, False, self.home).start()
                    self.spread(half, index, True, self.home).start()

                @pl.when(place != 2)
                def _():
                    self.spread(half, index, False).wait_recv()

                @pl.when(place == 1)
                def _():
                    self.spread(half, index, False).start()

                self.hooks[0](half, index)

            for later, hook in enumerate(self.hooks[1:]):
                after = index - LAGS[later]
                pl.when((after >= 0) & (after < self.count))(functools.partial(hook, half, after))

    def drain(self, index):
        for half in (0, 1):
            place = self.place(half)

            @pl.when(place != 2)
            def _():
                self.red(half, index, False).wait_send()

            @pl.when((place == 1) | (place == 2))
            def _():
                self.spread(half, index, False).wait_send()

            @pl.when(place == 2)
            def _():
                self.spread(half, index, True).wait_send()


def layer_kernel(
    ep_count, heads, n,
    tok_ref, seg_ref, key_ref, routes_ref, gates_ref, cot_ref, g1_ref, b1_ref, wq_ref, wk_ref, wv_ref, wo_ref,
    g2_ref, b2_ref, fin_hbm, fout_hbm, tin_hbm, tout_hbm,
    rg, pfin, small_out, grad_ref, layer_ref,
    weights, group_ref, qkv_ref, heads_ref, lse_ref, middle_ref, gx, gs, picks, joined, bias,
    part, core_slot, mix, x_slot, sx, ss, ax, as_, out_acc, back_acc, out_ref, back_ref,
    act, slope, own, stage, near_slot, acc, pstage, pgbuf, yslot, ret_back, ret_out,
    piece, up_heads, pgrad, bpart, bcore_slot, bmix, bx_slot,
    sm, sm_tp, sm_ep, sm_dp, sm_a, sm_b,
    w_sem, a_send, a_recv, c_send, c_recv, m_send, m_recv, e_send, e_recv, t_send, t_recv,
    red_send, recv_a, recv_b, bc_send, bc_recv, x_send, x_recv, out_sem,
    pred_send, precv_a, precv_b, pbc_send, pbc_recv, y_send, y_recv, g_send, g_recv,
    b_send, b_recv, s_send, s_recv,
):
    tp, tp1, tp2, tp3 = tp_peers()
    ep, dp = lax.axis_index("ep"), lax.axis_index("dp")
    rows, width = tok_ref.shape
    cols = wq_ref.shape[0]
    group_rows = seg_ref.shape[1]
    pieces = weights.shape[0]
    capacity = sx.shape[2]
    slots = ep_count * EXP_DEV * capacity
    tokens = ep_count * capacity
    frozen, train = 0, 1
    offsets = range(1, ep_count)

    def slot_of(expert, index):
        return index if expert == train else (tp + 1 + index) % pieces

    def weight_loads(expert, index):
        slot = slot_of(expert, index)
        source_in, source_out = ((fin_hbm, fout_hbm), (tin_hbm, tout_hbm))[expert]
        at = pl.ds(pl.multiple_of(index * width, width), width)
        return [
            pltpu.make_async_copy(source_in.at[:, at], weights.at[slot, 0], w_sem.at[expert, 0, index]),
            pltpu.make_async_copy(source_out.at[at, :], weights.at[slot, 1], w_sem.at[expert, 1, index]),
        ]

    residual = tok_ref[...].astype(F32)
    group_ref[tp] = ln_rows(residual, row_of(g1_ref), row_of(b1_ref)).astype(BF)
    entry_barrier(ep_count, 4)
    sends = []

    def send(copy):
        sends.append(copy)
        copy.start()

    def gather_copy(stage_of, buf, slot, index, peer):
        return remote(
            buf.at[slot], buf.at[slot], a_send.at[stage_of, index], a_recv.at[stage_of, index], {"tp": peer}
        )

    send(gather_copy(0, group_ref, tp, 1, tp2))
    send(gather_copy(0, group_ref, tp, 0, tp1))
    for index in range(pieces):
        for copy in weight_loads(train, index):
            copy.start()

    pick0, pick1, marks = route_picks(routes_ref, capacity, slots)
    picks[0] = pick0
    picks[1] = pick1
    sm[...] = jnp.zeros_like(sm)
    sm[4:5, 0:128] = jnp.sum(marks, axis=0, keepdims=True)
    upstream = cot_ref[...].astype(F32)
    gate0, gate1 = columns_of(gates_ref)
    share0 = (gate0 * upstream).astype(BF)
    share1 = (gate1 * upstream).astype(BF)
    ss[...] = (dot_tn(pick0, share0) + dot_tn(pick1, share1)).astype(BF).reshape(ss.shape)

    def landing(kind, expert, source):
        if expert == train:
            return (gx, gs)[kind].at[0, source]
        return (ax, as_)[kind].at[source]

    def owner_copy(kind, expert, off):
        peer = (ep + off) % ep_count
        return remote(
            (sx, ss)[kind].at[peer, expert], landing(kind, expert, ep),
            e_send.at[kind, expert, off - 1], e_recv.at[kind, expert, off - 1], {"ep": peer},
        )

    def owner_wait(kind, expert, off):
        source = (ep + ep_count - off) % ep_count
        target = landing(kind, expert, source)
        remote(
            target, target, e_send.at[kind, expert, off - 1], e_recv.at[kind, expert, off - 1], {"ep": source}
        ).wait_recv()

    def token_copy(kind, rel, hop):
        buf = (gx, gs)[kind]
        origin = (ep + ep_count - rel) % ep_count
        source, peer = ((0, tp1), (0, tp2), (2, tp1))[hop - 1]
        return remote(
            buf.at[source, origin], buf.at[hop, origin],
            t_send.at[kind, rel, hop - 1], t_recv.at[kind, rel, hop - 1], {"tp": peer},
        )

    def dispatch(kind, source):
        for off in offsets:
            send(owner_copy(kind, train, off))
        (gx, gs)[kind][0, ep] = source[ep, train]
        send(token_copy(kind, 0, 2))
        send(token_copy(kind, 0, 1))
        for off in offsets:
            send(owner_copy(kind, frozen, off))
        (ax, as_)[kind][ep] = source[ep, frozen]

    def pass_on(kind):
        for off in offsets:
            owner_wait(kind, train, off)
            send(token_copy(kind, off, 2))
            send(token_copy(kind, off, 1))

    def forward(kind, rel):
        token_copy(kind, rel, 2).wait_recv()
        send(token_copy(kind, rel, 3))

    dispatch(1, ss)
    for index, ref in enumerate((wq_ref, wk_ref, wv_ref)):
        joined[index * cols : (index + 1) * cols, :] = ref[...]
    fill_bias(seg_ref, key_ref, bias)

    def project(slot):
        at = pl.ds(pl.multiple_of(slot * rows, rows), rows)
        qkv_ref[at, :] = dot_nt(group_ref[slot], joined[...]).astype(BF)

    project(tp)
    gather_copy(0, group_ref, tp1, 0, tp1).wait_recv()
    project(tp1)
    gather_copy(0, group_ref, tp2, 1, tp2).wait_recv()
    send(gather_copy(0, group_ref, tp2, 2, tp1))
    project(tp2)
    pass_on(1)
    gather_copy(0, group_ref, tp3, 2, tp1).wait_recv()
    project(tp3)

    scale = HD ** (-0.5)
    block = min(256, group_rows)
    for head in range(heads):
        low, high = head * HD, (head + 1) * HD
        for index in range(group_rows // block):
            at = slice(index * block, (index + 1) * block)
            query = qkv_ref[at, low:high]
            keys = qkv_ref[:, cols + low : cols + high]
            values = qkv_ref[:, 2 * cols + low : 2 * cols + high]
            scores = dot_nt(query, keys) * scale + bias[at, :]
            highest = jnp.max(scores, axis=-1, keepdims=True)
            weight = jnp.exp(scores - highest)
            total = jnp.sum(weight, axis=-1, keepdims=True)
            probs = (weight * (1.0 / total)).astype(BF)
            heads_ref[at, low:high] = dot_nn(probs, values).astype(BF)
            lse_ref[at, head : head + 1] = highest + jnp.log(total)

    def partial(slot):
        at = pl.ds(pl.multiple_of(slot * rows, rows), rows)
        return dot_nn(heads_ref[at, :], wo_ref[...])

    def core_copy(index):
        return remote(part.at[index], core_slot.at[index], c_send.at[0, index], c_recv.at[0, index], {"tp": tp1})

    part[0] = partial(tp3)
    send(core_copy(0))
    part[1] = partial(tp1)
    send(core_copy(1))
    crossing = partial(tp2)
    mine = tok_ref[...].astype(F32) + partial(tp)
    core_copy(0).wait_recv()
    mix[...] = (crossing + core_slot[0]).astype(BF)
    cross = remote(mix, x_slot, m_send.at[0], m_recv.at[0], {"tp": tp2})
    send(cross)
    forward(1, 0)
    core_copy(1).wait_recv()
    mine = mine + core_slot[1]
    cross.wait_recv()
    middle = mine + x_slot[...].astype(F32)
    middle_ref[...] = middle
    normed = ln_rows(middle, row_of(g2_ref), row_of(b2_ref)).astype(BF)
    sx[...] = dot_tn(picks[0] + picks[1], normed).astype(BF).reshape(sx.shape)
    dispatch(0, sx)
    for off in offsets:
        forward(1, off)
    pass_on(0)

    def expert_piece(expert, index, inputs, shares):
        slot = slot_of(expert, index)
        before = dot_nn(inputs, weights[slot, 0])
        through = dot_nt(shares, weights[slot, 1])
        value, grad = gelu_pair(before)
        slopes = (through * grad).astype(BF)
        produced = dot_nn(value.astype(BF), weights[slot, 1])
        returned = dot_nt(slopes, weights[slot, 0])

        @pl.when(index == 0)
        def _():
            out_acc[...] = produced
            back_acc[...] = returned

        @pl.when(index > 0)
        def _():
            out_acc[...] += produced
            back_acc[...] += returned

    def return_copy(kind, expert, off):
        peer = (ep + off) % ep_count
        source, target = ((back_ref, ret_back), (out_ref, ret_out))[kind]
        return remote(
            source.at[peer, expert], target.at[ep, expert],
            b_send.at[kind, expert, off - 1], b_recv.at[kind, expert, off - 1], {"ep": peer},
        )

    def return_wait(kind):
        target = (ret_back, ret_out)[kind]
        for expert in range(EXP_DEV):
            for off in offsets:
                source = (ep + ep_count - off) % ep_count
                remote(
                    target.at[source, expert], target.at[source, expert],
                    b_send.at[kind, expert, off - 1], b_recv.at[kind, expert, off - 1], {"ep": source},
                ).wait_recv()

    def give_back(expert):
        back_ref[:, expert] = back_acc[...].astype(BF).reshape(ep_count, capacity, width)
        out_ref[:, expert] = out_acc[...].astype(BF).reshape(ep_count, capacity, width)
        for kind in (0, 1):
            for off in offsets:
                send(return_copy(kind, expert, off))
        ret_back[ep, expert] = back_ref[ep, expert]
        ret_out[ep, expert] = out_ref[ep, expert]

    def train_piece(index, _):
        for copy in weight_loads(train, index):
            copy.wait()
        expert_piece(train, index, gx[0].reshape(tokens, width), gs[0].reshape(tokens, width))

        @pl.when(index != tp)
        def _():
            for copy in weight_loads(frozen, (index + pieces - 1 - tp) % pieces):
                copy.start()

        @pl.when(index == 1)
        def _():
            token_copy(0, 0, 2).wait_recv()
            token_copy(0, 0, 3).start()

        return 0

    lax.fori_loop(0, pieces, train_piece, 0)
    sends.append(token_copy(0, 0, 3))
    give_back(train)
    for off in offsets:
        forward(0, off)

    def frozen_piece(index, _):
        for copy in weight_loads(frozen, index):
            copy.wait()
        expert_piece(frozen, index, ax[...].reshape(tokens, width), as_[...].reshape(tokens, width))
        return 0

    for kind in (0, 1):
        for off in offsets:
            owner_wait(kind, frozen, off)
    lax.fori_loop(0, AHEAD, frozen_piece, 0)

    def hidden_block(index, _):
        for hop, when in ((1, 1), (3, 3)):
            @pl.when(index == when)
            def _(hop=hop):
                for kind in (0, 1):
                    for rel in range(ep_count):
                        token_copy(kind, rel, hop).wait_recv()

        before = dot_nn(gx[index].reshape(tokens, width), weights[tp, 0])
        through = dot_nt(gs[index].reshape(tokens, width), weights[tp, 1])
        value, grad = gelu_pair(before)
        at = pl.ds(pl.multiple_of(index * tokens, tokens), tokens)
        act[at, :] = value.astype(BF)
        slope[at, :] = (through * grad).astype(BF)
        return 0

    lax.fori_loop(0, 4, hidden_block, 0)
    for copy in weight_loads(frozen, pieces - 1):
        copy.start()

    def x_copy(half, index, hop, owner=False):
        source, peer = ((0, tp1), (0, tp2), (2, tp1))[hop - 1]
        from_ref = stage.at[half, index] if owner else rg.at[half, index, source]
        return remote(
            from_ref, rg.at[half, index, hop],
            x_send.at[hop - 1, half, index], x_recv.at[hop - 1, half, index], {"tp": peer},
        )

    def out_copy_of(half, index):
        return pltpu.make_async_copy(stage.at[half, index], rg.at[half, index, 0], out_sem.at[half, index])

    def cross_first(half, index):
        owner = expert_chain.place(half) == 2

        @pl.when(owner)
        def _():
            x_copy(half, index, 2, True).start()
            x_copy(half, index, 1, True).start()
            out_copy_of(half, index).start()

        @pl.when(jnp.logical_not(owner))
        def _():
            x_copy(half, index, 2).start()
            x_copy(half, index, 1).start()

    def cross_second(half, index):
        x_copy(half, index, 2).wait_recv()
        x_copy(half, index, 3).start()

    def cross_third(half, index):
        x_copy(half, index, 1).wait_recv()
        x_copy(half, index, 3).wait_recv()

    expert_chain = Chain(
        0, n, lambda half, index: own[half, pl.ds(pl.multiple_of(index * CHUNK, CHUNK), CHUNK), :],
        stage, lambda half, index: near_slot.at[half, index], lambda half, index: stage.at[half, index],
        lambda half, index: rg.at[half, index, 0],
        (red_send, recv_a, recv_b, bc_send, bc_recv), (cross_first, cross_second, cross_third),
    )
    span = 128

    def outer(index, _):
        at = pl.ds(pl.multiple_of(index * span, span), span)
        own[0, at, :] = dot_tn(gx[:, :, :, at].reshape(-1, span), slope[...])
        own[1, at, :] = dot_tn(act[:, at], gs[...].reshape(-1, width))
        @pl.when(index < blocks - 1)
        def _():
            for part_of in range(share_of):
                expert_chain.offer(index * share_of + part_of)

        return 0

    blocks, share_of = width // span, span // CHUNK
    lax.fori_loop(0, FIRST, outer, 0)
    clock = [0]
    proj_chain = None

    def run(count):
        def body(s, _):
            if proj_chain is not None:
                proj_chain.step(s)
            expert_chain.step(s)
            return 0

        lax.fori_loop(clock[0], clock[0] + count, body, 0)
        clock[0] += count

    lax.fori_loop(AHEAD, pieces, frozen_piece, 0)
    give_back(frozen)
    lax.fori_loop(FIRST, blocks, outer, 0)
    run(STEPS[0])
    return_wait(0)
    second = dot_nn(picks[0] + picks[1], ret_back[...].reshape(slots, width))
    inner_grad, gain_two, bias_two = ln_backward(middle_ref[...], row_of(g2_ref), second)
    middle_grad = cot_ref[...].astype(F32) + inner_grad
    grad_ref[...] = middle_grad
    piece[tp] = middle_grad.astype(BF)
    send(gather_copy(1, piece, tp, 1, tp2))
    send(gather_copy(1, piece, tp, 0, tp1))
    sm[2:3, :] = gain_two
    sm[3:4, :] = bias_two
    run(STEPS[1])

    def head_rows(slot):
        at = pl.ds(pl.multiple_of(slot * rows, rows), rows)
        up_heads[at, :] = dot_nt(piece[slot], wo_ref[...]).astype(BF)

    head_rows(tp)
    gather_copy(1, piece, tp1, 0, tp1).wait_recv()
    head_rows(tp1)
    gather_copy(1, piece, tp2, 1, tp2).wait_recv()
    send(gather_copy(1, piece, tp2, 2, tp1))
    head_rows(tp2)
    run(STEPS[2])
    gather_copy(1, piece, tp3, 2, tp1).wait_recv()
    head_rows(tp3)

    def y_scatter(batch, off):
        peer = (ep + off) % ep_count
        return remote(
            pgbuf.at[batch, peer], yslot.at[batch, off - 1], y_send.at[batch, off - 1], y_recv.at[batch, off - 1],
            {"ep": peer},
        )

    def proj_start(batch, value):
        pgbuf[batch] = value.astype(BF).reshape(pgbuf.shape[1:])
        for off in offsets:
            send(y_scatter(batch, off))

    def proj_sum(batch):
        total = pgbuf[batch, ep].astype(F32)
        for off in offsets:
            y_scatter(batch, off).wait_recv()
            total = total + yslot[batch, off - 1].astype(F32)
        acc[3 * batch : 3 * batch + 3] = total.reshape((3,) + acc.shape[1:])

    proj_start(0, dot_tn(heads_ref[...], piece[...].reshape(group_rows, width)))
    for head in range(heads):
        low, high = head * HD, (head + 1) * HD
        key_sum = value_sum = None
        for index in range(group_rows // block):
            at = slice(index * block, (index + 1) * block)
            query = qkv_ref[at, low:high]
            keys = qkv_ref[:, cols + low : cols + high]
            values = qkv_ref[:, 2 * cols + low : 2 * cols + high]
            above = up_heads[at, low:high]
            scores = dot_nt(query, keys) * scale + bias[at, :]
            probs = jnp.exp(scores - lse_ref[at, head : head + 1])
            prob_grad = dot_nt(above, values)
            centered = jnp.sum(probs * prob_grad, axis=-1, keepdims=True)
            score_grad = (probs * (prob_grad - centered)).astype(BF)
            pgrad[at, low:high] = (dot_nn(score_grad, keys) * scale).astype(BF)
            key_part = dot_tn(score_grad, query)
            value_part = dot_tn(probs.astype(BF), above)
            key_sum = key_part if key_sum is None else key_sum + key_part
            value_sum = value_part if value_sum is None else value_sum + value_part
        pgrad[:, cols + low : cols + high] = (key_sum * scale).astype(BF)
        pgrad[:, 2 * cols + low : 2 * cols + high] = value_sum.astype(BF)
        run(STEPS[3])

    def back_partial(slot):
        at = pl.ds(pl.multiple_of(slot * rows, rows), rows)
        return dot_nn(pgrad[at, :], joined[...])

    def back_core_copy(index):
        return remote(bpart.at[index], bcore_slot.at[index], c_send.at[1, index], c_recv.at[1, index], {"tp": tp1})

    bpart[0] = back_partial(tp3).astype(BF)
    send(back_core_copy(0))
    bpart[1] = back_partial(tp1).astype(BF)
    send(back_core_copy(1))
    normed = group_ref[...].reshape(group_rows, width)
    for batch, part_index in ((1, 2), (2, 0), (3, 1)):
        proj_start(batch, dot_tn(pgrad[:, part_index * cols : (part_index + 1) * cols], normed))
    crossing = back_partial(tp2)
    mine = back_partial(tp)
    run(STEPS[4])
    back_core_copy(0).wait_recv()
    bmix[...] = (crossing + bcore_slot[0].astype(F32)).astype(BF)
    back_cross = remote(bmix, bx_slot, m_send.at[1], m_recv.at[1], {"tp": tp2})
    send(back_cross)
    run(STEPS[5])
    back_core_copy(1).wait_recv()
    back_cross.wait_recv()
    first = mine + bcore_slot[1].astype(F32) + bx_slot[...].astype(F32)
    residual_part, gain_one, bias_one = ln_backward(tok_ref[...].astype(F32), row_of(g1_ref), first)
    grad_ref[...] += residual_part
    sm[0:1, :] = gain_one
    sm[1:2, :] = bias_one

    small = []

    def small_copy(slot, source, target, where):
        small.append(remote(source, target, s_send.at[slot], s_recv.at[slot], where))
        send(small[-1])

    for hop, peer in ((1, tp1), (2, tp2), (3, tp3)):
        small_copy(hop - 1, sm, sm_tp.at[hop - 1], {"tp": peer})
    for batch in range(4):
        proj_sum(batch)

    def y_gather(half, index, off):
        chunk = 2 * index + half
        return remote(
            pfin.at[ep, chunk], pfin.at[ep, chunk], g_send.at[off - 1, half, index], g_recv.at[off - 1, half, index],
            {"ep": (ep + off) % ep_count},
        )

    def y_first(half, index):
        for off in offsets:
            y_gather(half, index, off).start()

    proj_n = acc.shape[0] // 2
    proj_base = n - share_of
    assert proj_n >= share_of and clock[0] <= proj_base + 2
    proj_chain = Chain(
        proj_base, proj_n, lambda half, index: acc[2 * index + half], pstage,
        *[lambda half, index: pfin.at[ep, 2 * index + half]] * 3,
        (pred_send, precv_a, precv_b, pbc_send, pbc_recv), (y_first,),
    )
    for index in range(proj_n):
        proj_chain.offer(index)
        if index < share_of:
            expert_chain.offer(n - share_of + index)
    run(STEPS[6])
    return_wait(1)
    returned = ret_out[...].reshape(slots, width)
    gate0, gate1 = columns_of(gates_ref)
    mixture = gate0 * dot_nn(picks[0], returned) + gate1 * dot_nn(picks[1], returned)
    layer_ref[...] = (middle_ref[...] + mixture).astype(BF)
    for copy in small:
        copy.wait_recv()
    sm_a[...] = sm[...] + sm_tp[0] + sm_tp[1] + sm_tp[2]
    for off in offsets:
        small_copy(2 + off, sm_a, sm_ep.at[off - 1], {"ep": (ep + off) % ep_count})
    run(STEPS[7])
    for copy in small[3:]:
        copy.wait_recv()
    total = sm_a[...]
    for off in offsets:
        total = total + sm_ep[off - 1]
    sm_b[...] = total
    for off in range(1, 4):
        small_copy(1 + ep_count + off, sm_b, sm_dp.at[off - 1], {"dp": (dp + off) % 4})
    run(max(n + 8 + LAGS[1], proj_base + proj_n + 8) - clock[0])
    for copy in small[2 + ep_count :]:
        copy.wait_recv()
    small_out[...] = sm_b[...] + sm_dp[0] + sm_dp[1] + sm_dp[2]

    def y_finish(index, _):
        for half in (0, 1):
            chunk = 2 * index + half
            for off in offsets:
                source = (ep + ep_count - off) % ep_count
                y_gather(half, index, off).wait_send()
                remote(
                    pfin.at[source, chunk], pfin.at[source, chunk],
                    g_send.at[off - 1, half, index], g_recv.at[off - 1, half, index], {"ep": source},
                ).wait_recv()
        proj_chain.drain(index)
        return 0

    lax.fori_loop(0, proj_n, y_finish, 0)
    for copy in sends:
        copy.wait_send()

    def drain(index, _):
        expert_chain.drain(index)
        for half in (0, 1):
            for hop in (1, 2, 3):
                x_copy(half, index, hop).wait_send()
            pl.when(expert_chain.place(half) == 2)(out_copy_of(half, index).wait)
        return 0

    lax.fori_loop(0, n, drain, 0)


def layer_step(tokens, segment, key_mask, routes, gates, cot, g1, b1, wq, wk, wv, wo, g2, b2, fin, fout, tin, tout):
    ep_count = lax.axis_size("ep")
    assert lax.axis_size("dp") == 4 and lax.axis_size("tp") == 4
    rows, width = tokens.shape
    group_rows = segment.shape[1]
    cols = wq.shape[0]
    hidden = tin.shape[1]
    quarter = hidden // 4
    assert quarter == width and 4 * cols == width
    capacity = 4 * rows // (EXP_DEV * ep_count)
    gathered = 4 * ep_count * capacity
    n = width // CHUNK
    proj = 12
    chunk = width // (proj * ep_count)
    dma = pltpu.SemaphoreType.DMA
    vmem = pl.BlockSpec(memory_space=pltpu.VMEM)
    hbm = pl.BlockSpec(memory_space=pl.ANY)
    struct = jax.ShapeDtypeStruct
    block = (ep_count, EXP_DEV, capacity, width)
    single = (ep_count, capacity, width)
    others = ep_count - 1
    small = (8, width)
    pg_shape = (4, ep_count, cols // ep_count, width)
    y_shape = (4, others, cols // ep_count, width)
    many = 3 + others + 3
    return pl.pallas_call(
        functools.partial(layer_kernel, ep_count, cols // HD, n),
        out_shape=(
            pltpu.VMEM((2, n, 4, CHUNK, width), BF),
            pltpu.VMEM((ep_count, proj, chunk, width), BF),
            pltpu.VMEM(small, F32), pltpu.VMEM((rows, width), F32), pltpu.VMEM((rows, width), BF),
        ),
        in_specs=[vmem] * 14 + [hbm] * 4,
        out_specs=(hbm, vmem, vmem, vmem, vmem),
        scratch_shapes=[
            pltpu.VMEM((hidden // width, 2, width, width), BF),
            pltpu.VMEM((4, rows, width), BF), pltpu.VMEM((group_rows, 3 * cols), BF),
            pltpu.VMEM((group_rows, cols), BF), pltpu.VMEM((group_rows, 8), F32), pltpu.VMEM((rows, width), F32),
            pltpu.VMEM((4,) + single, BF), pltpu.VMEM((4,) + single, BF),
            pltpu.VMEM((2, rows, ep_count * EXP_DEV * capacity), BF),
            pltpu.VMEM((3 * cols, width), BF), pltpu.VMEM((group_rows, group_rows), F32),
            pltpu.VMEM((2, rows, width), F32), pltpu.VMEM((2, rows, width), F32),
            pltpu.VMEM((rows, width), BF), pltpu.VMEM((rows, width), BF),
            pltpu.VMEM(block, BF), pltpu.VMEM(block, BF), pltpu.VMEM(single, BF), pltpu.VMEM(single, BF),
            pltpu.VMEM((ep_count * capacity, width), F32), pltpu.VMEM((ep_count * capacity, width), F32),
            pltpu.VMEM(block, BF), pltpu.VMEM(block, BF),
            pltpu.VMEM((gathered, quarter), BF), pltpu.VMEM((gathered, quarter), BF),
            pltpu.VMEM((2, width, width), F32),
            pltpu.VMEM((2, n, CHUNK, width), BF), pltpu.VMEM((2, n, CHUNK, width), BF),
            pltpu.VMEM((proj, chunk, width), F32), pltpu.VMEM((2, proj // 2, chunk, width), BF),
            pltpu.VMEM(pg_shape, BF), pltpu.VMEM(y_shape, BF),
            pltpu.VMEM(block, BF), pltpu.VMEM(block, BF),
            pltpu.VMEM((4, rows, width), BF),
            pltpu.VMEM((group_rows, cols), BF), pltpu.VMEM((group_rows, 3 * cols), BF),
            pltpu.VMEM((2, rows, width), BF), pltpu.VMEM((2, rows, width), BF),
            pltpu.VMEM((rows, width), BF), pltpu.VMEM((rows, width), BF),
            pltpu.VMEM(small, F32), pltpu.VMEM((3,) + small, F32), pltpu.VMEM((others,) + small, F32),
            pltpu.VMEM((3,) + small, F32), pltpu.VMEM(small, F32), pltpu.VMEM(small, F32),
            dma((2, 2, hidden // width)), dma((2, 3)), dma((2, 3)), dma((2, 2)), dma((2, 2)), dma((2,)), dma((2,)),
            dma((2, 2, others)), dma((2, 2, others)), dma((2, ep_count, 3)), dma((2, ep_count, 3)),
            dma((2, n)), dma((2, n)), dma((2, n)), dma((2, 2, n)), dma((2, n)),
            dma((3, 2, n)), dma((3, 2, n)), dma((2, n)),
            dma((2, proj // 2)), dma((2, proj // 2)), dma((2, proj // 2)), dma((2, 2, proj // 2)), dma((2, proj // 2)),
            dma((4, others)), dma((4, others)), dma((others, 2, proj // 2)), dma((others, 2, proj // 2)),
            dma((2, 2, others)), dma((2, 2, others)), dma((many,)), dma((many,)),
        ],
        compiler_params=pltpu.CompilerParams(
            collective_id=0, has_side_effects=True, vmem_limit_bytes=51 * 1024 * 1024
        ),
        name="layer",
    )(tokens, segment, key_mask, routes, gates, cot, g1, b1, wq, wk, wv, wo, g2, b2, fin, fout, tin, tout)


def finish_kernel(
    tp_ref, rg_ref, pfin_ref, small_ref, grad_ref, layer_ref,
    gin_ref, gout_ref, o_ref, v_ref, q_ref, k_ref, tokens_ref, result_ref, a_ref, b_ref, c_ref, d_ref, count_ref,
):
    width = gin_ref.shape[1]
    gin_ref[...] = rg_ref[0, :, 0].reshape(gin_ref.shape).astype(F32)
    gout_ref[...] = rg_ref[1, :, 0].reshape(gout_ref.shape).astype(F32)

    @pl.when((pl.program_id(0) == 0) & (pl.program_id(1) == 0))
    def _():
        owners = pfin_ref.shape[0]
        span = q_ref.shape[0] // owners
        for index, ref in enumerate((o_ref, v_ref, q_ref, k_ref)):
            for owner in range(owners):
                value = pfin_ref[owner, 3 * index : 3 * index + 3].reshape(span, width)
                ref[owner * span : (owner + 1) * span, :] = value.astype(F32)
        tokens_ref[...] = grad_ref[...]
        result_ref[...] = layer_ref[...]
        for index, ref in enumerate((a_ref, b_ref, c_ref, d_ref)):
            ref[...] = small_ref[index : index + 1, :].reshape(width)
        count_ref[...] = small_ref[4:5, 0:128].astype(jnp.int32).reshape(128)[: count_ref.shape[0]]


def finish(rg, pfin, small, grad, layer, cols, experts):
    _, n, _, chunk, width = rg.shape
    hidden = 4 * width
    parts = 1
    me = lax.axis_index("tp").astype(jnp.int32).reshape(1)
    struct = jax.ShapeDtypeStruct

    def where(quarter, me_ref):
        mine = me_ref[0]
        low = (quarter % 2) != (mine % 2)
        high = (quarter // 2) != (mine // 2)
        return jnp.where(low, 1, 0) + jnp.where(high, 2, 0)

    def whole(shape):
        return pl.BlockSpec(shape, lambda q, i, t: (0,) * len(shape))

    outs = [struct((cols, width), F32)] * 4 + [struct(grad.shape, F32), struct(layer.shape, BF)]
    outs += [struct((width,), F32)] * 4 + [struct((experts,), jnp.int32)]
    return pl.pallas_call(
        finish_kernel,
        grid_spec=pltpu.PrefetchScalarGridSpec(
            num_scalar_prefetch=1,
            grid=(4, parts),
            in_specs=[
                pl.BlockSpec((2, n // parts, 1, chunk, width), lambda q, i, t: (0, i, where(q, t), 0, 0)),
                *[pl.BlockSpec(memory_space=pltpu.VMEM)] * 4,
            ],
            out_specs=[
                pl.BlockSpec((width // parts, width), lambda q, i, t: (i, q)),
                pl.BlockSpec((width // parts, width), lambda q, i, t: (parts * q + i, 0)),
            ] + [whole(out.shape) for out in outs],
        ),
        out_shape=[struct((width, hidden), F32), struct((hidden, width), F32)] + outs,
        compiler_params=pltpu.CompilerParams(vmem_limit_bytes=40 * 1024 * 1024),
        name="finish",
    )(me, *[pltpu.with_memory_space_constraint(value, pltpu.VMEM) for value in (rg, pfin, small, grad, layer)])


def local(
    tokens,
    segment,
    key_mask,
    routes,
    gates,
    ln1_gain,
    ln1_bias,
    query_weight,
    key_weight,
    value_weight,
    out_weight,
    ln2_gain,
    ln2_bias,
    frozen_in,
    frozen_out,
    train_in,
    train_out,
    cotangent,
):
    vectors = (ln1_gain, ln1_bias, ln2_gain, ln2_bias)
    flat = (query_weight.T, key_weight.T, value_weight.T, out_weight)
    cols = out_weight.shape[0]
    token_args = (tokens[0], segment, key_mask, routes[0].T, gates[0].T, cotangent[0])
    rg, pfin, small, grad, layer = layer_step(
        *token_args, *vectors[:2], *flat, *vectors[2:], frozen_in[0], frozen_out[0], train_in[0], train_out[0]
    )
    grad_in, grad_out, out, value, query, key, grad, layer, *sums, counts = finish(
        rg, pfin, small, grad, layer, cols, EXP_DEV * lax.axis_size("ep")
    )
    gain_one, bias_one, gain_two, bias_two = sums
    return (
        layer[None], grad[None], gain_one, bias_one, query.T, key.T, value.T, out, gain_two, bias_two,
        grad_in[None], grad_out[None], counts,
    )


def solution(mesh):
    in_specs = (
        P(("ep", "dp"), "tp", None),
        P(("ep", "dp"), None),
        P(("ep", "dp"), None),
        P(("ep", "dp"), "tp", None),
        P(("ep", "dp"), "tp", None),
        P(),
        P(),
        P(None, "tp"),
        P(None, "tp"),
        P(None, "tp"),
        P("tp", None),
        P(),
        P(),
        P("ep", None, None),
        P("ep", None, None),
        P("ep", None, None),
        P("ep", None, None),
        P(("ep", "dp"), "tp", None),
    )
    out_specs = (
        P(("ep", "dp"), "tp", None),
        P(("ep", "dp"), "tp", None),
        P(),
        P(),
        P(None, "tp"),
        P(None, "tp"),
        P(None, "tp"),
        P("tp", None),
        P(),
        P(),
        P("ep", None, None),
        P("ep", None, None),
        P(),
    )
    return jax.shard_map(local, mesh=mesh, in_specs=in_specs, out_specs=out_specs, check_vma=False)
```

```python
import functools
import math

import jax
import jax.numpy as jnp
from jax import lax
from jax.experimental import pallas as pl
from jax.experimental.pallas import tpu as pltpu
from jax.sharding import PartitionSpec as P

HD = 64
EXP_DEV = 2
EPSILON = 1e-05
MASKED = -1e30
MESH = pl.DeviceIdType.MESH
BF = jnp.bfloat16
F32 = jnp.float32
CHUNK = 32
STEPS = (6, 3, 3, 1, 1, 3, 6, 6)
GAP = 2
LAGS = (6, 8)
AHEAD = 2
FIRST = 1


def tp_peers():
    me = lax.axis_index("tp")
    one = me + 1 - 2 * (me % 2)
    return (me, one, (me + 2) % 4, (one + 2) % 4)


def remote(src, dst, send, recv, where):
    return pltpu.make_async_remote_copy(
        src_ref=src, dst_ref=dst, send_sem=send, recv_sem=recv,
        device_id=where, device_id_type=MESH,
    )


def entry_barrier(ep_count, dp_count):
    barrier = pltpu.get_barrier_semaphore()
    _, tp1, tp2, tp3 = tp_peers()
    ep, dp = lax.axis_index("ep"), lax.axis_index("dp")
    for peer in (tp1, tp2, tp3):
        pl.semaphore_signal(barrier, inc=1, device_id={"tp": peer}, device_id_type=MESH)
    for off in range(1, ep_count):
        pl.semaphore_signal(
            barrier, inc=1, device_id={"ep": (ep + off) % ep_count}, device_id_type=MESH
        )
    for off in range(1, dp_count):
        pl.semaphore_signal(
            barrier, inc=1, device_id={"dp": (dp + off) % dp_count}, device_id_type=MESH
        )
    pl.semaphore_wait(barrier, 3 + ep_count - 1 + dp_count - 1)


def gelu_pair(hidden):
    phi = 0.5 * (1.0 + lax.erf(hidden * math.sqrt(0.5)))
    dens = jnp.exp(-0.5 * hidden * hidden) * (1.0 / math.sqrt(2.0 * math.pi))
    return hidden * phi, phi + hidden * dens


def row_of(ref):
    return ref[...].reshape(1, -1)


def columns_of(ref):
    value = ref[...].astype(F32)
    padded = jnp.concatenate([value, jnp.zeros((6, value.shape[1]), F32)], axis=0)
    flipped = padded.T
    return flipped[:, 0:1], flipped[:, 1:2]


def fill_bias(seg_ref, key_ref, bias):
    segment = seg_ref[...]
    group_rows = segment.shape[1]
    lane = lax.broadcasted_iota(jnp.int32, segment.shape, 1)
    starts = (segment != pltpu.roll(segment, 1, 1)) | (lane == 0)
    keep = (key_ref[...] == 1) | starts
    segment = segment.astype(F32)
    column = jnp.broadcast_to(segment, (8, group_rows)).T[:, 0:1]
    kept = jnp.where(keep, segment, -1.0)
    bias[...] = jnp.where(column == kept, 0.0, MASKED)


def ln_rows(values, gain, bias):
    center = jnp.mean(values, axis=-1, keepdims=True)
    shifted = values - center
    spread = jnp.mean(shifted * shifted, axis=-1, keepdims=True)
    return shifted * lax.rsqrt(spread + EPSILON) * gain + bias


def route_picks(routes_ref, capacity, slots):
    first, second = (column.astype(jnp.int32) for column in columns_of(routes_ref))
    rows = first.shape[0]
    lane = lax.broadcasted_iota(jnp.int32, (rows, 128), 1)
    marks = jnp.where((lane == first) | (lane == second), 1.0, 0.0)
    row_id = lax.broadcasted_iota(jnp.int32, (rows, rows), 0)
    col_id = lax.broadcasted_iota(jnp.int32, (rows, rows), 1)
    lower = jnp.where(row_id > col_id, 1.0, 0.0).astype(BF)
    before = jnp.dot(lower, marks.astype(BF), preferred_element_type=F32)
    slot = lax.broadcasted_iota(jnp.int32, (rows, slots), 1)
    picks = []
    for route in (first, second):
        place = jnp.sum(jnp.where(lane == route, before, 0.0), axis=1, keepdims=True)
        chosen = route * capacity + place.astype(jnp.int32)
        picks.append(jnp.where(slot == chosen, 1.0, 0.0).astype(BF))
    return picks[0], picks[1], marks


def dot_tn(left, right):
    return lax.dot_general(left, right, (((0,), (0,)), ((), ())), preferred_element_type=F32)


def dot_nt(left, right):
    return lax.dot_general(left, right, (((1,), (1,)), ((), ())), preferred_element_type=F32)


def dot_nn(left, right):
    return jnp.dot(left, right, preferred_element_type=F32)


def ln_backward(values, gain, upstream):
    center = jnp.mean(values, axis=-1, keepdims=True)
    shifted = values - center
    spread = jnp.mean(shifted * shifted, axis=-1, keepdims=True)
    scale = lax.rsqrt(spread + EPSILON)
    unit = shifted * scale
    inner = upstream * gain
    along = jnp.mean(inner * unit, axis=-1, keepdims=True)
    grad = scale * (inner - jnp.mean(inner, axis=-1, keepdims=True) - unit * along)
    return grad, jnp.sum(upstream * unit, axis=0, keepdims=True), jnp.sum(upstream, axis=0, keepdims=True)


class Chain:
    def __init__(self, base, count, own, stage, near, home, final, sems, hooks):
        self.base, self.count, self.own, self.stage = base, count, own, stage
        self.near, self.home, self.final, self.hooks = near, home, final, hooks
        self.red_send, self.recv_a, self.recv_b, self.bc_send, self.bc_recv = sems
        self.dp = lax.axis_index("dp")

    def place(self, half):
        return 3 - self.dp if half == 0 else self.dp

    def peers(self, half):
        down, up = (self.dp + 3) % 4, (self.dp + 1) % 4
        return (down, up) if half == 0 else (up, down)

    def red(self, half, index, near):
        toward, away = self.peers(half)
        landing = self.stage.at[half, index]
        target, sem = (self.near(half, index), self.recv_b) if near else (landing, self.recv_a)
        return remote(
            landing, target, self.red_send.at[half, index], sem.at[half, index],
            {"dp": away if near else toward},
        )

    def spread(self, half, index, near, source=None):
        toward, away = self.peers(half)
        ref = self.final(half, index)
        return remote(
            (source or self.final)(half, index), ref, self.bc_send.at[1 if near else 0, half, index], self.bc_recv.at[half, index],
            {"dp": toward if near else away},
        )

    def offer(self, index):
        for half in (0, 1):
            place = self.place(half)

            @pl.when((place == 0) | (place == 3))
            def _():
                self.stage[half, index] = self.own(half, index).astype(BF)

            pl.when(place == 0)(lambda: self.red(half, index, False).start())
            pl.when(place == 3)(lambda: self.red(half, index, True).start())

    def step(self, s):
        for half in (0, 1):
            place = self.place(half)
            index = s - self.base - GAP * place

            @pl.when((index >= 0) & (index < self.count) & ((place == 1) | (place == 2)))
            def _():
                own = self.own(half, index)

                @pl.when(place == 1)
                def _():
                    self.red(half, index, False).wait_recv()
                    self.stage[half, index] = (own + self.stage[half, index].astype(F32)).astype(BF)
                    self.red(half, index, False).start()

                @pl.when(place == 2)
                def _():
                    self.red(half, index, False).wait_recv()
                    self.red(half, index, True).wait_recv()
                    total = own + self.stage[half, index].astype(F32) + self.near(half, index)[...].astype(F32)
                    self.home(half, index)[...] = total.astype(BF)

        for half in (0, 1):
            place = self.place(half)
            index = s - self.base - GAP * (4 - place + 2 * (place // 3))

            @pl.when((index >= 0) & (index < self.count))
            def _():
                @pl.when(place == 2)
                def _():
                    self.spread(half, index, False, self.home).start()
                    self.spread(half, index, True, self.home).start()

                @pl.when(place != 2)
                def _():
                    self.spread(half, index, False).wait_recv()

                @pl.when(place == 1)
                def _():
                    self.spread(half, index, False).start()

                self.hooks[0](half, index)

            for later, hook in enumerate(self.hooks[1:]):
                after = index - LAGS[later]
                pl.when((after >= 0) & (after < self.count))(functools.partial(hook, half, after))

    def drain(self, index):
        for half in (0, 1):
            place = self.place(half)

            @pl.when(place != 2)
            def _():
                self.red(half, index, False).wait_send()

            @pl.when((place == 1) | (place == 2))
            def _():
                self.spread(half, index, False).wait_send()

            @pl.when(place == 2)
            def _():
                self.spread(half, index, True).wait_send()


def layer_kernel(
    ep_count, heads, n,
    tok_ref, seg_ref, key_ref, routes_ref, gates_ref, cot_ref, g1_ref, b1_ref, wq_ref, wk_ref, wv_ref, wo_ref,
    g2_ref, b2_ref, fin_hbm, fout_hbm, tin_hbm, tout_hbm,
    rg, pfin, small_out, grad_ref, layer_ref,
    weights, group_ref, qkv_ref, heads_ref, lse_ref, middle_ref, gx, gs, picks, joined, bias,
    part, core_slot, mix, x_slot, sx, ss, ax, as_, out_acc, back_acc, out_ref, back_ref,
    act, slope, own, stage, near_slot, acc, pstage, pgbuf, yslot, ret_back, ret_out,
    piece, up_heads, pgrad, bpart, bcore_slot, bmix, bx_slot,
    sm, sm_tp, sm_ep, sm_dp, sm_a, sm_b,
    w_sem, a_send, a_recv, c_send, c_recv, m_send, m_recv, e_send, e_recv, t_send, t_recv,
    red_send, recv_a, recv_b, bc_send, bc_recv, x_send, x_recv, out_sem,
    pred_send, precv_a, precv_b, pbc_send, pbc_recv, y_send, y_recv, g_send, g_recv,
    b_send, b_recv, s_send, s_recv,
):
    tp, tp1, tp2, tp3 = tp_peers()
    ep, dp = lax.axis_index("ep"), lax.axis_index("dp")
    rows, width = tok_ref.shape
    cols = wq_ref.shape[0]
    group_rows = seg_ref.shape[1]
    pieces = weights.shape[0]
    capacity = sx.shape[2]
    slots = ep_count * EXP_DEV * capacity
    tokens = ep_count * capacity
    frozen, train = 0, 1
    offsets = range(1, ep_count)

    def slot_of(expert, index):
        return index if expert == train else (tp + 1 + index) % pieces

    def weight_loads(expert, index):
        slot = slot_of(expert, index)
        source_in, source_out = ((fin_hbm, fout_hbm), (tin_hbm, tout_hbm))[expert]
        at = pl.ds(pl.multiple_of(index * width, width), width)
        return [
            pltpu.make_async_copy(source_in.at[:, at], weights.at[slot, 0], w_sem.at[expert, 0, index]),
            pltpu.make_async_copy(source_out.at[at, :], weights.at[slot, 1], w_sem.at[expert, 1, index]),
        ]

    residual = tok_ref[...].astype(F32)
    group_ref[tp] = ln_rows(residual, row_of(g1_ref), row_of(b1_ref)).astype(BF)
    entry_barrier(ep_count, 4)
    sends = []

    def send(copy):
        sends.append(copy)
        copy.start()

    def gather_copy(stage_of, buf, slot, index, peer):
        return remote(
            buf.at[slot], buf.at[slot], a_send.at[stage_of, index], a_recv.at[stage_of, index], {"tp": peer}
        )

    send(gather_copy(0, group_ref, tp, 1, tp2))
    send(gather_copy(0, group_ref, tp, 0, tp1))
    for index in range(pieces):
        for copy in weight_loads(train, index):
            copy.start()

    pick0, pick1, marks = route_picks(routes_ref, capacity, slots)
    picks[0] = pick0
    picks[1] = pick1
    sm[...] = jnp.zeros_like(sm)
    sm[4:5, 0:128] = jnp.sum(marks, axis=0, keepdims=True)
    upstream = cot_ref[...].astype(F32)
    gate0, gate1 = columns_of(gates_ref)
    share0 = (gate0 * upstream).astype(BF)
    share1 = (gate1 * upstream).astype(BF)
    ss[...] = (dot_tn(pick0, share0) + dot_tn(pick1, share1)).astype(BF).reshape(ss.shape)

    def landing(kind, expert, source):
        if expert == train:
            return (gx, gs)[kind].at[0, source]
        return (ax, as_)[kind].at[source]

    def owner_copy(kind, expert, off):
        peer = (ep + off) % ep_count
        return remote(
            (sx, ss)[kind].at[peer, expert], landing(kind, expert, ep),
            e_send.at[kind, expert, off - 1], e_recv.at[kind, expert, off - 1], {"ep": peer},
        )

    def owner_wait(kind, expert, off):
        source = (ep + ep_count - off) % ep_count
        target = landing(kind, expert, source)
        remote(
            target, target, e_send.at[kind, expert, off - 1], e_recv.at[kind, expert, off - 1], {"ep": source}
        ).wait_recv()

    def token_copy(kind, rel, hop):
        buf = (gx, gs)[kind]
        origin = (ep + ep_count - rel) % ep_count
        source, peer = ((0, tp1), (0, tp2), (2, tp1))[hop - 1]
        return remote(
            buf.at[source, origin], buf.at[hop, origin],
            t_send.at[kind, rel, hop - 1], t_recv.at[kind, rel, hop - 1], {"tp": peer},
        )

    def dispatch(kind, source):
        for off in offsets:
            send(owner_copy(kind, train, off))
        (gx, gs)[kind][0, ep] = source[ep, train]
        send(token_copy(kind, 0, 2))
        send(token_copy(kind, 0, 1))
        for off in offsets:
            send(owner_copy(kind, frozen, off))
        (ax, as_)[kind][ep] = source[ep, frozen]

    def pass_on(kind):
        for off in offsets:
            owner_wait(kind, train, off)
            send(token_copy(kind, off, 2))
            send(token_copy(kind, off, 1))

    def forward(kind, rel):
        token_copy(kind, rel, 2).wait_recv()
        send(token_copy(kind, rel, 3))

    dispatch(1, ss)
    for index, ref in enumerate((wq_ref, wk_ref, wv_ref)):
        joined[index * cols : (index + 1) * cols, :] = ref[...]
    fill_bias(seg_ref, key_ref, bias)

    def project(slot):
        at = pl.ds(pl.multiple_of(slot * rows, rows), rows)
        qkv_ref[at, :] = dot_nt(group_ref[slot], joined[...]).astype(BF)

    project(tp)
    gather_copy(0, group_ref, tp1, 0, tp1).wait_recv()
    project(tp1)
    gather_copy(0, group_ref, tp2, 1, tp2).wait_recv()
    send(gather_copy(0, group_ref, tp2, 2, tp1))
    project(tp2)
    gather_copy(0, group_ref, tp3, 2, tp1).wait_recv()
    project(tp3)

    scale = HD ** (-0.5)
    block = min(256, group_rows)
    for head in range(heads):
        low, high = head * HD, (head + 1) * HD
        for index in range(group_rows // block):
            at = slice(index * block, (index + 1) * block)
            query = qkv_ref[at, low:high]
            keys = qkv_ref[:, cols + low : cols + high]
            values = qkv_ref[:, 2 * cols + low : 2 * cols + high]
            scores = dot_nt(query, keys) * scale + bias[at, :]
            highest = jnp.max(scores, axis=-1, keepdims=True)
            weight = jnp.exp(scores - highest)
            total = jnp.sum(weight, axis=-1, keepdims=True)
            probs = (weight * (1.0 / total)).astype(BF)
            heads_ref[at, low:high] = dot_nn(probs, values).astype(BF)
            lse_ref[at, head : head + 1] = highest + jnp.log(total)

    def partial(slot):
        at = pl.ds(pl.multiple_of(slot * rows, rows), rows)
        return dot_nn(heads_ref[at, :], wo_ref[...])

    def core_copy(index):
        return remote(part.at[index], core_slot.at[index], c_send.at[0, index], c_recv.at[0, index], {"tp": tp1})

    part[0] = partial(tp3)
    send(core_copy(0))
    part[1] = partial(tp1)
    send(core_copy(1))
    crossing = partial(tp2)
    mine = tok_ref[...].astype(F32) + partial(tp)
    core_copy(0).wait_recv()
    mix[...] = (crossing + core_slot[0]).astype(BF)
    cross = remote(mix, x_slot, m_send.at[0], m_recv.at[0], {"tp": tp2})
    send(cross)
    pass_on(1)
    forward(1, 0)
    core_copy(1).wait_recv()
    mine = mine + core_slot[1]
    cross.wait_recv()
    middle = mine + x_slot[...].astype(F32)
    middle_ref[...] = middle
    normed = ln_rows(middle, row_of(g2_ref), row_of(b2_ref)).astype(BF)
    sx[...] = dot_tn(picks[0] + picks[1], normed).astype(BF).reshape(sx.shape)
    dispatch(0, sx)
    for off in offsets:
        forward(1, off)
    pass_on(0)

    def expert_piece(expert, index, inputs, shares):
        slot = slot_of(expert, index)
        before = dot_nn(inputs, weights[slot, 0])
        through = dot_nt(shares, weights[slot, 1])
        value, grad = gelu_pair(before)
        slopes = (through * grad).astype(BF)
        produced = dot_nn(value.astype(BF), weights[slot, 1])
        returned = dot_nt(slopes, weights[slot, 0])

        @pl.when(index == 0)
        def _():
            out_acc[...] = produced
            back_acc[...] = returned

        @pl.when(index > 0)
        def _():
            out_acc[...] += produced
            back_acc[...] += returned

    def return_copy(kind, expert, off):
        peer = (ep + off) % ep_count
        source, target = ((back_ref, ret_back), (out_ref, ret_out))[kind]
        return remote(
            source.at[peer, expert], target.at[ep, expert],
            b_send.at[kind, expert, off - 1], b_recv.at[kind, expert, off - 1], {"ep": peer},
        )

    def return_wait(kind):
        target = (ret_back, ret_out)[kind]
        for expert in range(EXP_DEV):
            for off in offsets:
                source = (ep + ep_count - off) % ep_count
                remote(
                    target.at[source, expert], target.at[source, expert],
                    b_send.at[kind, expert, off - 1], b_recv.at[kind, expert, off - 1], {"ep": source},
                ).wait_recv()

    def give_back(expert):
        back_ref[:, expert] = back_acc[...].astype(BF).reshape(ep_count, capacity, width)
        out_ref[:, expert] = out_acc[...].astype(BF).reshape(ep_count, capacity, width)
        for kind in (0, 1):
            for off in offsets:
                send(return_copy(kind, expert, off))
        ret_back[ep, expert] = back_ref[ep, expert]
        ret_out[ep, expert] = out_ref[ep, expert]

    def train_piece(index, _):
        for copy in weight_loads(train, index):
            copy.wait()
        expert_piece(train, index, gx[0].reshape(tokens, width), gs[0].reshape(tokens, width))

        @pl.when(index != tp)
        def _():
            for copy in weight_loads(frozen, (index + pieces - 1 - tp) % pieces):
                copy.start()

        @pl.when(index == 1)
        def _():
            token_copy(0, 0, 2).wait_recv()
            token_copy(0, 0, 3).start()

        return 0

    lax.fori_loop(0, pieces, train_piece, 0)
    sends.append(token_copy(0, 0, 3))
    give_back(train)
    for off in offsets:
        forward(0, off)

    def frozen_piece(index, _):
        for copy in weight_loads(frozen, index):
            copy.wait()
        expert_piece(frozen, index, ax[...].reshape(tokens, width), as_[...].reshape(tokens, width))
        return 0

    for kind in (0, 1):
        for off in offsets:
            owner_wait(kind, frozen, off)
    lax.fori_loop(0, AHEAD, frozen_piece, 0)

    def hidden_block(index, _):
        for hop, when in ((1, 1), (3, 3)):
            @pl.when(index == when)
            def _(hop=hop):
                for kind in (0, 1):
                    for rel in range(ep_count):
                        token_copy(kind, rel, hop).wait_recv()

        before = dot_nn(gx[index].reshape(tokens, width), weights[tp, 0])
        through = dot_nt(gs[index].reshape(tokens, width), weights[tp, 1])
        value, grad = gelu_pair(before)
        at = pl.ds(pl.multiple_of(index * tokens, tokens), tokens)
        act[at, :] = value.astype(BF)
        slope[at, :] = (through * grad).astype(BF)
        return 0

    lax.fori_loop(0, 4, hidden_block, 0)
    for copy in weight_loads(frozen, pieces - 1):
        copy.start()

    def x_copy(half, index, hop, owner=False):
        source, peer = ((0, tp1), (0, tp2), (2, tp1))[hop - 1]
        from_ref = stage.at[half, index] if owner else rg.at[half, index, source]
        return remote(
            from_ref, rg.at[half, index, hop],
            x_send.at[hop - 1, half, index], x_recv.at[hop - 1, half, index], {"tp": peer},
        )

    def out_copy_of(half, index):
        return pltpu.make_async_copy(stage.at[half, index], rg.at[half, index, 0], out_sem.at[half, index])

    def cross_first(half, index):
        owner = expert_chain.place(half) == 2

        @pl.when(owner)
        def _():
            x_copy(half, index, 2, True).start()
            x_copy(half, index, 1, True).start()
            out_copy_of(half, index).start()

        @pl.when(jnp.logical_not(owner))
        def _():
            x_copy(half, index, 2).start()
            x_copy(half, index, 1).start()

    def cross_second(half, index):
        x_copy(half, index, 2).wait_recv()
        x_copy(half, index, 3).start()

    def cross_third(half, index):
        x_copy(half, index, 1).wait_recv()
        x_copy(half, index, 3).wait_recv()

    expert_chain = Chain(
        0, n, lambda half, index: own[half, pl.ds(pl.multiple_of(index * CHUNK, CHUNK), CHUNK), :],
        stage, lambda half, index: near_slot.at[half, index], lambda half, index: stage.at[half, index],
        lambda half, index: rg.at[half, index, 0],
        (red_send, recv_a, recv_b, bc_send, bc_recv), (cross_first, cross_second, cross_third),
    )
    span = 128

    def outer(index, _):
        at = pl.ds(pl.multiple_of(index * span, span), span)
        own[0, at, :] = dot_tn(gx[:, :, :, at].reshape(-1, span), slope[...])
        own[1, at, :] = dot_tn(act[:, at], gs[...].reshape(-1, width))
        @pl.when(index < blocks - 1)
        def _():
            for part_of in range(share_of):
                expert_chain.offer(index * share_of + part_of)

        return 0

    blocks, share_of = width // span, span // CHUNK
    lax.fori_loop(0, FIRST, outer, 0)
    clock = [0]
    proj_chain = None

    def run(count):
        def body(s, _):
            if proj_chain is not None:
                proj_chain.step(s)
            expert_chain.step(s)
            return 0

        lax.fori_loop(clock[0], clock[0] + count, body, 0)
        clock[0] += count

    lax.fori_loop(AHEAD, pieces, frozen_piece, 0)
    give_back(frozen)
    lax.fori_loop(FIRST, blocks, outer, 0)
    run(STEPS[0])
    return_wait(0)
    second = dot_nn(picks[0] + picks[1], ret_back[...].reshape(slots, width))
    inner_grad, gain_two, bias_two = ln_backward(middle_ref[...], row_of(g2_ref), second)
    middle_grad = cot_ref[...].astype(F32) + inner_grad
    grad_ref[...] = middle_grad
    piece[tp] = middle_grad.astype(BF)
    send(gather_copy(1, piece, tp, 1, tp2))
    send(gather_copy(1, piece, tp, 0, tp1))
    sm[2:3, :] = gain_two
    sm[3:4, :] = bias_two
    run(STEPS[1])

    def head_rows(slot):
        at = pl.ds(pl.multiple_of(slot * rows, rows), rows)
        up_heads[at, :] = dot_nt(piece[slot], wo_ref[...]).astype(BF)

    head_rows(tp)
    gather_copy(1, piece, tp1, 0, tp1).wait_recv()
    head_rows(tp1)
    gather_copy(1, piece, tp2, 1, tp2).wait_recv()
    send(gather_copy(1, piece, tp2, 2, tp1))
    head_rows(tp2)
    run(STEPS[2])
    gather_copy(1, piece, tp3, 2, tp1).wait_recv()
    head_rows(tp3)

    def y_scatter(batch, off):
        peer = (ep + off) % ep_count
        return remote(
            pgbuf.at[batch, peer], yslot.at[batch, off - 1], y_send.at[batch, off - 1], y_recv.at[batch, off - 1],
            {"ep": peer},
        )

    def proj_start(batch, value):
        pgbuf[batch] = value.astype(BF).reshape(pgbuf.shape[1:])
        for off in offsets:
            send(y_scatter(batch, off))

    def proj_sum(batch):
        total = pgbuf[batch, ep].astype(F32)
        for off in offsets:
            y_scatter(batch, off).wait_recv()
            total = total + yslot[batch, off - 1].astype(F32)
        acc[3 * batch : 3 * batch + 3] = total.reshape((3,) + acc.shape[1:])

    proj_start(0, dot_tn(heads_ref[...], piece[...].reshape(group_rows, width)))
    for head in range(heads):
        low, high = head * HD, (head + 1) * HD
        key_sum = value_sum = None
        for index in range(group_rows // block):
            at = slice(index * block, (index + 1) * block)
            query = qkv_ref[at, low:high]
            keys = qkv_ref[:, cols + low : cols + high]
            values = qkv_ref[:, 2 * cols + low : 2 * cols + high]
            above = up_heads[at, low:high]
            scores = dot_nt(query, keys) * scale + bias[at, :]
            probs = jnp.exp(scores - lse_ref[at, head : head + 1])
            prob_grad = dot_nt(above, values)
            centered = jnp.sum(probs * prob_grad, axis=-1, keepdims=True)
            score_grad = (probs * (prob_grad - centered)).astype(BF)
            pgrad[at, low:high] = (dot_nn(score_grad, keys) * scale).astype(BF)
            key_part = dot_tn(score_grad, query)
            value_part = dot_tn(probs.astype(BF), above)
            key_sum = key_part if key_sum is None else key_sum + key_part
            value_sum = value_part if value_sum is None else value_sum + value_part
        pgrad[:, cols + low : cols + high] = (key_sum * scale).astype(BF)
        pgrad[:, 2 * cols + low : 2 * cols + high] = value_sum.astype(BF)
        run(STEPS[3])

    def back_partial(slot):
        at = pl.ds(pl.multiple_of(slot * rows, rows), rows)
        return dot_nn(pgrad[at, :], joined[...])

    def back_core_copy(index):
        return remote(bpart.at[index], bcore_slot.at[index], c_send.at[1, index], c_recv.at[1, index], {"tp": tp1})

    bpart[0] = back_partial(tp3).astype(BF)
    send(back_core_copy(0))
    bpart[1] = back_partial(tp1).astype(BF)
    send(back_core_copy(1))
    normed = group_ref[...].reshape(group_rows, width)
    for batch, part_index in ((1, 2), (2, 0), (3, 1)):
        proj_start(batch, dot_tn(pgrad[:, part_index * cols : (part_index + 1) * cols], normed))
    crossing = back_partial(tp2)
    mine = back_partial(tp)
    run(STEPS[4])
    back_core_copy(0).wait_recv()
    bmix[...] = (crossing + bcore_slot[0].astype(F32)).astype(BF)
    back_cross = remote(bmix, bx_slot, m_send.at[1], m_recv.at[1], {"tp": tp2})
    send(back_cross)
    def y_gather(half, index, off):
        chunk = 2 * index + half
        return remote(
            pfin.at[ep, chunk], pfin.at[ep, chunk], g_send.at[off - 1, half, index], g_recv.at[off - 1, half, index],
            {"ep": (ep + off) % ep_count},
        )

    def y_first(half, index):
        for off in offsets:
            y_gather(half, index, off).start()

    proj_n = acc.shape[0] // 2
    proj_base = n - share_of
    assert proj_n >= share_of and clock[0] <= proj_base + GAP
    proj_chain = Chain(
        proj_base, proj_n, lambda half, index: acc[2 * index + half], pstage,
        *[lambda half, index: pfin.at[ep, 2 * index + half]] * 3,
        (pred_send, precv_a, precv_b, pbc_send, pbc_recv), (y_first,),
    )

    def proj_offer(batches):
        for batch in batches:
            proj_sum(batch)
        for index in range((3 * batches[0] + 1) // 2, 3 * (batches[-1] + 1) // 2):
            proj_chain.offer(index)
            if index < share_of:
                expert_chain.offer(n - share_of + index)

    run(STEPS[5])
    proj_offer((0, 1))
    back_core_copy(1).wait_recv()
    back_cross.wait_recv()
    first = mine + bcore_slot[1].astype(F32) + bx_slot[...].astype(F32)
    residual_part, gain_one, bias_one = ln_backward(tok_ref[...].astype(F32), row_of(g1_ref), first)
    grad_ref[...] += residual_part
    sm[0:1, :] = gain_one
    sm[1:2, :] = bias_one

    small = []

    def small_copy(slot, source, target, where):
        small.append(remote(source, target, s_send.at[slot], s_recv.at[slot], where))
        send(small[-1])

    for hop, peer in ((1, tp1), (2, tp2), (3, tp3)):
        small_copy(hop - 1, sm, sm_tp.at[hop - 1], {"tp": peer})
    proj_offer((2, 3))

    run(STEPS[6])
    return_wait(1)
    returned = ret_out[...].reshape(slots, width)
    gate0, gate1 = columns_of(gates_ref)
    mixture = gate0 * dot_nn(picks[0], returned) + gate1 * dot_nn(picks[1], returned)
    layer_ref[...] = (middle_ref[...] + mixture).astype(BF)
    for copy in small:
        copy.wait_recv()
    sm_a[...] = sm[...] + sm_tp[0] + sm_tp[1] + sm_tp[2]
    for off in offsets:
        small_copy(2 + off, sm_a, sm_ep.at[off - 1], {"ep": (ep + off) % ep_count})
    run(STEPS[7])
    for copy in small[3:]:
        copy.wait_recv()
    total = sm_a[...]
    for off in offsets:
        total = total + sm_ep[off - 1]
    sm_b[...] = total
    for off in range(1, 4):
        small_copy(1 + ep_count + off, sm_b, sm_dp.at[off - 1], {"dp": (dp + off) % 4})
    run(max(n + 4 * GAP + LAGS[1], proj_base + proj_n + 4 * GAP) - clock[0])
    for copy in small[2 + ep_count :]:
        copy.wait_recv()
    small_out[...] = sm_b[...] + sm_dp[0] + sm_dp[1] + sm_dp[2]

    def y_finish(index, _):
        for half in (0, 1):
            chunk = 2 * index + half
            for off in offsets:
                source = (ep + ep_count - off) % ep_count
                y_gather(half, index, off).wait_send()
                remote(
                    pfin.at[source, chunk], pfin.at[source, chunk],
                    g_send.at[off - 1, half, index], g_recv.at[off - 1, half, index], {"ep": source},
                ).wait_recv()
        proj_chain.drain(index)
        return 0

    lax.fori_loop(0, proj_n, y_finish, 0)
    for copy in sends:
        copy.wait_send()

    def drain(index, _):
        expert_chain.drain(index)
        for half in (0, 1):
            for hop in (1, 2, 3):
                x_copy(half, index, hop).wait_send()
            pl.when(expert_chain.place(half) == 2)(out_copy_of(half, index).wait)
        return 0

    lax.fori_loop(0, n, drain, 0)


def layer_step(tokens, segment, key_mask, routes, gates, cot, g1, b1, wq, wk, wv, wo, g2, b2, fin, fout, tin, tout):
    ep_count = lax.axis_size("ep")
    assert lax.axis_size("dp") == 4 and lax.axis_size("tp") == 4
    rows, width = tokens.shape
    group_rows = segment.shape[1]
    cols = wq.shape[0]
    hidden = tin.shape[1]
    quarter = hidden // 4
    assert quarter == width and 4 * cols == width
    capacity = 4 * rows // (EXP_DEV * ep_count)
    gathered = 4 * ep_count * capacity
    n = width // CHUNK
    proj = 12
    chunk = width // (proj * ep_count)
    dma = pltpu.SemaphoreType.DMA
    vmem = pl.BlockSpec(memory_space=pltpu.VMEM)
    hbm = pl.BlockSpec(memory_space=pl.ANY)
    struct = jax.ShapeDtypeStruct
    block = (ep_count, EXP_DEV, capacity, width)
    single = (ep_count, capacity, width)
    others = ep_count - 1
    small = (8, width)
    pg_shape = (4, ep_count, cols // ep_count, width)
    y_shape = (4, others, cols // ep_count, width)
    many = 3 + others + 3
    return pl.pallas_call(
        functools.partial(layer_kernel, ep_count, cols // HD, n),
        out_shape=(
            pltpu.VMEM((2, n, 4, CHUNK, width), BF),
            pltpu.VMEM((ep_count, proj, chunk, width), BF),
            pltpu.VMEM(small, F32), pltpu.VMEM((rows, width), F32), pltpu.VMEM((rows, width), BF),
        ),
        in_specs=[vmem] * 14 + [hbm] * 4,
        out_specs=(hbm, vmem, vmem, vmem, vmem),
        scratch_shapes=[
            pltpu.VMEM((hidden // width, 2, width, width), BF),
            pltpu.VMEM((4, rows, width), BF), pltpu.VMEM((group_rows, 3 * cols), BF),
            pltpu.VMEM((group_rows, cols), BF), pltpu.VMEM((group_rows, 8), F32), pltpu.VMEM((rows, width), F32),
            pltpu.VMEM((4,) + single, BF), pltpu.VMEM((4,) + single, BF),
            pltpu.VMEM((2, rows, ep_count * EXP_DEV * capacity), BF),
            pltpu.VMEM((3 * cols, width), BF), pltpu.VMEM((group_rows, group_rows), F32),
            pltpu.VMEM((2, rows, width), F32), pltpu.VMEM((2, rows, width), F32),
            pltpu.VMEM((rows, width), BF), pltpu.VMEM((rows, width), BF),
            pltpu.VMEM(block, BF), pltpu.VMEM(block, BF), pltpu.VMEM(single, BF), pltpu.VMEM(single, BF),
            pltpu.VMEM((ep_count * capacity, width), F32), pltpu.VMEM((ep_count * capacity, width), F32),
            pltpu.VMEM(block, BF), pltpu.VMEM(block, BF),
            pltpu.VMEM((gathered, quarter), BF), pltpu.VMEM((gathered, quarter), BF),
            pltpu.VMEM((2, width, width), F32),
            pltpu.VMEM((2, n, CHUNK, width), BF), pltpu.VMEM((2, n, CHUNK, width), BF),
            pltpu.VMEM((proj, chunk, width), F32), pltpu.VMEM((2, proj // 2, chunk, width), BF),
            pltpu.VMEM(pg_shape, BF), pltpu.VMEM(y_shape, BF),
            pltpu.VMEM(block, BF), pltpu.VMEM(block, BF),
            pltpu.VMEM((4, rows, width), BF),
            pltpu.VMEM((group_rows, cols), BF), pltpu.VMEM((group_rows, 3 * cols), BF),
            pltpu.VMEM((2, rows, width), BF), pltpu.VMEM((2, rows, width), BF),
            pltpu.VMEM((rows, width), BF), pltpu.VMEM((rows, width), BF),
            pltpu.VMEM(small, F32), pltpu.VMEM((3,) + small, F32), pltpu.VMEM((others,) + small, F32),
            pltpu.VMEM((3,) + small, F32), pltpu.VMEM(small, F32), pltpu.VMEM(small, F32),
            dma((2, 2, hidden // width)), dma((2, 3)), dma((2, 3)), dma((2, 2)), dma((2, 2)), dma((2,)), dma((2,)),
            dma((2, 2, others)), dma((2, 2, others)), dma((2, ep_count, 3)), dma((2, ep_count, 3)),
            dma((2, n)), dma((2, n)), dma((2, n)), dma((2, 2, n)), dma((2, n)),
            dma((3, 2, n)), dma((3, 2, n)), dma((2, n)),
            dma((2, proj // 2)), dma((2, proj // 2)), dma((2, proj // 2)), dma((2, 2, proj // 2)), dma((2, proj // 2)),
            dma((4, others)), dma((4, others)), dma((others, 2, proj // 2)), dma((others, 2, proj // 2)),
            dma((2, 2, others)), dma((2, 2, others)), dma((many,)), dma((many,)),
        ],
        compiler_params=pltpu.CompilerParams(
            collective_id=0, has_side_effects=True, vmem_limit_bytes=51 * 1024 * 1024
        ),
        name="layer",
    )(tokens, segment, key_mask, routes, gates, cot, g1, b1, wq, wk, wv, wo, g2, b2, fin, fout, tin, tout)


def finish_kernel(
    tp_ref, rg_ref, pfin_ref, small_ref, grad_ref, layer_ref,
    gin_ref, gout_ref, o_ref, v_ref, q_ref, k_ref, tokens_ref, result_ref, a_ref, b_ref, c_ref, d_ref, count_ref,
):
    width = gin_ref.shape[1]
    gin_ref[...] = rg_ref[0, :, 0].reshape(gin_ref.shape).astype(F32)
    gout_ref[...] = rg_ref[1, :, 0].reshape(gout_ref.shape).astype(F32)

    @pl.when((pl.program_id(0) == 0) & (pl.program_id(1) == 0))
    def _():
        owners = pfin_ref.shape[0]
        span = q_ref.shape[0] // owners
        for index, ref in enumerate((o_ref, v_ref, q_ref, k_ref)):
            for owner in range(owners):
                value = pfin_ref[owner, 3 * index : 3 * index + 3].reshape(span, width)
                ref[owner * span : (owner + 1) * span, :] = value.astype(F32)
        tokens_ref[...] = grad_ref[...]
        result_ref[...] = layer_ref[...]
        for index, ref in enumerate((a_ref, b_ref, c_ref, d_ref)):
            ref[...] = small_ref[index : index + 1, :].reshape(width)
        count_ref[...] = small_ref[4:5, 0:128].astype(jnp.int32).reshape(128)[: count_ref.shape[0]]


def finish(rg, pfin, small, grad, layer, cols, experts):
    _, n, _, chunk, width = rg.shape
    hidden = 4 * width
    parts = 1
    me = lax.axis_index("tp").astype(jnp.int32).reshape(1)
    struct = jax.ShapeDtypeStruct

    def where(quarter, me_ref):
        mine = me_ref[0]
        low = (quarter % 2) != (mine % 2)
        high = (quarter // 2) != (mine // 2)
        return jnp.where(low, 1, 0) + jnp.where(high, 2, 0)

    def whole(shape):
        return pl.BlockSpec(shape, lambda q, i, t: (0,) * len(shape))

    outs = [struct((cols, width), F32)] * 4 + [struct(grad.shape, F32), struct(layer.shape, BF)]
    outs += [struct((width,), F32)] * 4 + [struct((experts,), jnp.int32)]
    return pl.pallas_call(
        finish_kernel,
        grid_spec=pltpu.PrefetchScalarGridSpec(
            num_scalar_prefetch=1,
            grid=(4, parts),
            in_specs=[
                pl.BlockSpec((2, n // parts, 1, chunk, width), lambda q, i, t: (0, i, where(q, t), 0, 0)),
                *[pl.BlockSpec(memory_space=pltpu.VMEM)] * 4,
            ],
            out_specs=[
                pl.BlockSpec((width // parts, width), lambda q, i, t: (i, q)),
                pl.BlockSpec((width // parts, width), lambda q, i, t: (parts * q + i, 0)),
            ] + [whole(out.shape) for out in outs],
        ),
        out_shape=[struct((width, hidden), F32), struct((hidden, width), F32)] + outs,
        compiler_params=pltpu.CompilerParams(vmem_limit_bytes=40 * 1024 * 1024),
        name="finish",
    )(me, *[pltpu.with_memory_space_constraint(value, pltpu.VMEM) for value in (rg, pfin, small, grad, layer)])


def local(
    tokens,
    segment,
    key_mask,
    routes,
    gates,
    ln1_gain,
    ln1_bias,
    query_weight,
    key_weight,
    value_weight,
    out_weight,
    ln2_gain,
    ln2_bias,
    frozen_in,
    frozen_out,
    train_in,
    train_out,
    cotangent,
):
    vectors = (ln1_gain, ln1_bias, ln2_gain, ln2_bias)
    flat = (query_weight.T, key_weight.T, value_weight.T, out_weight)
    cols = out_weight.shape[0]
    token_args = (tokens[0], segment, key_mask, routes[0].T, gates[0].T, cotangent[0])
    rg, pfin, small, grad, layer = layer_step(
        *token_args, *vectors[:2], *flat, *vectors[2:], frozen_in[0], frozen_out[0], train_in[0], train_out[0]
    )
    grad_in, grad_out, out, value, query, key, grad, layer, *sums, counts = finish(
        rg, pfin, small, grad, layer, cols, EXP_DEV * lax.axis_size("ep")
    )
    gain_one, bias_one, gain_two, bias_two = sums
    return (
        layer[None], grad[None], gain_one, bias_one, query.T, key.T, value.T, out, gain_two, bias_two,
        grad_in[None], grad_out[None], counts,
    )


def solution(mesh):
    in_specs = (
        P(("ep", "dp"), "tp", None),
        P(("ep", "dp"), None),
        P(("ep", "dp"), None),
        P(("ep", "dp"), "tp", None),
        P(("ep", "dp"), "tp", None),
        P(),
        P(),
        P(None, "tp"),
        P(None, "tp"),
        P(None, "tp"),
        P("tp", None),
        P(),
        P(),
        P("ep", None, None),
        P("ep", None, None),
        P("ep", None, None),
        P("ep", None, None),
        P(("ep", "dp"), "tp", None),
    )
    out_specs = (
        P(("ep", "dp"), "tp", None),
        P(("ep", "dp"), "tp", None),
        P(),
        P(),
        P(None, "tp"),
        P(None, "tp"),
        P(None, "tp"),
        P("tp", None),
        P(),
        P(),
        P("ep", None, None),
        P("ep", None, None),
        P(),
    )
    return jax.shard_map(local, mesh=mesh, in_specs=in_specs, out_specs=out_specs, check_vma=False)
```

```python
import functools
import math

import jax
import jax.numpy as jnp
from jax import lax
from jax.experimental import pallas as pl
from jax.experimental.pallas import tpu as pltpu
from jax.sharding import PartitionSpec as P

HD = 64
EXP_DEV = 2
EPSILON = 1e-05
MASKED = -1e30
MESH = pl.DeviceIdType.MESH
BF = jnp.bfloat16
F32 = jnp.float32
CHUNK = 32
STEPS = (6, 3, 3, 1, 1, 3, 6, 6)
GAP = 2
LAGS = (6, 8)
AHEAD = 1
FIRST = 1


def tp_peers():
    me = lax.axis_index("tp")
    one = me + 1 - 2 * (me % 2)
    return (me, one, (me + 2) % 4, (one + 2) % 4)


def remote(src, dst, send, recv, where):
    return pltpu.make_async_remote_copy(
        src_ref=src, dst_ref=dst, send_sem=send, recv_sem=recv,
        device_id=where, device_id_type=MESH,
    )


def entry_barrier(ep_count, dp_count):
    barrier = pltpu.get_barrier_semaphore()
    _, tp1, tp2, tp3 = tp_peers()
    ep, dp = lax.axis_index("ep"), lax.axis_index("dp")
    for peer in (tp1, tp2, tp3):
        pl.semaphore_signal(barrier, inc=1, device_id={"tp": peer}, device_id_type=MESH)
    for off in range(1, ep_count):
        pl.semaphore_signal(
            barrier, inc=1, device_id={"ep": (ep + off) % ep_count}, device_id_type=MESH
        )
    for off in range(1, dp_count):
        pl.semaphore_signal(
            barrier, inc=1, device_id={"dp": (dp + off) % dp_count}, device_id_type=MESH
        )
    pl.semaphore_wait(barrier, 3 + ep_count - 1 + dp_count - 1)


def gelu_pair(hidden):
    phi = 0.5 * (1.0 + lax.erf(hidden * math.sqrt(0.5)))
    dens = jnp.exp(-0.5 * hidden * hidden) * (1.0 / math.sqrt(2.0 * math.pi))
    return hidden * phi, phi + hidden * dens


def row_of(ref):
    return ref[...].reshape(1, -1)


def columns_of(ref):
    value = ref[...].astype(F32)
    padded = jnp.concatenate([value, jnp.zeros((6, value.shape[1]), F32)], axis=0)
    flipped = padded.T
    return flipped[:, 0:1], flipped[:, 1:2]


def fill_bias(seg_ref, key_ref, bias):
    segment = seg_ref[...]
    group_rows = segment.shape[1]
    lane = lax.broadcasted_iota(jnp.int32, segment.shape, 1)
    starts = (segment != pltpu.roll(segment, 1, 1)) | (lane == 0)
    keep = (key_ref[...] == 1) | starts
    segment = segment.astype(F32)
    column = jnp.broadcast_to(segment, (8, group_rows)).T[:, 0:1]
    kept = jnp.where(keep, segment, -1.0)
    bias[...] = jnp.where(column == kept, 0.0, MASKED)


def ln_rows(values, gain, bias):
    center = jnp.mean(values, axis=-1, keepdims=True)
    shifted = values - center
    spread = jnp.mean(shifted * shifted, axis=-1, keepdims=True)
    return shifted * lax.rsqrt(spread + EPSILON) * gain + bias


def route_picks(routes_ref, capacity, slots):
    first, second = (column.astype(jnp.int32) for column in columns_of(routes_ref))
    rows = first.shape[0]
    lane = lax.broadcasted_iota(jnp.int32, (rows, 128), 1)
    marks = jnp.where((lane == first) | (lane == second), 1.0, 0.0)
    row_id = lax.broadcasted_iota(jnp.int32, (rows, rows), 0)
    col_id = lax.broadcasted_iota(jnp.int32, (rows, rows), 1)
    lower = jnp.where(row_id > col_id, 1.0, 0.0).astype(BF)
    before = jnp.dot(lower, marks.astype(BF), preferred_element_type=F32)
    slot = lax.broadcasted_iota(jnp.int32, (rows, slots), 1)
    picks = []
    for route in (first, second):
        place = jnp.sum(jnp.where(lane == route, before, 0.0), axis=1, keepdims=True)
        chosen = route * capacity + place.astype(jnp.int32)
        picks.append(jnp.where(slot == chosen, 1.0, 0.0).astype(BF))
    return picks[0], picks[1], marks


def dot_tn(left, right):
    return lax.dot_general(left, right, (((0,), (0,)), ((), ())), preferred_element_type=F32)


def dot_nt(left, right):
    return lax.dot_general(left, right, (((1,), (1,)), ((), ())), preferred_element_type=F32)


def dot_nn(left, right):
    return jnp.dot(left, right, preferred_element_type=F32)


def ln_backward(values, gain, upstream):
    center = jnp.mean(values, axis=-1, keepdims=True)
    shifted = values - center
    spread = jnp.mean(shifted * shifted, axis=-1, keepdims=True)
    scale = lax.rsqrt(spread + EPSILON)
    unit = shifted * scale
    inner = upstream * gain
    along = jnp.mean(inner * unit, axis=-1, keepdims=True)
    grad = scale * (inner - jnp.mean(inner, axis=-1, keepdims=True) - unit * along)
    return grad, jnp.sum(upstream * unit, axis=0, keepdims=True), jnp.sum(upstream, axis=0, keepdims=True)


class Chain:
    def __init__(self, base, count, own, stage, near, home, final, sems, hooks):
        self.base, self.count, self.own, self.stage = base, count, own, stage
        self.near, self.home, self.final, self.hooks = near, home, final, hooks
        self.red_send, self.recv_a, self.recv_b, self.bc_send, self.bc_recv = sems
        self.dp = lax.axis_index("dp")

    def place(self, half):
        return 3 - self.dp if half == 0 else self.dp

    def peers(self, half):
        down, up = (self.dp + 3) % 4, (self.dp + 1) % 4
        return (down, up) if half == 0 else (up, down)

    def red(self, half, index, near):
        toward, away = self.peers(half)
        landing = self.stage.at[half, index]
        target, sem = (self.near(half, index), self.recv_b) if near else (landing, self.recv_a)
        return remote(
            landing, target, self.red_send.at[half, index], sem.at[half, index],
            {"dp": away if near else toward},
        )

    def spread(self, half, index, near, source=None):
        toward, away = self.peers(half)
        ref = self.final(half, index)
        return remote(
            (source or self.final)(half, index), ref, self.bc_send.at[1 if near else 0, half, index], self.bc_recv.at[half, index],
            {"dp": toward if near else away},
        )

    def offer(self, index):
        for half in (0, 1):
            place = self.place(half)

            @pl.when((place == 0) | (place == 3))
            def _():
                self.stage[half, index] = self.own(half, index).astype(BF)

            pl.when(place == 0)(lambda: self.red(half, index, False).start())
            pl.when(place == 3)(lambda: self.red(half, index, True).start())

    def step(self, s):
        for half in (0, 1):
            place = self.place(half)
            index = s - self.base - GAP * place

            @pl.when((index >= 0) & (index < self.count) & ((place == 1) | (place == 2)))
            def _():
                own = self.own(half, index)

                @pl.when(place == 1)
                def _():
                    self.red(half, index, False).wait_recv()
                    self.stage[half, index] = (own + self.stage[half, index].astype(F32)).astype(BF)
                    self.red(half, index, False).start()

                @pl.when(place == 2)
                def _():
                    self.red(half, index, False).wait_recv()
                    self.red(half, index, True).wait_recv()
                    total = own + self.stage[half, index].astype(F32) + self.near(half, index)[...].astype(F32)
                    self.home(half, index)[...] = total.astype(BF)

        for half in (0, 1):
            place = self.place(half)
            index = s - self.base - GAP * (4 - place + 2 * (place // 3))

            @pl.when((index >= 0) & (index < self.count))
            def _():
                @pl.when(place == 2)
                def _():
                    self.spread(half, index, False, self.home).start()
                    self.spread(half, index, True, self.home).start()

                @pl.when(place != 2)
                def _():
                    self.spread(half, index, False).wait_recv()

                @pl.when(place == 1)
                def _():
                    self.spread(half, index, False).start()

                self.hooks[0](half, index)

            for later, hook in enumerate(self.hooks[1:]):
                after = index - LAGS[later]
                pl.when((after >= 0) & (after < self.count))(functools.partial(hook, half, after))

    def drain(self, index):
        for half in (0, 1):
            place = self.place(half)

            @pl.when(place != 2)
            def _():
                self.red(half, index, False).wait_send()

            @pl.when((place == 1) | (place == 2))
            def _():
                self.spread(half, index, False).wait_send()

            @pl.when(place == 2)
            def _():
                self.spread(half, index, True).wait_send()


def layer_kernel(
    ep_count, heads, n,
    tok_ref, seg_ref, key_ref, routes_ref, gates_ref, cot_ref, g1_ref, b1_ref, wq_ref, wk_ref, wv_ref, wo_ref,
    g2_ref, b2_ref, fin_hbm, fout_hbm, tin_hbm, tout_hbm,
    rg, pfin, small_out, grad_ref, layer_ref,
    weights, group_ref, qkv_ref, heads_ref, lse_ref, middle_ref, gx, gs, picks, joined, bias,
    part, core_slot, mix, x_slot, sx, ss, ax, as_, out_acc, back_acc, out_ref, back_ref,
    act, slope, own, stage, near_slot, acc, pstage, pgbuf, yslot, ret_back, ret_out,
    piece, up_heads, pgrad, bpart, bcore_slot, bmix, bx_slot,
    sm, sm_tp, sm_ep, sm_dp, sm_a, sm_b,
    w_sem, a_send, a_recv, c_send, c_recv, m_send, m_recv, e_send, e_recv, t_send, t_recv,
    red_send, recv_a, recv_b, bc_send, bc_recv, x_send, x_recv, out_sem,
    pred_send, precv_a, precv_b, pbc_send, pbc_recv, y_send, y_recv, g_send, g_recv,
    b_send, b_recv, s_send, s_recv,
):
    tp, tp1, tp2, tp3 = tp_peers()
    ep, dp = lax.axis_index("ep"), lax.axis_index("dp")
    rows, width = tok_ref.shape
    cols = wq_ref.shape[0]
    group_rows = seg_ref.shape[1]
    pieces = weights.shape[0]
    capacity = sx.shape[2]
    slots = ep_count * EXP_DEV * capacity
    tokens = ep_count * capacity
    frozen, train = 0, 1
    offsets = range(1, ep_count)

    def slot_of(expert, index):
        return index if expert == train else (tp + 1 + index) % pieces

    def weight_loads(expert, index):
        slot = slot_of(expert, index)
        source_in, source_out = ((fin_hbm, fout_hbm), (tin_hbm, tout_hbm))[expert]
        at = pl.ds(pl.multiple_of(index * width, width), width)
        return [
            pltpu.make_async_copy(source_in.at[:, at], weights.at[slot, 0], w_sem.at[expert, 0, index]),
            pltpu.make_async_copy(source_out.at[at, :], weights.at[slot, 1], w_sem.at[expert, 1, index]),
        ]

    residual = tok_ref[...].astype(F32)
    group_ref[tp] = ln_rows(residual, row_of(g1_ref), row_of(b1_ref)).astype(BF)
    entry_barrier(ep_count, 4)
    sends = []

    def send(copy):
        sends.append(copy)
        copy.start()

    def gather_copy(stage_of, buf, slot, index, peer):
        return remote(
            buf.at[slot], buf.at[slot], a_send.at[stage_of, index], a_recv.at[stage_of, index], {"tp": peer}
        )

    send(gather_copy(0, group_ref, tp, 1, tp2))
    send(gather_copy(0, group_ref, tp, 0, tp1))
    for index in range(pieces):
        for copy in weight_loads(train, index):
            copy.start()

    pick0, pick1, marks = route_picks(routes_ref, capacity, slots)
    picks[0] = pick0
    picks[1] = pick1
    sm[...] = jnp.zeros_like(sm)
    sm[4:5, 0:128] = jnp.sum(marks, axis=0, keepdims=True)
    upstream = cot_ref[...].astype(F32)
    gate0, gate1 = columns_of(gates_ref)
    share0 = (gate0 * upstream).astype(BF)
    share1 = (gate1 * upstream).astype(BF)
    ss[...] = (dot_tn(pick0, share0) + dot_tn(pick1, share1)).astype(BF).reshape(ss.shape)

    def landing(kind, expert, source):
        if expert == train:
            return (gx, gs)[kind].at[0, source]
        return (ax, as_)[kind].at[source]

    def owner_copy(kind, expert, off):
        peer = (ep + off) % ep_count
        return remote(
            (sx, ss)[kind].at[peer, expert], landing(kind, expert, ep),
            e_send.at[kind, expert, off - 1], e_recv.at[kind, expert, off - 1], {"ep": peer},
        )

    def owner_wait(kind, expert, off):
        source = (ep + ep_count - off) % ep_count
        target = landing(kind, expert, source)
        remote(
            target, target, e_send.at[kind, expert, off - 1], e_recv.at[kind, expert, off - 1], {"ep": source}
        ).wait_recv()

    def token_copy(kind, rel, hop):
        buf = (gx, gs)[kind]
        origin = (ep + ep_count - rel) % ep_count
        source, peer = ((0, tp1), (0, tp2), (2, tp1))[hop - 1]
        return remote(
            buf.at[source, origin], buf.at[hop, origin],
            t_send.at[kind, rel, hop - 1], t_recv.at[kind, rel, hop - 1], {"tp": peer},
        )

    def dispatch(kind, source):
        for off in offsets:
            send(owner_copy(kind, train, off))
        (gx, gs)[kind][0, ep] = source[ep, train]
        send(token_copy(kind, 0, 2))
        send(token_copy(kind, 0, 1))
        for off in offsets:
            send(owner_copy(kind, frozen, off))
        (ax, as_)[kind][ep] = source[ep, frozen]

    def pass_on(kind):
        for off in offsets:
            owner_wait(kind, train, off)
            send(token_copy(kind, off, 2))
            send(token_copy(kind, off, 1))

    def forward(kind, rel):
        token_copy(kind, rel, 2).wait_recv()
        send(token_copy(kind, rel, 3))

    dispatch(1, ss)
    for index, ref in enumerate((wq_ref, wk_ref, wv_ref)):
        joined[index * cols : (index + 1) * cols, :] = ref[...]
    fill_bias(seg_ref, key_ref, bias)

    def project(slot):
        at = pl.ds(pl.multiple_of(slot * rows, rows), rows)
        qkv_ref[at, :] = dot_nt(group_ref[slot], joined[...]).astype(BF)

    project(tp)
    gather_copy(0, group_ref, tp1, 0, tp1).wait_recv()
    project(tp1)
    gather_copy(0, group_ref, tp2, 1, tp2).wait_recv()
    send(gather_copy(0, group_ref, tp2, 2, tp1))
    project(tp2)
    gather_copy(0, group_ref, tp3, 2, tp1).wait_recv()
    project(tp3)

    scale = HD ** (-0.5)
    block = min(256, group_rows)
    for head in range(heads):
        low, high = head * HD, (head + 1) * HD
        for index in range(group_rows // block):
            at = slice(index * block, (index + 1) * block)
            query = qkv_ref[at, low:high]
            keys = qkv_ref[:, cols + low : cols + high]
            values = qkv_ref[:, 2 * cols + low : 2 * cols + high]
            scores = dot_nt(query, keys) * scale + bias[at, :]
            highest = jnp.max(scores, axis=-1, keepdims=True)
            weight = jnp.exp(scores - highest)
            total = jnp.sum(weight, axis=-1, keepdims=True)
            probs = (weight * (1.0 / total)).astype(BF)
            heads_ref[at, low:high] = dot_nn(probs, values).astype(BF)
            lse_ref[at, head : head + 1] = highest + jnp.log(total)

    def partial(slot):
        at = pl.ds(pl.multiple_of(slot * rows, rows), rows)
        return dot_nn(heads_ref[at, :], wo_ref[...])

    def core_copy(index):
        return remote(part.at[index], core_slot.at[index], c_send.at[0, index], c_recv.at[0, index], {"tp": tp1})

    part[0] = partial(tp3).astype(BF)
    send(core_copy(0))
    part[1] = partial(tp1).astype(BF)
    send(core_copy(1))
    crossing = partial(tp2)
    mine = tok_ref[...].astype(F32) + partial(tp)
    core_copy(0).wait_recv()
    mix[...] = (crossing + core_slot[0].astype(F32)).astype(BF)
    cross = remote(mix, x_slot, m_send.at[0], m_recv.at[0], {"tp": tp2})
    send(cross)
    pass_on(1)
    forward(1, 0)
    core_copy(1).wait_recv()
    mine = mine + core_slot[1].astype(F32)
    cross.wait_recv()
    middle = mine + x_slot[...].astype(F32)
    middle_ref[...] = middle
    normed = ln_rows(middle, row_of(g2_ref), row_of(b2_ref)).astype(BF)
    sx[...] = dot_tn(picks[0] + picks[1], normed).astype(BF).reshape(sx.shape)
    dispatch(0, sx)
    for off in offsets:
        forward(1, off)
    pass_on(0)

    def expert_piece(expert, index, inputs, shares):
        slot = slot_of(expert, index)
        before = dot_nn(inputs, weights[slot, 0])
        through = dot_nt(shares, weights[slot, 1])
        value, grad = gelu_pair(before)
        slopes = (through * grad).astype(BF)
        produced = dot_nn(value.astype(BF), weights[slot, 1])
        returned = dot_nt(slopes, weights[slot, 0])

        @pl.when(index == 0)
        def _():
            out_acc[...] = produced
            back_acc[...] = returned

        @pl.when(index > 0)
        def _():
            out_acc[...] += produced
            back_acc[...] += returned

    def return_copy(kind, expert, off):
        peer = (ep + off) % ep_count
        source, target = ((back_ref, ret_back), (out_ref, ret_out))[kind]
        return remote(
            source.at[peer, expert], target.at[ep, expert],
            b_send.at[kind, expert, off - 1], b_recv.at[kind, expert, off - 1], {"ep": peer},
        )

    def return_wait(kind):
        target = (ret_back, ret_out)[kind]
        for expert in range(EXP_DEV):
            for off in offsets:
                source = (ep + ep_count - off) % ep_count
                remote(
                    target.at[source, expert], target.at[source, expert],
                    b_send.at[kind, expert, off - 1], b_recv.at[kind, expert, off - 1], {"ep": source},
                ).wait_recv()

    def give_back(expert):
        back_ref[:, expert] = back_acc[...].astype(BF).reshape(ep_count, capacity, width)
        out_ref[:, expert] = out_acc[...].astype(BF).reshape(ep_count, capacity, width)
        for kind in (0, 1):
            for off in offsets:
                send(return_copy(kind, expert, off))
        ret_back[ep, expert] = back_ref[ep, expert]
        ret_out[ep, expert] = out_ref[ep, expert]

    def train_piece(index, _):
        for copy in weight_loads(train, index):
            copy.wait()
        expert_piece(train, index, gx[0].reshape(tokens, width), gs[0].reshape(tokens, width))

        @pl.when(index != tp)
        def _():
            for copy in weight_loads(frozen, (index + pieces - 1 - tp) % pieces):
                copy.start()

        @pl.when(index == 1)
        def _():
            token_copy(0, 0, 2).wait_recv()
            token_copy(0, 0, 3).start()

        return 0

    lax.fori_loop(0, pieces, train_piece, 0)
    sends.append(token_copy(0, 0, 3))
    give_back(train)
    for off in offsets:
        forward(0, off)

    def frozen_piece(index, _):
        for copy in weight_loads(frozen, index):
            copy.wait()
        expert_piece(frozen, index, ax[...].reshape(tokens, width), as_[...].reshape(tokens, width))
        return 0

    for kind in (0, 1):
        for off in offsets:
            owner_wait(kind, frozen, off)
    lax.fori_loop(0, AHEAD, frozen_piece, 0)

    def hidden_block(index, _):
        for hop, when in ((1, 1), (3, 3)):
            @pl.when(index == when)
            def _(hop=hop):
                for kind in (0, 1):
                    for rel in range(ep_count):
                        token_copy(kind, rel, hop).wait_recv()

        before = dot_nn(gx[index].reshape(tokens, width), weights[tp, 0])
        through = dot_nt(gs[index].reshape(tokens, width), weights[tp, 1])
        value, grad = gelu_pair(before)
        at = pl.ds(pl.multiple_of(index * tokens, tokens), tokens)
        act[at, :] = value.astype(BF)
        slope[at, :] = (through * grad).astype(BF)
        return 0

    lax.fori_loop(0, 4, hidden_block, 0)
    for copy in weight_loads(frozen, pieces - 1):
        copy.start()

    def x_copy(half, index, hop, owner=False):
        source, peer = ((0, tp1), (0, tp2), (2, tp1))[hop - 1]
        from_ref = stage.at[half, index] if owner else rg.at[half, index, source]
        return remote(
            from_ref, rg.at[half, index, hop],
            x_send.at[hop - 1, half, index], x_recv.at[hop - 1, half, index], {"tp": peer},
        )

    def out_copy_of(half, index):
        return pltpu.make_async_copy(stage.at[half, index], rg.at[half, index, 0], out_sem.at[half, index])

    def cross_first(half, index):
        owner = expert_chain.place(half) == 2

        @pl.when(owner)
        def _():
            x_copy(half, index, 2, True).start()
            x_copy(half, index, 1, True).start()
            out_copy_of(half, index).start()

        @pl.when(jnp.logical_not(owner))
        def _():
            x_copy(half, index, 2).start()
            x_copy(half, index, 1).start()

    def cross_second(half, index):
        x_copy(half, index, 2).wait_recv()
        x_copy(half, index, 3).start()

    def cross_third(half, index):
        x_copy(half, index, 1).wait_recv()
        x_copy(half, index, 3).wait_recv()

    expert_chain = Chain(
        0, n, lambda half, index: own[half, pl.ds(pl.multiple_of(index * CHUNK, CHUNK), CHUNK), :],
        stage, lambda half, index: near_slot.at[half, index], lambda half, index: stage.at[half, index],
        lambda half, index: rg.at[half, index, 0],
        (red_send, recv_a, recv_b, bc_send, bc_recv), (cross_first, cross_second, cross_third),
    )
    span = 128

    def outer(index, _):
        at = pl.ds(pl.multiple_of(index * span, span), span)
        own[0, at, :] = dot_tn(gx[:, :, :, at].reshape(-1, span), slope[...])
        own[1, at, :] = dot_tn(act[:, at], gs[...].reshape(-1, width))
        @pl.when(index < blocks - 1)
        def _():
            for part_of in range(share_of):
                expert_chain.offer(index * share_of + part_of)

        return 0

    blocks, share_of = width // span, span // CHUNK
    lax.fori_loop(0, FIRST, outer, 0)
    clock = [0]
    proj_chain = None

    def run(count):
        def body(s, _):
            if proj_chain is not None:
                proj_chain.step(s)
            expert_chain.step(s)
            return 0

        lax.fori_loop(clock[0], clock[0] + count, body, 0)
        clock[0] += count

    lax.fori_loop(AHEAD, pieces, frozen_piece, 0)
    give_back(frozen)
    lax.fori_loop(FIRST, blocks, outer, 0)
    run(STEPS[0])
    return_wait(0)
    second = dot_nn(picks[0] + picks[1], ret_back[...].reshape(slots, width))
    inner_grad, gain_two, bias_two = ln_backward(middle_ref[...], row_of(g2_ref), second)
    middle_grad = cot_ref[...].astype(F32) + inner_grad
    grad_ref[...] = middle_grad
    piece[tp] = middle_grad.astype(BF)
    send(gather_copy(1, piece, tp, 1, tp2))
    send(gather_copy(1, piece, tp, 0, tp1))
    sm[2:3, :] = gain_two
    sm[3:4, :] = bias_two
    run(STEPS[1])

    def head_rows(slot):
        at = pl.ds(pl.multiple_of(slot * rows, rows), rows)
        up_heads[at, :] = dot_nt(piece[slot], wo_ref[...]).astype(BF)

    head_rows(tp)
    gather_copy(1, piece, tp1, 0, tp1).wait_recv()
    head_rows(tp1)
    gather_copy(1, piece, tp2, 1, tp2).wait_recv()
    send(gather_copy(1, piece, tp2, 2, tp1))
    head_rows(tp2)
    run(STEPS[2])
    gather_copy(1, piece, tp3, 2, tp1).wait_recv()
    head_rows(tp3)

    def y_scatter(batch, off):
        peer = (ep + off) % ep_count
        return remote(
            pgbuf.at[batch, peer], yslot.at[batch, off - 1], y_send.at[batch, off - 1], y_recv.at[batch, off - 1],
            {"ep": peer},
        )

    def proj_start(batch, value):
        pgbuf[batch] = value.astype(BF).reshape(pgbuf.shape[1:])
        for off in offsets:
            send(y_scatter(batch, off))

    def proj_sum(batch):
        total = pgbuf[batch, ep].astype(F32)
        for off in offsets:
            y_scatter(batch, off).wait_recv()
            total = total + yslot[batch, off - 1].astype(F32)
        acc[3 * batch : 3 * batch + 3] = total.reshape((3,) + acc.shape[1:])

    proj_start(0, dot_tn(heads_ref[...], piece[...].reshape(group_rows, width)))
    for head in range(heads):
        low, high = head * HD, (head + 1) * HD
        key_sum = value_sum = None
        for index in range(group_rows // block):
            at = slice(index * block, (index + 1) * block)
            query = qkv_ref[at, low:high]
            keys = qkv_ref[:, cols + low : cols + high]
            values = qkv_ref[:, 2 * cols + low : 2 * cols + high]
            above = up_heads[at, low:high]
            scores = dot_nt(query, keys) * scale + bias[at, :]
            probs = jnp.exp(scores - lse_ref[at, head : head + 1])
            prob_grad = dot_nt(above, values)
            centered = jnp.sum(probs * prob_grad, axis=-1, keepdims=True)
            score_grad = (probs * (prob_grad - centered)).astype(BF)
            pgrad[at, low:high] = (dot_nn(score_grad, keys) * scale).astype(BF)
            key_part = dot_tn(score_grad, query)
            value_part = dot_tn(probs.astype(BF), above)
            key_sum = key_part if key_sum is None else key_sum + key_part
            value_sum = value_part if value_sum is None else value_sum + value_part
        pgrad[:, cols + low : cols + high] = (key_sum * scale).astype(BF)
        pgrad[:, 2 * cols + low : 2 * cols + high] = value_sum.astype(BF)
        run(STEPS[3])

    def back_partial(slot):
        at = pl.ds(pl.multiple_of(slot * rows, rows), rows)
        return dot_nn(pgrad[at, :], joined[...])

    def back_core_copy(index):
        return remote(bpart.at[index], bcore_slot.at[index], c_send.at[1, index], c_recv.at[1, index], {"tp": tp1})

    bpart[0] = back_partial(tp3).astype(BF)
    send(back_core_copy(0))
    bpart[1] = back_partial(tp1).astype(BF)
    send(back_core_copy(1))
    normed = group_ref[...].reshape(group_rows, width)
    for batch, part_index in ((1, 2), (2, 0), (3, 1)):
        proj_start(batch, dot_tn(pgrad[:, part_index * cols : (part_index + 1) * cols], normed))
    crossing = back_partial(tp2)
    mine = back_partial(tp)
    run(STEPS[4])
    back_core_copy(0).wait_recv()
    bmix[...] = (crossing + bcore_slot[0].astype(F32)).astype(BF)
    back_cross = remote(bmix, bx_slot, m_send.at[1], m_recv.at[1], {"tp": tp2})
    send(back_cross)
    def y_gather(half, index, off):
        chunk = 2 * index + half
        return remote(
            pfin.at[ep, chunk], pfin.at[ep, chunk], g_send.at[off - 1, half, index], g_recv.at[off - 1, half, index],
            {"ep": (ep + off) % ep_count},
        )

    def y_first(half, index):
        for off in offsets:
            y_gather(half, index, off).start()

    proj_n = acc.shape[0] // 2
    proj_base = n - share_of
    assert proj_n >= share_of and clock[0] <= proj_base + GAP
    proj_chain = Chain(
        proj_base, proj_n, lambda half, index: acc[2 * index + half], pstage,
        *[lambda half, index: pfin.at[ep, 2 * index + half]] * 3,
        (pred_send, precv_a, precv_b, pbc_send, pbc_recv), (y_first,),
    )

    def proj_offer(batches):
        for batch in batches:
            proj_sum(batch)
        for index in range((3 * batches[0] + 1) // 2, 3 * (batches[-1] + 1) // 2):
            proj_chain.offer(index)
            if index < share_of:
                expert_chain.offer(n - share_of + index)

    run(STEPS[5])
    proj_offer((0, 1))
    back_core_copy(1).wait_recv()
    back_cross.wait_recv()
    first = mine + bcore_slot[1].astype(F32) + bx_slot[...].astype(F32)
    residual_part, gain_one, bias_one = ln_backward(tok_ref[...].astype(F32), row_of(g1_ref), first)
    grad_ref[...] += residual_part
    sm[0:1, :] = gain_one
    sm[1:2, :] = bias_one

    small = []

    def small_copy(slot, source, target, where):
        small.append(remote(source, target, s_send.at[slot], s_recv.at[slot], where))
        send(small[-1])

    for hop, peer in ((1, tp1), (2, tp2), (3, tp3)):
        small_copy(hop - 1, sm, sm_tp.at[hop - 1], {"tp": peer})
    proj_offer((2, 3))

    run(STEPS[6])
    return_wait(1)
    returned = ret_out[...].reshape(slots, width)
    gate0, gate1 = columns_of(gates_ref)
    mixture = gate0 * dot_nn(picks[0], returned) + gate1 * dot_nn(picks[1], returned)
    layer_ref[...] = (middle_ref[...] + mixture).astype(BF)
    for copy in small:
        copy.wait_recv()
    sm_a[...] = sm[...] + sm_tp[0] + sm_tp[1] + sm_tp[2]
    for off in offsets:
        small_copy(2 + off, sm_a, sm_ep.at[off - 1], {"ep": (ep + off) % ep_count})
    run(STEPS[7])
    for copy in small[3:]:
        copy.wait_recv()
    total = sm_a[...]
    for off in offsets:
        total = total + sm_ep[off - 1]
    sm_b[...] = total
    for off in range(1, 4):
        small_copy(1 + ep_count + off, sm_b, sm_dp.at[off - 1], {"dp": (dp + off) % 4})
    run(max(n + 4 * GAP + LAGS[1], proj_base + proj_n + 4 * GAP) - clock[0])
    for copy in small[2 + ep_count :]:
        copy.wait_recv()
    small_out[...] = sm_b[...] + sm_dp[0] + sm_dp[1] + sm_dp[2]

    def y_finish(index, _):
        for half in (0, 1):
            chunk = 2 * index + half
            for off in offsets:
                source = (ep + ep_count - off) % ep_count
                y_gather(half, index, off).wait_send()
                remote(
                    pfin.at[source, chunk], pfin.at[source, chunk],
                    g_send.at[off - 1, half, index], g_recv.at[off - 1, half, index], {"ep": source},
                ).wait_recv()
        proj_chain.drain(index)
        return 0

    lax.fori_loop(0, proj_n, y_finish, 0)
    for copy in sends:
        copy.wait_send()

    def drain(index, _):
        expert_chain.drain(index)
        for half in (0, 1):
            for hop in (1, 2, 3):
                x_copy(half, index, hop).wait_send()
            pl.when(expert_chain.place(half) == 2)(out_copy_of(half, index).wait)
        return 0

    lax.fori_loop(0, n, drain, 0)


def layer_step(tokens, segment, key_mask, routes, gates, cot, g1, b1, wq, wk, wv, wo, g2, b2, fin, fout, tin, tout):
    ep_count = lax.axis_size("ep")
    assert lax.axis_size("dp") == 4 and lax.axis_size("tp") == 4
    rows, width = tokens.shape
    group_rows = segment.shape[1]
    cols = wq.shape[0]
    hidden = tin.shape[1]
    quarter = hidden // 4
    assert quarter == width and 4 * cols == width
    capacity = 4 * rows // (EXP_DEV * ep_count)
    gathered = 4 * ep_count * capacity
    n = width // CHUNK
    proj = 12
    chunk = width // (proj * ep_count)
    dma = pltpu.SemaphoreType.DMA
    vmem = pl.BlockSpec(memory_space=pltpu.VMEM)
    hbm = pl.BlockSpec(memory_space=pl.ANY)
    struct = jax.ShapeDtypeStruct
    block = (ep_count, EXP_DEV, capacity, width)
    single = (ep_count, capacity, width)
    others = ep_count - 1
    small = (8, width)
    pg_shape = (4, ep_count, cols // ep_count, width)
    y_shape = (4, others, cols // ep_count, width)
    many = 3 + others + 3
    return pl.pallas_call(
        functools.partial(layer_kernel, ep_count, cols // HD, n),
        out_shape=(
            pltpu.VMEM((2, n, 4, CHUNK, width), BF),
            pltpu.VMEM((ep_count, proj, chunk, width), BF),
            pltpu.VMEM(small, F32), pltpu.VMEM((rows, width), F32), pltpu.VMEM((rows, width), BF),
        ),
        in_specs=[vmem] * 14 + [hbm] * 4,
        out_specs=(hbm, vmem, vmem, vmem, vmem),
        scratch_shapes=[
            pltpu.VMEM((hidden // width, 2, width, width), BF),
            pltpu.VMEM((4, rows, width), BF), pltpu.VMEM((group_rows, 3 * cols), BF),
            pltpu.VMEM((group_rows, cols), BF), pltpu.VMEM((group_rows, 8), F32), pltpu.VMEM((rows, width), F32),
            pltpu.VMEM((4,) + single, BF), pltpu.VMEM((4,) + single, BF),
            pltpu.VMEM((2, rows, ep_count * EXP_DEV * capacity), BF),
            pltpu.VMEM((3 * cols, width), BF), pltpu.VMEM((group_rows, group_rows), F32),
            pltpu.VMEM((2, rows, width), BF), pltpu.VMEM((2, rows, width), BF),
            pltpu.VMEM((rows, width), BF), pltpu.VMEM((rows, width), BF),
            pltpu.VMEM(block, BF), pltpu.VMEM(block, BF), pltpu.VMEM(single, BF), pltpu.VMEM(single, BF),
            pltpu.VMEM((ep_count * capacity, width), F32), pltpu.VMEM((ep_count * capacity, width), F32),
            pltpu.VMEM(block, BF), pltpu.VMEM(block, BF),
            pltpu.VMEM((gathered, quarter), BF), pltpu.VMEM((gathered, quarter), BF),
            pltpu.VMEM((2, width, width), F32),
            pltpu.VMEM((2, n, CHUNK, width), BF), pltpu.VMEM((2, n, CHUNK, width), BF),
            pltpu.VMEM((proj, chunk, width), F32), pltpu.VMEM((2, proj // 2, chunk, width), BF),
            pltpu.VMEM(pg_shape, BF), pltpu.VMEM(y_shape, BF),
            pltpu.VMEM(block, BF), pltpu.VMEM(block, BF),
            pltpu.VMEM((4, rows, width), BF),
            pltpu.VMEM((group_rows, cols), BF), pltpu.VMEM((group_rows, 3 * cols), BF),
            pltpu.VMEM((2, rows, width), BF), pltpu.VMEM((2, rows, width), BF),
            pltpu.VMEM((rows, width), BF), pltpu.VMEM((rows, width), BF),
            pltpu.VMEM(small, F32), pltpu.VMEM((3,) + small, F32), pltpu.VMEM((others,) + small, F32),
            pltpu.VMEM((3,) + small, F32), pltpu.VMEM(small, F32), pltpu.VMEM(small, F32),
            dma((2, 2, hidden // width)), dma((2, 3)), dma((2, 3)), dma((2, 2)), dma((2, 2)), dma((2,)), dma((2,)),
            dma((2, 2, others)), dma((2, 2, others)), dma((2, ep_count, 3)), dma((2, ep_count, 3)),
            dma((2, n)), dma((2, n)), dma((2, n)), dma((2, 2, n)), dma((2, n)),
            dma((3, 2, n)), dma((3, 2, n)), dma((2, n)),
            dma((2, proj // 2)), dma((2, proj // 2)), dma((2, proj // 2)), dma((2, 2, proj // 2)), dma((2, proj // 2)),
            dma((4, others)), dma((4, others)), dma((others, 2, proj // 2)), dma((others, 2, proj // 2)),
            dma((2, 2, others)), dma((2, 2, others)), dma((many,)), dma((many,)),
        ],
        compiler_params=pltpu.CompilerParams(
            collective_id=0, has_side_effects=True, vmem_limit_bytes=51 * 1024 * 1024
        ),
        name="layer",
    )(tokens, segment, key_mask, routes, gates, cot, g1, b1, wq, wk, wv, wo, g2, b2, fin, fout, tin, tout)


def finish_kernel(
    tp_ref, rg_ref, pfin_ref, small_ref, grad_ref, layer_ref,
    gin_ref, gout_ref, o_ref, v_ref, q_ref, k_ref, tokens_ref, result_ref, a_ref, b_ref, c_ref, d_ref, count_ref,
):
    width = gin_ref.shape[1]
    gin_ref[...] = rg_ref[0, :, 0].reshape(gin_ref.shape).astype(F32)
    gout_ref[...] = rg_ref[1, :, 0].reshape(gout_ref.shape).astype(F32)

    @pl.when((pl.program_id(0) == 0) & (pl.program_id(1) == 0))
    def _():
        owners = pfin_ref.shape[0]
        span = q_ref.shape[0] // owners
        for index, ref in enumerate((o_ref, v_ref, q_ref, k_ref)):
            for owner in range(owners):
                value = pfin_ref[owner, 3 * index : 3 * index + 3].reshape(span, width)
                ref[owner * span : (owner + 1) * span, :] = value.astype(F32)
        tokens_ref[...] = grad_ref[...]
        result_ref[...] = layer_ref[...]
        for index, ref in enumerate((a_ref, b_ref, c_ref, d_ref)):
            ref[...] = small_ref[index : index + 1, :].reshape(width)
        count_ref[...] = small_ref[4:5, 0:128].astype(jnp.int32).reshape(128)[: count_ref.shape[0]]


def finish(rg, pfin, small, grad, layer, cols, experts):
    _, n, _, chunk, width = rg.shape
    hidden = 4 * width
    parts = 1
    me = lax.axis_index("tp").astype(jnp.int32).reshape(1)
    struct = jax.ShapeDtypeStruct

    def where(quarter, me_ref):
        mine = me_ref[0]
        low = (quarter % 2) != (mine % 2)
        high = (quarter // 2) != (mine // 2)
        return jnp.where(low, 1, 0) + jnp.where(high, 2, 0)

    def whole(shape):
        return pl.BlockSpec(shape, lambda q, i, t: (0,) * len(shape))

    outs = [struct((cols, width), F32)] * 4 + [struct(grad.shape, F32), struct(layer.shape, BF)]
    outs += [struct((width,), F32)] * 4 + [struct((experts,), jnp.int32)]
    return pl.pallas_call(
        finish_kernel,
        grid_spec=pltpu.PrefetchScalarGridSpec(
            num_scalar_prefetch=1,
            grid=(4, parts),
            in_specs=[
                pl.BlockSpec((2, n // parts, 1, chunk, width), lambda q, i, t: (0, i, where(q, t), 0, 0)),
                *[pl.BlockSpec(memory_space=pltpu.VMEM)] * 4,
            ],
            out_specs=[
                pl.BlockSpec((width // parts, width), lambda q, i, t: (i, q)),
                pl.BlockSpec((width // parts, width), lambda q, i, t: (parts * q + i, 0)),
            ] + [whole(out.shape) for out in outs],
        ),
        out_shape=[struct((width, hidden), F32), struct((hidden, width), F32)] + outs,
        compiler_params=pltpu.CompilerParams(vmem_limit_bytes=40 * 1024 * 1024),
        name="finish",
    )(me, *[pltpu.with_memory_space_constraint(value, pltpu.VMEM) for value in (rg, pfin, small, grad, layer)])


def local(
    tokens,
    segment,
    key_mask,
    routes,
    gates,
    ln1_gain,
    ln1_bias,
    query_weight,
    key_weight,
    value_weight,
    out_weight,
    ln2_gain,
    ln2_bias,
    frozen_in,
    frozen_out,
    train_in,
    train_out,
    cotangent,
):
    vectors = (ln1_gain, ln1_bias, ln2_gain, ln2_bias)
    flat = (query_weight.T, key_weight.T, value_weight.T, out_weight)
    cols = out_weight.shape[0]
    token_args = (tokens[0], segment, key_mask, routes[0].T, gates[0].T, cotangent[0])
    rg, pfin, small, grad, layer = layer_step(
        *token_args, *vectors[:2], *flat, *vectors[2:], frozen_in[0], frozen_out[0], train_in[0], train_out[0]
    )
    grad_in, grad_out, out, value, query, key, grad, layer, *sums, counts = finish(
        rg, pfin, small, grad, layer, cols, EXP_DEV * lax.axis_size("ep")
    )
    gain_one, bias_one, gain_two, bias_two = sums
    return (
        layer[None], grad[None], gain_one, bias_one, query.T, key.T, value.T, out, gain_two, bias_two,
        grad_in[None], grad_out[None], counts,
    )


def solution(mesh):
    in_specs = (
        P(("ep", "dp"), "tp", None),
        P(("ep", "dp"), None),
        P(("ep", "dp"), None),
        P(("ep", "dp"), "tp", None),
        P(("ep", "dp"), "tp", None),
        P(),
        P(),
        P(None, "tp"),
        P(None, "tp"),
        P(None, "tp"),
        P("tp", None),
        P(),
        P(),
        P("ep", None, None),
        P("ep", None, None),
        P("ep", None, None),
        P("ep", None, None),
        P(("ep", "dp"), "tp", None),
    )
    out_specs = (
        P(("ep", "dp"), "tp", None),
        P(("ep", "dp"), "tp", None),
        P(),
        P(),
        P(None, "tp"),
        P(None, "tp"),
        P(None, "tp"),
        P("tp", None),
        P(),
        P(),
        P("ep", None, None),
        P("ep", None, None),
        P(),
    )
    return jax.shard_map(local, mesh=mesh, in_specs=in_specs, out_specs=out_specs, check_vma=False)
```
